32 devices in a mesh: dom: 16 (over z, y, x), segment: 2 (over core).
Axes of the slice: x: 2, y: 2, z: 4, core: 2. Of those that a mesh axis runs over, the one named last changes fastest.
Arguments:
- feats: bfloat16 [4096, 512], P('dom'), may hold values from -6 to 6
- adj_local: bfloat16 [4096, 256], P('dom'), as said below
- couple: bfloat16 [4096, 256], P('dom'), as said below
- send_rows: int32 [16, 256], P('dom'), may hold values from 0 to 255, as said below
- weights: bfloat16 [1024, 512], P('segment'), may hold values from -0.25 to 0.25
- cotangent: bfloat16 [4096, 512], P('dom'), may hold values from -1.5 to 1.5
Outputs:
- acts: bfloat16 [2, 4096, 512], P('segment', 'dom')
- grad_weights: float32 [2, 512, 512], P('segment', 'dom')
- grad_feats: float32 [4096, 512], P('dom', 'segment')
The draws below stay inside these ranges and needn't reach their ends.
Inputs may be any that keep to these rules, and one draw needn't show every extreme that they name: `adj_local`: entries are non-negative. `couple`: entries are non-negative. `send_rows`: the 128 local indices that a partition sends in one round are distinct.
All inputs are finite; a program needn't handle non-finite values.
Results may differ from the reference program's by a relative error of at most 0.013.
Values may be sent and summed in bfloat16 or wider, within the bound.
No kernel may reach another device: no remote copies, remote signals or barrier semaphores. Data moves between devices by JAX's collectives and lax.ppermute only.
A program may use at most 64 MiB of HBM per device.

```python
import jax
import jax.numpy as jnp

WIDTH = 512
PART_ROWS = 256
BOUND_ROWS = 128
NODES = 4096
N_DOM = 16
N_SEGMENT = 2


def draw_adj_local(key, part):
    rows = N_DOM * PART_ROWS
    key_mask, key_vals, key_diag = jax.random.split(key, 3)
    density = 8
    local_row = jnp.arange(rows) % PART_ROWS
    column = jnp.arange(PART_ROWS)
    diagonal = (local_row[:, None] == column[None, :]).astype(jnp.float32)
    present = (jax.random.randint(key_mask, (rows, PART_ROWS), 0, PART_ROWS) < density).astype(jnp.float32)
    values = jax.random.uniform(key_vals, (rows, PART_ROWS), jnp.float32, 0.5, 1.5) * (0.3 / density)
    diag_vals = 0.35 * jax.random.uniform(key_diag, (rows, PART_ROWS), jnp.float32, 0.8, 1.2)
    result = diagonal * diag_vals + (1.0 - diagonal) * present * values
    return result.astype(jnp.bfloat16)


def draw_couple(key, part):
    rows = N_DOM * PART_ROWS
    cols = 2 * BOUND_ROWS
    key_mask, key_vals, key_base = jax.random.split(key, 3)
    weight_each = 0.05
    local_row = jnp.arange(rows) % PART_ROWS
    column = jnp.arange(cols)
    base = (local_row[:, None] % cols == column[None, :]).astype(jnp.float32)
    present = (jax.random.randint(key_mask, (rows, cols), 0, BOUND_ROWS) < 2).astype(jnp.float32)
    values = jax.random.uniform(key_vals, (rows, cols), jnp.float32, 0.5, 1.5) * weight_each
    base_vals = jax.random.uniform(key_base, (rows, cols), jnp.float32, 0.05, 0.12)
    result = base * base_vals + (1.0 - base) * present * values
    return result.astype(jnp.bfloat16)


def draw_send_rows(key, part):
    keys = jax.random.split(key, N_DOM * 2)
    chosen = jax.vmap(lambda one_key: jax.random.permutation(one_key, PART_ROWS)[:BOUND_ROWS])(keys)
    return chosen.reshape(N_DOM, 2 * BOUND_ROWS).astype(jnp.int32)


def steps_of(stream_key, shape, cuts, least, high):
    gain = 1.0
    for dim, blocks in cuts:
        steps = jax.random.uniform(jax.random.fold_in(jax.random.fold_in(stream_key, 6), dim), (blocks,), jnp.float32, least / len(cuts), high / len(cuts))
        gain = gain * jnp.repeat(jnp.exp(steps), shape[dim] // blocks).reshape((-1,) + (1,) * (len(shape) - 1 - dim))
    return gain


def noise(rng, extent, spread, reach, shards=(), held_as=jnp.bfloat16):
    values = spread * jax.random.normal(rng, extent, jnp.float32)
    if shards:
        values = values * steps_of(rng, extent, shards, -0.22, 0.18)
    return jnp.clip(values, -reach, reach).astype(held_as)


def setup_inputs(seed: int = 0) -> dict:
    key_of = jax.random.split(jax.random.key(seed), 7)
    feats = noise(key_of[0], (NODES, WIDTH), 1.0, 6.0, ((0, 16),))
    adj_local = draw_adj_local(jax.random.fold_in(key_of[6], 71), 0)
    couple = draw_couple(jax.random.fold_in(key_of[6], 71), 0)
    send_rows = draw_send_rows(jax.random.fold_in(key_of[6], 71), 0)
    weights = noise(key_of[4], (N_SEGMENT * WIDTH, WIDTH), WIDTH ** -0.5, 0.25, ((0, 2),))
    cotangent = noise(key_of[5], (NODES, WIDTH), (NODES // 256) ** -0.5, 1.5, ((0, 16),))
    return {"feats": feats, "adj_local": adj_local, "couple": couple, "send_rows": send_rows, "weights": weights, "cotangent": cotangent}


RESIDUAL_SHARE = 0.1
BETA_SCALE = 0.5


def silu_slope(preact):
    sigmoid_z = jax.nn.sigmoid(preact)
    return sigmoid_z * (1.0 + preact * (1.0 - sigmoid_z))


def add_rows(grad_part, row_index, values):
    return grad_part.at[row_index].add(values)


def reference(feats, adj_local, couple, send_rows, weights, cotangent):
    share = RESIDUAL_SHARE
    first_acts = feats.reshape(N_DOM, PART_ROWS, WIDTH)
    adjacency = adj_local.reshape(N_DOM, PART_ROWS, PART_ROWS).astype(jnp.float32)
    coupling = couple.reshape(N_DOM, PART_ROWS, 2 * BOUND_ROWS).astype(jnp.float32)
    sending = send_rows.astype(jnp.int32)
    parts = jnp.arange(N_DOM, dtype=jnp.int32)
    near_part = jnp.bitwise_xor(parts, 1)
    far_part = jnp.bitwise_xor(parts, N_DOM // 2)
    layer_weights = weights.reshape(N_SEGMENT, WIDTH, WIDTH).astype(jnp.float32)
    inputs = first_acts
    mixes = []
    preacts = []
    outputs = []
    betas = []
    for depth in range(N_SEGMENT):
        beta_coef = jnp.log(BETA_SCALE / (jnp.float32(depth) + 1.0) + 1.0)
        betas.append(beta_coef)
        outgoing = jnp.take_along_axis(inputs, sending[:, :, None], axis=1)
        incoming = jnp.concatenate([outgoing[near_part, :BOUND_ROWS], outgoing[far_part, BOUND_ROWS:]], axis=1)
        aggregate = jnp.einsum('pij,pjh->pih', adjacency, inputs.astype(jnp.float32))
        aggregate = aggregate + jnp.einsum('pik,pkh->pih', coupling, incoming.astype(jnp.float32))
        mixed = ((1.0 - share) * aggregate + share * first_acts.astype(jnp.float32)).astype(jnp.bfloat16)
        mixed_f = mixed.astype(jnp.float32)
        preact = (1.0 - beta_coef) * mixed_f + beta_coef * jnp.einsum('pnh,hk->pnk', mixed_f, layer_weights[depth])
        inputs = jax.nn.silu(preact).astype(jnp.bfloat16)
        mixes.append(mixed)
        preacts.append(preact)
        outputs.append(inputs)
    upstream = cotangent.reshape(N_DOM, PART_ROWS, WIDTH)
    accum = jnp.zeros((N_DOM, PART_ROWS, WIDTH), jnp.float32)
    weight_grads = [None] * N_SEGMENT
    grad_full = accum
    for depth in range(N_SEGMENT - 1, -1, -1):
        beta_coef = betas[depth]
        grad_pre = (upstream.astype(jnp.float32) * silu_slope(preacts[depth])).astype(jnp.bfloat16)
        grad_pre_f = grad_pre.astype(jnp.float32)
        weight_grads[depth] = beta_coef * jnp.einsum('pnh,pnk->hk', mixes[depth].astype(jnp.float32), grad_pre_f)
        grad_mix = ((1.0 - beta_coef) * grad_pre_f + beta_coef * jnp.einsum('pnk,hk->pnh', grad_pre_f, layer_weights[depth])).astype(jnp.bfloat16)
        grad_mix_f = grad_mix.astype(jnp.float32)
        backward_rows = ((1.0 - share) * jnp.einsum('pik,pih->pkh', coupling, grad_mix_f)).astype(jnp.bfloat16)
        returned = jnp.concatenate([backward_rows[near_part, :BOUND_ROWS], backward_rows[far_part, BOUND_ROWS:]], axis=1)
        grad_full = (1.0 - share) * jnp.einsum('pji,pjh->pih', adjacency, grad_mix_f)
        grad_full = jax.vmap(add_rows)(grad_full, sending, returned.astype(jnp.float32))
        accum = accum + share * grad_mix_f
        upstream = grad_full.astype(jnp.bfloat16)
    acts = jnp.stack([item.reshape(N_DOM * PART_ROWS, WIDTH) for item in outputs])
    grad_weights = jnp.stack(weight_grads)
    grad_feats = (grad_full + accum).reshape(N_DOM * PART_ROWS, WIDTH)
    return acts, grad_weights, grad_feats
```

```python
import jax
import jax.numpy as jnp
from jax import lax
from jax.sharding import PartitionSpec as P

SHARE = 0.1
BETA_SCALE = 0.5
BF16 = jnp.bfloat16
F32 = jnp.float32


def swapped(x, mask):
    return lax.ppermute(x, "dom", [(i, i ^ mask) for i in range(lax.axis_size("dom"))])


def across(x, shift):
    n = lax.axis_size("segment")
    return lax.ppermute(x, "segment", [(i, (i + shift) % n) for i in range(n)])


def gathered(piece, seg):
    n = lax.axis_size("segment")
    if n == 1:
        return piece
    if n == 2:
        other = across(piece, 1)
        first = seg == 0
        return jnp.concatenate([jnp.where(first, piece, other), jnp.where(first, other, piece)], axis=0)
    parts = jnp.stack([piece] + [across(piece, n - k) for k in range(1, n)])
    order = (jnp.arange(n, dtype=jnp.int32) - seg) % n
    return parts[order].reshape((-1,) + piece.shape[1:])


def chosen(items, seg):
    out = items[0]
    for k in range(1, len(items)):
        out = jnp.where(seg == k, items[k], out)
    return out


def mm(a, b):
    return jnp.dot(a, b, preferred_element_type=F32)


def mm_t(a, b):
    return lax.dot_general(a, b, (((0,), (0,)), ((), ())), preferred_element_type=F32)


def on_device(feats, adj, couple, send_rows, weights, cot):
    seg = lax.axis_index("segment")
    layers = lax.axis_size("segment")
    n_dom = lax.axis_size("dom")
    top = n_dom // 2
    rows, width = feats.shape
    piece = rows // layers
    bound = couple.shape[1] // 2

    ac = jnp.concatenate([adj, couple], axis=1)
    sr_row = jnp.zeros((16, ac.shape[1]), BF16).at[0, : send_rows.shape[1]].set(send_rows[0].astype(BF16))
    ac_mine = jnp.concatenate([lax.dynamic_slice_in_dim(ac, seg * piece, piece, 0), sr_row], axis=0)
    f_mine = lax.dynamic_slice_in_dim(feats, seg * piece, piece, 0)
    c_mine = lax.dynamic_slice_in_dim(cot, seg * piece, piece, 0)

    fwd_mine = jnp.concatenate([f_mine, ac_mine], axis=0)
    far_fwd = swapped(fwd_mine, top)
    near_fwd = swapped(fwd_mine, 1)
    far_cot = swapped(c_mine, top)
    near_cot = swapped(c_mine, 1)
    diag_fwd = swapped(far_fwd, 1)
    diag_cot = swapped(far_cot, 1)

    all_w = gathered(weights, seg).reshape(layers, width, width)

    def spread(got):
        both = gathered(got[None], seg)
        f = both[:, :piece].reshape(rows, width)
        a = both[:, piece : 2 * piece].reshape(rows, -1)
        s = both[0, 2 * piece, : 2 * bound]
        return f, a, s

    own = (feats, ac, send_rows[0].astype(BF16))
    groups = [own] + [spread(g) for g in (near_fwd, far_fwd, diag_fwd)]
    x0 = [g[0] for g in groups]
    ids = lax.broadcasted_iota(jnp.int32, (2 * bound, rows), 1).astype(F32)
    picks = [(g[2].astype(F32)[:, None] == ids).astype(BF16) for g in groups]
    blocks = []
    for r in range(4):
        a = groups[r][1]
        near_blk = mm(a[:, rows : rows + bound], picks[r ^ 1][:bound]).astype(BF16)
        far_blk = mm(a[:, rows + bound :], picks[r ^ 2][bound:]).astype(BF16)
        blocks.append((a[:, :rows], near_blk, far_blk))

    betas = [jnp.log(BETA_SCALE / (jnp.float32(k) + 1.0) + 1.0) for k in range(layers)]
    xs = x0
    mixes, pres, outs = [], [], []
    for k in range(layers):
        mixed = []
        for r in range(4):
            own_b, near_b, far_b = blocks[r]
            agg = mm(own_b, xs[r]) + mm(near_b, xs[r ^ 1]) + mm(far_b, xs[r ^ 2])
            mixed.append(((1.0 - SHARE) * agg + SHARE * x0[r].astype(F32)).astype(BF16))
        pre = [(1.0 - betas[k]) * m.astype(F32) + betas[k] * mm(m, all_w[k]) for m in mixed]
        xs = [jax.nn.silu(p).astype(BF16) for p in pre]
        mixes.append(mixed)
        pres.append(pre)
        outs.append(xs[0])

    acts = chosen(outs, seg)

    ups = [cot] + [gathered(g, seg) for g in (near_cot, far_cot, diag_cot)]
    ups = [u.astype(BF16) for u in ups]
    others = n_dom // 4
    out_rows = width // n_dom
    dom = lax.axis_index("dom")
    low = dom & 1
    high = dom // top
    grads = []
    carried = jnp.zeros((rows, width), F32)
    full = None
    for k in range(layers - 1, -1, -1):
        dpre = []
        for r in range(4):
            sg = jax.nn.sigmoid(pres[k][r])
            slope = sg * (1.0 + pres[k][r] * (1.0 - sg))
            dpre.append((ups[r].astype(F32) * slope).astype(BF16))
        mix_all = jnp.concatenate(mixes[k], axis=0)
        cols = mix_all.reshape(4 * rows, 2, others, 2, out_rows)
        cols = lax.dynamic_index_in_dim(cols, high, 1, keepdims=False)
        cols = lax.dynamic_index_in_dim(cols, low, 2, keepdims=False)
        grads.append(betas[k] * mm_t(cols.reshape(4 * rows, others * out_rows), jnp.concatenate(dpre, axis=0)))
        dmix = [
            (
                (1.0 - betas[k]) * d.astype(F32)
                + betas[k] * lax.dot_general(d, all_w[k], (((1,), (1,)), ((), ())), preferred_element_type=F32)
            ).astype(BF16)
            for d in dpre
        ]
        carried = carried + SHARE * dmix[0].astype(F32)
        wanted = range(4) if k else range(1)
        full = [
            (1.0 - SHARE)
            * (mm_t(blocks[r][0], dmix[r]) + mm_t(blocks[r ^ 1][1], dmix[r ^ 1]) + mm_t(blocks[r ^ 2][2], dmix[r ^ 2]))
            for r in wanted
        ]
        ups = [f.astype(BF16) for f in full]

    total = full[0] + carried
    feat_grads = lax.dynamic_slice_in_dim(total, seg * (width // layers), width // layers, 1)

    part = chosen(grads[::-1], seg).reshape(others, out_rows, width)
    place = (dom // 2) % others
    wgrad = lax.dynamic_index_in_dim(part, place, 0, keepdims=False)
    for m in range(1, others):
        block = lax.dynamic_index_in_dim(part, place ^ m, 0, keepdims=False).astype(BF16)
        wgrad = wgrad + swapped(block, 2 * m).astype(F32)
    return (acts[None], wgrad[None], feat_grads)


def solution(mesh):
    in_specs = (
        P("dom", None),
        P("dom", None),
        P("dom", None),
        P("dom", None),
        P("segment", None),
        P("dom", None),
    )
    out_specs = (P("segment", "dom", None), P("segment", "dom", None), P("dom", "segment"))
    return jax.shard_map(on_device, mesh=mesh, in_specs=in_specs, out_specs=out_specs, check_vma=False)
```

```python
import math

import jax
import jax.numpy as jnp
from jax import lax
from jax.experimental import pallas as pl
from jax.experimental.pallas import tpu as pltpu
from jax.sharding import PartitionSpec as P

SHARE = 0.1
BETA_SCALE = 0.5
BF16 = jnp.bfloat16
F32 = jnp.float32


def swapped(x, mask):
    return lax.ppermute(x, "dom", [(i, i ^ mask) for i in range(lax.axis_size("dom"))])


def every_piece(x):
    n = lax.axis_size("segment")
    return [x] + [lax.ppermute(x, "segment", [(i, (i + k) % n) for i in range(n)]) for k in range(1, n)]


def beta_of(k):
    return math.log(BETA_SCALE / (k + 1.0) + 1.0)


def mm(a, b):
    return jnp.dot(a, b, preferred_element_type=F32)


def mm_nt(a, b):
    return lax.dot_general(a, b, (((1,), (1,)), ((), ())), preferred_element_type=F32)


def mm_tn(a, b):
    return lax.dot_general(a, b, (((0,), (0,)), ((), ())), preferred_element_type=F32)


def place_of(seg, k, n):
    return lax.rem(seg - k + n, n)


def forward_call(scalars, feats, adj, couple, send_rows, got, w_pieces):
    layers = len(w_pieces)
    rows, width = feats.shape
    piece = rows // layers
    bound = couple.shape[1] // 2

    def body(sc, feats_r, adj_r, couple_r, sr_r, *refs):
        got_r = [refs[g * layers : (g + 1) * layers] for g in range(3)]
        w_r = refs[3 * layers : 4 * layers]
        acts_o, mix_o, slope_o, blocks_o, w_o, x_s, ac_s = refs[4 * layers :]
        seg = sc[0]
        x_s[0] = feats_r[...]
        for g in range(3):
            for k in range(layers):
                at = pl.multiple_of(place_of(seg, k, layers) * piece, piece)
                x_s[g + 1, pl.ds(at, piece), :] = got_r[g][k][:piece, :]
                ac_s[g, pl.ds(at, piece), :] = got_r[g][k][piece : 2 * piece, :]
        for k in range(layers):
            w_o[place_of(seg, k, layers)] = w_r[k][...]
        ids = lax.broadcasted_iota(jnp.int32, (rows, 2 * bound), 0)
        picks = []
        for g in range(4):
            sr = sr_r[...] if g == 0 else got_r[g - 1][0][2 * piece : 2 * piece + 1, : 2 * bound].astype(F32).astype(jnp.int32)
            picks.append((ids == sr).astype(F32).astype(BF16))
        for g in range(4):
            own = adj_r[...] if g == 0 else ac_s[g - 1, :, :rows]
            cp = couple_r[...] if g == 0 else ac_s[g - 1, :, rows:]
            blocks_o[g, :, :rows] = own
            blocks_o[g, :, rows : 2 * rows] = mm_nt(cp[:, :bound], picks[g ^ 1][:, :bound]).astype(BF16)
            blocks_o[g, :, 2 * rows :] = mm_nt(cp[:, bound:], picks[g ^ 2][:, bound:]).astype(BF16)
        for k in range(layers):
            beta = beta_of(k)
            src = 0 if k == 0 else 4 + 4 * (k % 2)
            dst = 4 + 4 * ((k + 1) % 2)
            for g in range(4):
                agg = (
                    mm(blocks_o[g, :, :rows], x_s[src + g])
                    + mm(blocks_o[g, :, rows : 2 * rows], x_s[src + (g ^ 1)])
                    + mm(blocks_o[g, :, 2 * rows :], x_s[src + (g ^ 2)])
                )
                mixed = ((1.0 - SHARE) * agg + SHARE * x_s[g].astype(F32)).astype(BF16)
                mix_o[k, g] = mixed
                pre = (1.0 - beta) * mixed.astype(F32) + beta * mm(mixed, w_o[k])
                sig = 1.0 / (1.0 + jnp.exp(-pre))
                slope_o[k, g] = sig * (1.0 + pre * (1.0 - sig))
                out = (pre * sig).astype(BF16)
                if k + 1 < layers:
                    x_s[dst + g] = out
                if g == 0:

                    @pl.when(seg == k)
                    def _():
                        acts_o[...] = out

    n_in = 4 + 4 * layers
    vm = pl.BlockSpec(memory_space=pltpu.VMEM)
    return pl.pallas_call(
        body,
        out_shape=(
            jax.ShapeDtypeStruct((rows, width), BF16),
            jax.ShapeDtypeStruct((layers, 4, rows, width), BF16),
            jax.ShapeDtypeStruct((layers, 4, rows, width), F32),
            jax.ShapeDtypeStruct((4, rows, 3 * rows), BF16),
            jax.ShapeDtypeStruct((layers, width, width), BF16),
        ),
        in_specs=[pl.BlockSpec(memory_space=pltpu.SMEM)] + [vm] * n_in,
        out_specs=(vm,) * 5,
        scratch_shapes=[pltpu.VMEM((12, rows, width), BF16), pltpu.VMEM((3, rows, 2 * rows), BF16)],
        name="forward",
    )(scalars, feats, adj, couple, send_rows, *[p for g in got for p in g], *w_pieces)


def backward_call(scalars, cot, got, mix, slope, blocks, w):
    layers = w.shape[0]
    rows, width = cot.shape
    piece = rows // layers
    n_dom = lax.axis_size("dom")
    others = n_dom // 4
    out_rows = width // n_dom
    half = width // 2
    cols = width // layers

    def body(sc, cot_r, *refs):
        got_r = [refs[g * layers : (g + 1) * layers] for g in range(3)]
        mix_r, slope_r, blocks_r, w_r = refs[3 * layers : 3 * layers + 4]
        outs = refs[3 * layers + 4 :]
        feat_o, own_o = outs[:2]
        send_o = outs[2 : 1 + others]
        up_s, dpre_s, dmix_s, carry_s, part_s = outs[1 + others :]
        seg, low, high, place = sc[0], sc[1], sc[2], sc[3]
        for g in range(3):
            for k in range(layers):
                at = pl.multiple_of(place_of(seg, k, layers) * piece, piece)
                up_s[g + 1, pl.ds(at, piece), :] = got_r[g][k][...].astype(F32)
        up_s[0] = cot_r[...].astype(F32)
        for k in range(layers - 1, -1, -1):
            beta = beta_of(k)
            for g in range(4):
                up = up_s[g]
                if k + 1 < layers:
                    up = up.astype(BF16).astype(F32)
                dpre = (up * slope_r[k, g]).astype(BF16)
                dpre_s[pl.ds(g * rows, rows), :] = dpre
                if k or g < 3:
                    dmix = ((1.0 - beta) * dpre.astype(F32) + beta * mm_nt(dpre, w_r[k])).astype(BF16)
                    dmix_s[g] = dmix
                if g == 0:
                    carry_s[...] = SHARE * dmix.astype(F32) + (carry_s[...] if k + 1 < layers else 0.0)

            @pl.when(seg == k)
            def _():
                part = jnp.zeros((half, width), F32)
                for g in range(4):
                    chosen = mix_r[k, g, :, pl.ds(pl.multiple_of(high * half, half), half)]
                    part = part + mm_tn(chosen, dpre_s[pl.ds(g * rows, rows), :])
                part_s[...] = beta * part

            if k:
                for g in range(4):
                    up_s[g] = (1.0 - SHARE) * (
                        mm_tn(blocks_r[g, :, :rows], dmix_s[g])
                        + mm_tn(blocks_r[g ^ 1, :, rows : 2 * rows], dmix_s[g ^ 1])
                        + mm_tn(blocks_r[g ^ 2, :, 2 * rows :], dmix_s[g ^ 2])
                    )

        def block(m):
            at = (place ^ m) * (2 * out_rows) + low * out_rows
            return part_s[pl.ds(pl.multiple_of(at, out_rows), out_rows), :]

        own_o[...] = block(0)
        for m in range(1, others):
            send_o[m - 1][...] = block(m).astype(BF16)
        if cols % 128 == 0:
            at = pl.ds(pl.multiple_of(seg * cols, cols), cols)
            feat_o[...] = (
                (1.0 - SHARE)
                * (
                    mm_tn(blocks_r[0, :, :rows], dmix_s[0, :, at])
                    + mm_tn(blocks_r[1, :, rows : 2 * rows], dmix_s[1, :, at])
                    + mm_tn(blocks_r[2, :, 2 * rows :], dmix_s[2, :, at])
                )
                + carry_s[:, at]
            )
        else:
            feat_o[...] = (1.0 - SHARE) * (
                mm_tn(blocks_r[0, :, :rows], dmix_s[0])
                + mm_tn(blocks_r[1, :, rows : 2 * rows], dmix_s[1])
                + mm_tn(blocks_r[2, :, 2 * rows :], dmix_s[2])
            ) + carry_s[...]

    n_in = 1 + 3 * layers + 4
    vm = pl.BlockSpec(memory_space=pltpu.VMEM)
    feat_cols = cols if cols % 128 == 0 else width
    got_out = pl.pallas_call(
        body,
        out_shape=(jax.ShapeDtypeStruct((rows, feat_cols), F32), jax.ShapeDtypeStruct((out_rows, width), F32))
        + tuple(jax.ShapeDtypeStruct((out_rows, width), BF16) for _ in range(1, others)),
        in_specs=[pl.BlockSpec(memory_space=pltpu.SMEM)] + [vm] * n_in,
        out_specs=(vm,) * (1 + others),
        scratch_shapes=[
            pltpu.VMEM((4, rows, width), F32),
            pltpu.VMEM((4 * rows, width), BF16),
            pltpu.VMEM((4, rows, width), BF16),
            pltpu.VMEM((rows, width), F32),
            pltpu.VMEM((half, width), F32),
        ],
        name="backward",
    )(scalars, cot, *[p for g in got for p in g], mix, slope, blocks, w)
    feat, own = got_out[:2]
    if cols % 128:
        feat = lax.dynamic_slice_in_dim(feat, scalars[0] * cols, cols, 1)
    return feat, own, got_out[2:]


def on_device(feats, adj, couple, send_rows, weights, cot):
    seg = lax.axis_index("segment")
    dom = lax.axis_index("dom")
    layers = lax.axis_size("segment")
    n_dom = lax.axis_size("dom")
    top = n_dom // 2
    others = n_dom // 4
    rows, width = feats.shape
    piece = rows // layers
    place = (dom // 2) % others
    scalars = jnp.stack([seg, dom & 1, dom // top, place]).astype(jnp.int32)

    ac = jnp.concatenate([adj, couple], axis=1)
    sr_row = jnp.zeros((16, width), BF16).at[0, : send_rows.shape[1]].set(send_rows[0].astype(BF16))

    def mine(x):
        return lax.dynamic_slice_in_dim(x, seg * piece, piece, 0)

    fwd_mine = jnp.concatenate([mine(feats), mine(ac), sr_row], axis=0)
    cot_mine = mine(cot)
    far_fwd = swapped(fwd_mine, top)
    near_fwd = swapped(fwd_mine, 1)
    far_cot = swapped(cot_mine, top)
    near_cot = swapped(cot_mine, 1)
    diag_fwd = swapped(far_fwd, 1)
    diag_cot = swapped(far_cot, 1)
    w_pieces = every_piece(weights)

    acts, mix, slope, blocks, w = forward_call(
        scalars, feats, adj, couple, send_rows, [every_piece(x) for x in (near_fwd, far_fwd, diag_fwd)], w_pieces
    )
    feat, wgrad, sends = backward_call(
        scalars, cot, [every_piece(x) for x in (near_cot, far_cot, diag_cot)], mix, slope, blocks, w
    )
    for m in range(1, others):
        wgrad = wgrad + swapped(sends[m - 1], 2 * m).astype(F32)
    return (acts[None], wgrad[None], feat)


def solution(mesh):
    in_specs = (
        P("dom", None),
        P("dom", None),
        P("dom", None),
        P("dom", None),
        P("segment", None),
        P("dom", None),
    )
    out_specs = (P("segment", "dom", None), P("segment", "dom", None), P("dom", "segment"))
    return jax.shard_map(on_device, mesh=mesh, in_specs=in_specs, out_specs=out_specs, check_vma=False)
```

```python
import math

import jax
import jax.numpy as jnp
from jax import lax
from jax.experimental import pallas as pl
from jax.experimental.pallas import tpu as pltpu
from jax.sharding import PartitionSpec as P


SHARE = 0.1
BETA_SCALE = 0.5
BF16 = jnp.bfloat16
F32 = jnp.float32


def vmem_of(layers):
    return min(60, 14 + 6 * layers) << 20


def swapped(x, mask):
    return lax.ppermute(x, "dom", [(i, i ^ mask) for i in range(lax.axis_size("dom"))])


def every_piece(x):
    n = lax.axis_size("segment")
    return [x] + [lax.ppermute(x, "segment", [(i, (i + k) % n) for i in range(n)]) for k in range(1, n)]


def beta_of(k):
    return math.log(BETA_SCALE / (k + 1.0) + 1.0)


def mm(a, b):
    return jnp.dot(a, b, preferred_element_type=F32)


def mm_nt(a, b):
    return lax.dot_general(a, b, (((1,), (1,)), ((), ())), preferred_element_type=F32)


def mm_tn(a, b):
    return lax.dot_general(a, b, (((0,), (0,)), ((), ())), preferred_element_type=F32)


def place_of(seg, k, n):
    return lax.rem(seg - k + n, n)


def first_layer_call(scalars, feats, adj, couple, send_rows, got, w_pieces):
    layers = len(w_pieces)
    rows, width = feats.shape
    piece = rows // layers
    bound = couple.shape[1] // 2

    def body(sc, feats_r, adj_r, couple_r, sr_r, *refs):
        got_r = [refs[g * layers : (g + 1) * layers] for g in range(3)]
        w_r = refs[3 * layers : 4 * layers]
        x0_o, x1_o, mix_o, slope_o, blocks_o, w_o, ac_s = refs[4 * layers :]
        seg = sc[0]
        x0_o[0] = feats_r[...]
        for g in range(3):
            for k in range(layers):
                at = pl.multiple_of(place_of(seg, k, layers) * piece, piece)
                x0_o[g + 1, pl.ds(at, piece), :] = got_r[g][k][:piece, :]
                ac_s[g, pl.ds(at, piece), :] = got_r[g][k][piece : 2 * piece, :]
        for k in range(layers):
            w_o[place_of(seg, k, layers)] = w_r[k][...]
        ids = lax.broadcasted_iota(jnp.int32, (rows, 2 * bound), 0)
        picks = []
        for g in range(4):
            sr = sr_r[...] if g == 0 else got_r[g - 1][0][2 * piece : 2 * piece + 1, : 2 * bound].astype(F32).astype(jnp.int32)
            picks.append((ids == sr).astype(F32).astype(BF16))
        for g in range(4):
            own = adj_r[...] if g == 0 else ac_s[g - 1, :, :rows]
            cp = couple_r[...] if g == 0 else ac_s[g - 1, :, rows:]
            blocks_o[g, :, :rows] = own
            blocks_o[g, :, rows : 2 * rows] = mm_nt(cp[:, :bound], picks[g ^ 1][:, :bound]).astype(BF16)
            blocks_o[g, :, 2 * rows :] = mm_nt(cp[:, bound:], picks[g ^ 2][:, bound:]).astype(BF16)
        for g in range(4):
            mixed, slope, out = layer_of(0, g, blocks_o, x0_o, x0_o, w_o)
            mix_o[g] = mixed
            slope_o[g] = slope
            x1_o[g] = out

    n_in = 4 + 4 * layers
    vm = pl.BlockSpec(memory_space=pltpu.VMEM)
    return pl.pallas_call(
        body,
        out_shape=(
            jax.ShapeDtypeStruct((4, rows, width), BF16),
            jax.ShapeDtypeStruct((4, rows, width), BF16),
            jax.ShapeDtypeStruct((4, rows, width), BF16),
            jax.ShapeDtypeStruct((4, rows, width), F32),
            jax.ShapeDtypeStruct((4, rows, 3 * rows), BF16),
            jax.ShapeDtypeStruct((layers, width, width), BF16),
        ),
        in_specs=[pl.BlockSpec(memory_space=pltpu.SMEM)] + [vm] * n_in,
        out_specs=(vm,) * 6,
        scratch_shapes=[pltpu.VMEM((3, rows, 2 * rows), BF16)],
        compiler_params=pltpu.CompilerParams(vmem_limit_bytes=vmem_of(layers)),
        name="first_layer",
    )(scalars, feats, adj, couple, send_rows, *[p for g in got for p in g], *w_pieces)


def layer_of(k, g, blocks, x_in, x0, w):
    rows = x_in.shape[1]
    beta = beta_of(k)
    agg = (
        mm(blocks[g, :, :rows], x_in[g])
        + mm(blocks[g, :, rows : 2 * rows], x_in[g ^ 1])
        + mm(blocks[g, :, 2 * rows :], x_in[g ^ 2])
    )
    mixed = ((1.0 - SHARE) * agg + SHARE * x0[g].astype(F32)).astype(BF16)
    pre = (1.0 - beta) * mixed.astype(F32) + beta * mm(mixed, w[k])
    sig = 1.0 / (1.0 + jnp.exp(-pre))
    return mixed, sig * (1.0 + pre * (1.0 - sig)), (pre * sig).astype(BF16)


def later_layers_call(scalars, x0, x1, blocks, w):
    layers = w.shape[0]
    rows, width = x0.shape[1:]

    def body(sc, x0_r, x1_r, blocks_r, w_r, acts_o, mix_o, slope_o, xa_s, xb_s):
        seg = sc[0]

        @pl.when(seg == 0)
        def _():
            acts_o[...] = x1_r[0]

        src = x1_r
        for k in range(1, layers):
            dst = (xa_s, xb_s)[k % 2]
            for g in range(4):
                mixed, slope, out = layer_of(k, g, blocks_r, src, x0_r, w_r)
                mix_o[k - 1, g] = mixed
                slope_o[k - 1, g] = slope
                if k + 1 < layers:
                    dst[g] = out
                if g == 0:

                    @pl.when(seg == k)
                    def _():
                        acts_o[...] = out

            src = dst

    vm = pl.BlockSpec(memory_space=pltpu.VMEM)
    return pl.pallas_call(
        body,
        out_shape=(
            jax.ShapeDtypeStruct((rows, width), BF16),
            jax.ShapeDtypeStruct((layers - 1, 4, rows, width), BF16),
            jax.ShapeDtypeStruct((layers - 1, 4, rows, width), F32),
        ),
        in_specs=[pl.BlockSpec(memory_space=pltpu.SMEM)] + [vm] * 4,
        out_specs=(vm,) * 3,
        scratch_shapes=[pltpu.VMEM((4, rows, width), BF16)] * 2,
        compiler_params=pltpu.CompilerParams(vmem_limit_bytes=vmem_of(layers)),
        name="later_layers",
    )(scalars, x0, x1, blocks, w)


def backward_call(scalars, cot, got, mix, slope, later_mix, later_slope, blocks, w):
    layers = w.shape[0]
    rows, width = cot.shape
    piece = rows // layers
    n_dom = lax.axis_size("dom")
    others = n_dom // 4
    out_rows = width // n_dom
    half = width // 2
    cols = width // layers

    def body(sc, cot_r, *refs):
        got_r = [refs[g * layers : (g + 1) * layers] for g in range(3)]
        mix_r, slope_r, later_mix_r, later_slope_r, blocks_r, w_r = refs[3 * layers : 3 * layers + 6]
        outs = refs[3 * layers + 6 :]
        feat_o, own_o = outs[:2]
        send_o = outs[2 : 1 + others]
        up_s, dpre_s, dmix_s, carry_s, part_s = outs[1 + others :]
        seg, low, high, place = sc[0], sc[1], sc[2], sc[3]
        for g in range(3):
            for k in range(layers):
                at = pl.multiple_of(place_of(seg, k, layers) * piece, piece)
                up_s[g + 1, pl.ds(at, piece), :] = got_r[g][k][...].astype(F32)
        up_s[0] = cot_r[...].astype(F32)
        for k in range(layers - 1, -1, -1):
            beta = beta_of(k)
            for g in range(4):
                up = up_s[g]
                if k + 1 < layers:
                    up = up.astype(BF16).astype(F32)
                dpre = (up * (later_slope_r[k - 1, g] if k else slope_r[g])).astype(BF16)
                dpre_s[pl.ds(g * rows, rows), :] = dpre
                if k or g < 3:
                    dmix = ((1.0 - beta) * dpre.astype(F32) + beta * mm_nt(dpre, w_r[k])).astype(BF16)
                    dmix_s[g] = dmix
                if g == 0:
                    carry_s[...] = SHARE * dmix.astype(F32) + (carry_s[...] if k + 1 < layers else 0.0)

            @pl.when(seg == k)
            def _():
                part = jnp.zeros((half, width), F32)
                for g in range(4):
                    at = pl.ds(pl.multiple_of(high * half, half), half)
                    chosen = later_mix_r[k - 1, g, :, at] if k else mix_r[g, :, at]
                    part = part + mm_tn(chosen, dpre_s[pl.ds(g * rows, rows), :])
                part_s[...] = beta * part

            if k:
                for g in range(4):
                    up_s[g] = (1.0 - SHARE) * (
                        mm_tn(blocks_r[g, :, :rows], dmix_s[g])
                        + mm_tn(blocks_r[g ^ 1, :, rows : 2 * rows], dmix_s[g ^ 1])
                        + mm_tn(blocks_r[g ^ 2, :, 2 * rows :], dmix_s[g ^ 2])
                    )

        def block(m):
            at = (place ^ m) * (2 * out_rows) + low * out_rows
            return part_s[pl.ds(pl.multiple_of(at, out_rows), out_rows), :]

        own_o[...] = block(0)
        for m in range(1, others):
            send_o[m - 1][...] = block(m).astype(BF16)
        if cols % 128 == 0:
            at = pl.ds(pl.multiple_of(seg * cols, cols), cols)
            feat_o[...] = (
                (1.0 - SHARE)
                * (
                    mm_tn(blocks_r[0, :, :rows], dmix_s[0, :, at])
                    + mm_tn(blocks_r[1, :, rows : 2 * rows], dmix_s[1, :, at])
                    + mm_tn(blocks_r[2, :, 2 * rows :], dmix_s[2, :, at])
                )
                + carry_s[:, at]
            )
        else:
            feat_o[...] = (1.0 - SHARE) * (
                mm_tn(blocks_r[0, :, :rows], dmix_s[0])
                + mm_tn(blocks_r[1, :, rows : 2 * rows], dmix_s[1])
                + mm_tn(blocks_r[2, :, 2 * rows :], dmix_s[2])
            ) + carry_s[...]

    n_in = 1 + 3 * layers + 6
    vm = pl.BlockSpec(memory_space=pltpu.VMEM)
    feat_cols = cols if cols % 128 == 0 else width
    got_out = pl.pallas_call(
        body,
        out_shape=(jax.ShapeDtypeStruct((rows, feat_cols), F32), jax.ShapeDtypeStruct((out_rows, width), F32))
        + tuple(jax.ShapeDtypeStruct((out_rows, width), BF16) for _ in range(1, others)),
        in_specs=[pl.BlockSpec(memory_space=pltpu.SMEM)] + [vm] * n_in,
        out_specs=(vm,) * (1 + others),
        scratch_shapes=[
            pltpu.VMEM((4, rows, width), F32),
            pltpu.VMEM((4 * rows, width), BF16),
            pltpu.VMEM((4, rows, width), BF16),
            pltpu.VMEM((rows, width), F32),
            pltpu.VMEM((half, width), F32),
        ],
        compiler_params=pltpu.CompilerParams(vmem_limit_bytes=vmem_of(layers)),
        name="backward",
    )(scalars, cot, *[p for g in got for p in g], mix, slope, later_mix, later_slope, blocks, w)
    feat, own = got_out[:2]
    if cols % 128:
        feat = lax.dynamic_slice_in_dim(feat, scalars[0] * cols, cols, 1)
    return feat, own, got_out[2:]


def step(feats, adj, couple, send_rows, weights, cot):
    seg = lax.axis_index("segment")
    dom = lax.axis_index("dom")
    layers = lax.axis_size("segment")
    n_dom = lax.axis_size("dom")
    top = n_dom // 2
    others = n_dom // 4
    rows, width = feats.shape
    piece = rows // layers
    place = (dom // 2) % others
    scalars = jnp.stack([seg, dom & 1, dom // top, place]).astype(jnp.int32)

    ac = jnp.concatenate([adj, couple], axis=1)
    sr_row = jnp.zeros((16, width), BF16).at[0, : send_rows.shape[1]].set(send_rows[0].astype(BF16))

    def mine(x):
        return lax.dynamic_slice_in_dim(x, seg * piece, piece, 0)

    fwd_mine = jnp.concatenate([mine(feats), mine(ac), sr_row], axis=0)
    cot_mine = mine(cot)
    far_fwd = swapped(fwd_mine, top)
    near_fwd = swapped(fwd_mine, 1)
    far_cot = swapped(cot_mine, top)
    near_cot = swapped(cot_mine, 1)
    w_pieces = every_piece(weights)
    near_fwd = every_piece(near_fwd)
    diag_fwd = swapped(far_fwd, 1)
    far_fwd = every_piece(far_fwd)
    diag_cot = swapped(far_cot, 1)
    far_cot = every_piece(far_cot)
    near_cot = every_piece(near_cot)
    diag_fwd = every_piece(diag_fwd)
    x0, x1, mix, slope, blocks, w = first_layer_call(
        scalars, feats, adj, couple, send_rows, [near_fwd, far_fwd, diag_fwd], w_pieces
    )
    diag_cot = every_piece(diag_cot)
    acts, later_mix, later_slope = later_layers_call(scalars, x0, x1, blocks, w)
    feat, wgrad, sends = backward_call(
        scalars, cot, [near_cot, far_cot, diag_cot], mix, slope, later_mix, later_slope, blocks, w
    )
    for m in range(others - 1, 0, -1):
        wgrad = wgrad + swapped(sends[m - 1], 2 * m).astype(F32)
    return (acts[None], wgrad[None], feat)


def solution(mesh):
    in_specs = (
        P("dom", None),
        P("dom", None),
        P("dom", None),
        P("dom", None),
        P("segment", None),
        P("dom", None),
    )
    out_specs = (P("segment", "dom", None), P("segment", "dom", None), P("dom", "segment"))
    return jax.shard_map(step, mesh=mesh, in_specs=in_specs, out_specs=out_specs, check_vma=False)
```

```python
import math

import jax
import jax.numpy as jnp
from jax import lax
from jax.experimental import pallas as pl
from jax.experimental.pallas import tpu as pltpu
from jax.sharding import PartitionSpec as P


SHARE = 0.1
BETA_SCALE = 0.5
BF16 = jnp.bfloat16
F32 = jnp.float32


def vmem_of(layers):
    return min(60, 14 + 6 * layers) << 20


def swapped(x, mask):
    return lax.ppermute(x, "dom", [(i, i ^ mask) for i in range(lax.axis_size("dom"))])


def every_piece(x):
    n = lax.axis_size("segment")
    return [x] + [lax.ppermute(x, "segment", [(i, (i + k) % n) for i in range(n)]) for k in range(1, n)]


def beta_of(k):
    return math.log(BETA_SCALE / (k + 1.0) + 1.0)


def mm(a, b):
    return jnp.dot(a, b, preferred_element_type=F32)


def mm_nt(a, b):
    return lax.dot_general(a, b, (((1,), (1,)), ((), ())), preferred_element_type=F32)


def mm_tn(a, b):
    return lax.dot_general(a, b, (((0,), (0,)), ((), ())), preferred_element_type=F32)


def place_of(seg, k, n):
    return lax.rem(seg - k + n, n)


def pack_call(scalars, feats, adj, couple, send_rows, cot, layers):
    rows, width = feats.shape
    piece = rows // layers
    picked = send_rows.shape[1]

    def body(sc, feats_r, adj_r, couple_r, sr_r, cot_r, fwd_o, cot_o, sr_s, sems):
        at = pl.ds(pl.multiple_of(sc[0] * piece, piece), piece)
        split = adj_r.shape[1]
        copies = [
            pltpu.make_async_copy(feats_r.at[at, :], fwd_o.at[:piece, :], sems.at[0]),
            pltpu.make_async_copy(adj_r.at[at, :], fwd_o.at[piece : 2 * piece, :split], sems.at[1]),
            pltpu.make_async_copy(couple_r.at[at, :], fwd_o.at[piece : 2 * piece, split:], sems.at[2]),
            pltpu.make_async_copy(cot_r.at[at, :], cot_o, sems.at[3]),
        ]
        sr_copy = pltpu.make_async_copy(sr_r, sr_s, sems.at[4])
        sr_copy.start()
        for c in copies:
            c.start()
        fwd_o[2 * piece :, picked:] = jnp.zeros((16, width - picked), BF16)
        sr_copy.wait()
        fwd_o[2 * piece :, :picked] = jnp.broadcast_to(sr_s[...].astype(F32), (16, picked)).astype(BF16)
        for c in copies:
            c.wait()

    vm = pl.BlockSpec(memory_space=pltpu.VMEM)
    hbm = pl.BlockSpec(memory_space=pltpu.HBM)
    return pl.pallas_call(
        body,
        out_shape=(
            jax.ShapeDtypeStruct((2 * piece + 16, width), BF16),
            jax.ShapeDtypeStruct((piece, width), BF16),
        ),
        in_specs=[pl.BlockSpec(memory_space=pltpu.SMEM), hbm, hbm, hbm, hbm, hbm],
        out_specs=(vm, vm),
        scratch_shapes=[pltpu.VMEM(send_rows.shape, jnp.int32), pltpu.SemaphoreType.DMA((5,))],
        compiler_params=pltpu.CompilerParams(vmem_limit_bytes=4 << 20),
        name="pack",
    )(scalars, feats, adj, couple, send_rows, cot)


def picks_of(sr, rows):
    ids = lax.broadcasted_iota(jnp.int32, (rows, sr.shape[1]), 0).astype(F32)
    return (ids == sr).astype(F32).astype(BF16)


def mixed_of(agg, first):
    return ((1.0 - SHARE) * agg + SHARE * first.astype(F32)).astype(BF16)


def activate(mixed, w, k):
    beta = beta_of(k)
    pre = (1.0 - beta) * mixed.astype(F32) + beta * mm(mixed, w)
    sig = 1.0 / (1.0 + jnp.exp(-pre))
    out = pre * sig
    return sig + out * (1.0 - sig), out.astype(BF16)


def own_part_call(scalars, feats, adj, couple, send_rows, near, far, w_pieces):
    layers = len(w_pieces)
    rows, width = feats.shape
    piece = rows // layers
    bound = couple.shape[1] // 2

    def body(sc, feats_r, adj_r, couple_r, sr_r, *refs):
        got_r = [refs[g * layers : (g + 1) * layers] for g in range(2)]
        w_r = refs[2 * layers : 3 * layers]
        outs = refs[3 * layers :]
        x_o, own_o, near_o, far_o, cp_o, pick_o, agg_o, mix_o, slope_o, x1_o, w_o = outs[:11]
        ac_s, couple_s, sr_s, sems = outs[11:]
        seg = sc[0]
        copies = [
            pltpu.make_async_copy(sr_r, sr_s, sems.at[0]),
            pltpu.make_async_copy(couple_r, couple_s, sems.at[1]),
            pltpu.make_async_copy(feats_r, x_o.at[0], sems.at[2]),
            pltpu.make_async_copy(adj_r, own_o.at[0], sems.at[3]),
            pltpu.make_async_copy(w_r[0], w_o.at[seg], sems.at[4]),
        ]
        for c in copies:
            c.start()
        for g in range(2):
            for k in range(layers):
                at = pl.ds(pl.multiple_of(place_of(seg, k, layers) * piece, piece), piece)
                x_o[g + 1, at, :] = got_r[g][k][:piece, :]
                own_o[g + 1, at, :] = got_r[g][k][piece : 2 * piece, :rows]
                ac_s[g, at, :] = got_r[g][k][piece : 2 * piece, rows:]
        for k in range(1, layers):
            w_o[place_of(seg, k, layers)] = w_r[k][...]
        for c in copies:
            c.wait()
        picks = [picks_of(sr_s[...].astype(F32), rows)]
        for g in range(2):
            picks.append(picks_of(got_r[g][0][2 * piece : 2 * piece + 1, : 2 * bound].astype(F32), rows))
        near_o[0] = mm_nt(couple_s[:, :bound], picks[1][:, :bound]).astype(BF16)
        far_o[0] = mm_nt(couple_s[:, bound:], picks[2][:, bound:]).astype(BF16)
        near_o[1] = mm_nt(ac_s[0, :, :bound], picks[0][:, :bound]).astype(BF16)
        far_o[1] = mm_nt(ac_s[1, :, bound:], picks[0][:, bound:]).astype(BF16)
        cp_o[0] = ac_s[0, :, bound:]
        cp_o[1] = ac_s[1, :, :bound]
        pick_o[0] = picks[1][:, bound:]
        pick_o[1] = picks[2][:, :bound]
        agg_o[0] = mm(own_o[1], x_o[1]) + mm(near_o[1], x_o[0])
        agg_o[1] = mm(own_o[2], x_o[2]) + mm(far_o[1], x_o[0])
        agg = mm(own_o[0], x_o[0]) + mm(near_o[0], x_o[1]) + mm(far_o[0], x_o[2])
        mixed = mixed_of(agg, x_o[0])
        mix_o[...] = mixed
        slope_o[...], x1_o[...] = activate(mixed, w_o[0], 0)

    hbm = pl.BlockSpec(memory_space=pltpu.HBM)
    vm = pl.BlockSpec(memory_space=pltpu.VMEM)
    sds = jax.ShapeDtypeStruct
    return pl.pallas_call(
        body,
        out_shape=(
            sds((3, rows, width), BF16),
            sds((3, rows, rows), BF16),
            sds((2, rows, rows), BF16),
            sds((2, rows, rows), BF16),
            sds((2, rows, bound), BF16),
            sds((2, rows, bound), BF16),
            sds((2, rows, width), F32),
            sds((rows, width), BF16),
            sds((rows, width), F32),
            sds((rows, width), BF16),
            sds((layers, width, width), BF16),
        ),
        in_specs=[pl.BlockSpec(memory_space=pltpu.SMEM)] + [hbm] * 4 + [vm] * (2 * layers) + [hbm] + [vm] * (layers - 1),
        out_specs=(vm,) * 11,
        scratch_shapes=[
            pltpu.VMEM((2, rows, 2 * bound), BF16),
            pltpu.VMEM((rows, 2 * bound), BF16),
            pltpu.VMEM(send_rows.shape, jnp.int32),
            pltpu.SemaphoreType.DMA((5,)),
        ],
        compiler_params=pltpu.CompilerParams(vmem_limit_bytes=vmem_of(layers)),
        name="own_part",
    )(scalars, feats, adj, couple, send_rows, *near, *far, *w_pieces)


def rest_part_call(scalars, diag, part):
    x, _, _, _, cp, pick, agg, _, _, _, w = part
    layers = w.shape[0]
    _, rows, width = x.shape
    piece = rows // layers
    bound = cp.shape[2]

    def body(sc, *refs):
        got_r = refs[:layers]
        x_r, cp_r, pick_r, agg_r, w_r, x3_o, own3_o, near_o, far_o, mix_o, slope_o, x1_o, ac_s = refs[layers:]
        seg = sc[0]
        for k in range(layers):
            at = pl.ds(pl.multiple_of(place_of(seg, k, layers) * piece, piece), piece)
            x3_o[at, :] = got_r[k][:piece, :]
            own3_o[at, :] = got_r[k][piece : 2 * piece, :rows]
            ac_s[at, :] = got_r[k][piece : 2 * piece, rows:]
        picks = picks_of(got_r[0][2 * piece : 2 * piece + 1, : 2 * bound].astype(F32), rows)
        far_o[0] = mm_nt(cp_r[0], picks[:, bound:]).astype(BF16)
        near_o[0] = mm_nt(cp_r[1], picks[:, :bound]).astype(BF16)
        near_o[1] = mm_nt(ac_s[:, :bound], pick_r[1]).astype(BF16)
        far_o[1] = mm_nt(ac_s[:, bound:], pick_r[0]).astype(BF16)
        for g in range(3):
            if g == 0:
                sums = agg_r[0] + mm(far_o[0], x3_o[...])
            elif g == 1:
                sums = agg_r[1] + mm(near_o[0], x3_o[...])
            else:
                sums = mm(own3_o[...], x3_o[...]) + mm(near_o[1], x_r[2]) + mm(far_o[1], x_r[1])
            mixed = mixed_of(sums, x_r[g + 1] if g < 2 else x3_o[...])
            mix_o[g] = mixed
            slope_o[g], x1_o[g] = activate(mixed, w_r[0], 0)

    vm = pl.BlockSpec(memory_space=pltpu.VMEM)
    sds = jax.ShapeDtypeStruct
    return pl.pallas_call(
        body,
        out_shape=(
            sds((rows, width), BF16),
            sds((rows, rows), BF16),
            sds((2, rows, rows), BF16),
            sds((2, rows, rows), BF16),
            sds((3, rows, width), BF16),
            sds((3, rows, width), F32),
            sds((3, rows, width), BF16),
        ),
        in_specs=[pl.BlockSpec(memory_space=pltpu.SMEM)] + [vm] * (5 + layers),
        out_specs=(vm,) * 7,
        scratch_shapes=[pltpu.VMEM((rows, 2 * bound), BF16)],
        compiler_params=pltpu.CompilerParams(vmem_limit_bytes=vmem_of(layers)),
        name="rest_part",
    )(scalars, *diag, x, cp, pick, agg, w)


def blocks_at(own, near, far, own3, near3, far3):
    return (
        lambda g: own[g] if g < 3 else own3[...],
        lambda g: (near[0], near[1], near3[0], near3[1])[g],
        lambda g: (far[0], far3[0], far[1], far3[1])[g],
    )


def later_layers_call(scalars, part, rest):
    x, own, near, far, _, _, _, _, _, x1, w = part
    x3, own3, near3, far3, _, _, x1_rest = rest
    layers = w.shape[0]
    rows, width = x.shape[1:]

    def body(sc, x_r, own_r, near_r, far_r, x1_r, w_r, x3_r, own3_r, near3_r, far3_r, x1n_r, acts_o, mix_o, slope_o, xa_s, xb_s):
        seg = sc[0]
        own_at, near_at, far_at = blocks_at(own_r, near_r, far_r, own3_r, near3_r, far3_r)

        @pl.when(seg == 0)
        def _():
            acts_o[...] = x1_r[...]

        def src(g):
            return x1n_r[g - 1] if g else x1_r[...]

        for k in range(1, layers):
            dst = (xa_s, xb_s)[k % 2]
            for g in range(4):
                agg = mm(own_at(g), src(g)) + mm(near_at(g), src(g ^ 1)) + mm(far_at(g), src(g ^ 2))
                mixed = mixed_of(agg, x_r[g] if g < 3 else x3_r[...])
                mix_o[k - 1, g] = mixed
                slope_o[k - 1, g], out = activate(mixed, w_r[k], k)
                if k + 1 < layers:
                    dst[g] = out
                if g == 0:

                    @pl.when(seg == k)
                    def _():
                        acts_o[...] = out

            def src(g, dst=dst):
                return dst[g]

    vm = pl.BlockSpec(memory_space=pltpu.VMEM)
    return pl.pallas_call(
        body,
        out_shape=(
            jax.ShapeDtypeStruct((rows, width), BF16),
            jax.ShapeDtypeStruct((layers - 1, 4, rows, width), BF16),
            jax.ShapeDtypeStruct((layers - 1, 4, rows, width), F32),
        ),
        in_specs=[pl.BlockSpec(memory_space=pltpu.SMEM)] + [vm] * 11,
        out_specs=(vm,) * 3,
        scratch_shapes=[pltpu.VMEM((4, rows, width), BF16)] * 2,
        compiler_params=pltpu.CompilerParams(vmem_limit_bytes=vmem_of(layers)),
        name="later_layers",
    )(scalars, x, own, near, far, x1, w, x3, own3, near3, far3, x1_rest)


def backward_call(scalars, cot, got, part, rest, later_mix, later_slope):
    _, own, near, far, _, _, _, mix, slope, _, w = part
    _, own3, near3, far3, mix_rest, slope_rest, _ = rest
    layers = w.shape[0]
    rows, width = cot.shape
    piece = rows // layers
    n_dom = lax.axis_size("dom")
    others = n_dom // 4
    out_rows = width // n_dom
    half = width // 2

    def body(sc, cot_r, *refs):
        got_r = [refs[g * layers : (g + 1) * layers] for g in range(3)]
        own_r, near_r, far_r, mix_r, slope_r, w_r, own3_r, near3_r, far3_r, mixn_r, slopen_r, later_mix_r, later_slope_r = refs[
            3 * layers : 3 * layers + 13
        ]
        outs = refs[3 * layers + 13 :]
        dpre_o, carry_o, mine_o = outs[:3]
        send_o = outs[3 : 2 + others]
        up_s, dmix_s, part_s = outs[2 + others :]
        seg, low, high, place = sc[0], sc[1], sc[2], sc[3]
        own_at, near_at, far_at = blocks_at(own_r, near_r, far_r, own3_r, near3_r, far3_r)
        for g in range(3):
            for k in range(layers):
                at = pl.ds(pl.multiple_of(place_of(seg, k, layers) * piece, piece), piece)
                up_s[g + 1, at, :] = got_r[g][k][...]
        up_s[0] = cot_r[...]
        if layers == 1:
            carry_o[...] = jnp.zeros((rows, width), F32)
        for k in range(layers - 1, -1, -1):
            beta = beta_of(k)
            for g in range(4):
                slope_now = later_slope_r[k - 1, g] if k else (slopen_r[g - 1] if g else slope_r[...])
                dpre = (up_s[g].astype(F32) * slope_now).astype(BF16)
                dpre_o[pl.ds(g * rows, rows), :] = dpre
                if k:
                    dmix = ((1.0 - beta) * dpre.astype(F32) + beta * mm_nt(dpre, w_r[k])).astype(BF16)
                    dmix_s[g] = dmix
                    if g == 0:
                        carry_o[...] = SHARE * dmix.astype(F32) + (carry_o[...] if k + 1 < layers else 0.0)

            @pl.when(seg == k)
            def _():
                at = pl.ds(pl.multiple_of(high * half, half), half)
                part = jnp.zeros((half, width), F32)
                for g in range(4):
                    chosen = later_mix_r[k - 1, g, :, at] if k else (mixn_r[g - 1, :, at] if g else mix_r[:, at])
                    part = part + mm_tn(chosen, dpre_o[pl.ds(g * rows, rows), :])
                part_s[...] = beta * part

            if k:
                for g in range(4):
                    up_s[g] = (
                        (1.0 - SHARE)
                        * (
                            mm_tn(own_at(g), dmix_s[g])
                            + mm_tn(near_at(g ^ 1), dmix_s[g ^ 1])
                            + mm_tn(far_at(g ^ 2), dmix_s[g ^ 2])
                        )
                    ).astype(BF16)

        def block(m):
            at = (place ^ m) * (2 * out_rows) + low * out_rows
            return part_s[pl.ds(pl.multiple_of(at, out_rows), out_rows), :]

        mine_o[...] = block(0)
        for m in range(1, others):
            send_o[m - 1][...] = block(m).astype(BF16)

    vm = pl.BlockSpec(memory_space=pltpu.VMEM)
    sds = jax.ShapeDtypeStruct
    got_out = pl.pallas_call(
        body,
        out_shape=(sds((4 * rows, width), BF16), sds((rows, width), F32), sds((out_rows, width), F32))
        + tuple(sds((out_rows, width), BF16) for _ in range(1, others)),
        in_specs=[pl.BlockSpec(memory_space=pltpu.SMEM)] + [vm] * (1 + 3 * layers + 13),
        out_specs=(vm,) * (2 + others),
        scratch_shapes=[
            pltpu.VMEM((4, rows, width), BF16),
            pltpu.VMEM((4, rows, width), BF16),
            pltpu.VMEM((half, width), F32),
        ],
        compiler_params=pltpu.CompilerParams(vmem_limit_bytes=vmem_of(layers)),
        name="backward",
    )(
        scalars,
        cot,
        *[p for g in got for p in g],
        own,
        near,
        far,
        mix,
        slope,
        w,
        own3,
        near3,
        far3,
        mix_rest,
        slope_rest,
        later_mix,
        later_slope,
    )
    return got_out[0], got_out[1], got_out[2], got_out[3:]


def feat_call(scalars, dpre, carry, part):
    _, own, near, far, _, _, _, _, _, _, w = part
    layers = w.shape[0]
    rows, width = carry.shape
    cols = width // layers
    beta = beta_of(0)
    sliced = cols % 128 == 0
    kept = cols if sliced else width

    def body(sc, dpre_r, carry_r, own_r, near_r, far_r, w_r, feat_o):
        at = pl.ds(pl.multiple_of(sc[0] * cols, cols), cols) if sliced else slice(None)
        w_rows = w_r[0, at, :]
        dmix = []
        for g in range(3):
            d_at = pl.ds(g * rows, rows)
            through = mm_nt(dpre_r[d_at, :], w_rows)
            dmix.append(((1.0 - beta) * dpre_r[d_at, at].astype(F32) + beta * through).astype(BF16))
        sums = mm_tn(own_r[0], dmix[0]) + mm_tn(near_r[1], dmix[1]) + mm_tn(far_r[1], dmix[2])
        feat_o[...] = (1.0 - SHARE) * sums + (carry_r[:, at] + SHARE * dmix[0].astype(F32))

    vm = pl.BlockSpec(memory_space=pltpu.VMEM)
    feat = pl.pallas_call(
        body,
        out_shape=jax.ShapeDtypeStruct((rows, kept), F32),
        in_specs=[pl.BlockSpec(memory_space=pltpu.SMEM)] + [vm] * 6,
        out_specs=vm,
        compiler_params=pltpu.CompilerParams(vmem_limit_bytes=vmem_of(layers)),
        name="feat",
    )(scalars, dpre, carry, own, near, far, w)
    return feat if sliced else lax.dynamic_slice_in_dim(feat, scalars[0] * cols, cols, 1)


def step(feats, adj, couple, send_rows, weights, cot):
    seg = lax.axis_index("segment")
    dom = lax.axis_index("dom")
    layers = lax.axis_size("segment")
    n_dom = lax.axis_size("dom")
    top = n_dom // 2
    others = n_dom // 4
    place = (dom // 2) % others
    scalars = jnp.stack([seg, dom & 1, dom // top, place]).astype(jnp.int32)

    fwd_mine, cot_mine = pack_call(scalars, feats, adj, couple, send_rows, cot, layers)
    far_fwd = swapped(fwd_mine, top)
    near_fwd = swapped(fwd_mine, 1)
    near_cot = swapped(cot_mine, 1)
    w_pieces = every_piece(weights)
    near_fwd = every_piece(near_fwd)
    diag_fwd = swapped(far_fwd, 1)
    far_fwd = every_piece(far_fwd)
    far_cot = swapped(cot_mine, top)
    near_cot = every_piece(near_cot)
    part = own_part_call(scalars, feats, adj, couple, send_rows, near_fwd, far_fwd, w_pieces)
    diag_fwd = every_piece(diag_fwd)
    diag_cot = swapped(far_cot, 1)
    far_cot = every_piece(far_cot)
    rest = rest_part_call(scalars, diag_fwd, part)
    diag_cot = every_piece(diag_cot)
    acts, later_mix, later_slope = later_layers_call(scalars, part, rest)
    dpre, carry, wgrad, sends = backward_call(
        scalars, cot, [near_cot, far_cot, diag_cot], part, rest, later_mix, later_slope
    )
    for m in range(others - 1, 0, -1):
        wgrad = wgrad + swapped(sends[m - 1], 2 * m).astype(F32)
    feat = feat_call(scalars, dpre, carry, part)
    return (acts[None], wgrad[None], feat)


def solution(mesh):
    in_specs = (
        P("dom", None),
        P("dom", None),
        P("dom", None),
        P("dom", None),
        P("segment", None),
        P("dom", None),
    )
    out_specs = (P("segment", "dom", None), P("segment", "dom", None), P("dom", "segment"))
    return jax.shard_map(step, mesh=mesh, in_specs=in_specs, out_specs=out_specs, check_vma=False)
```

```python
import math

import jax
import jax.numpy as jnp
from jax import lax
from jax.experimental import pallas as pl
from jax.experimental.pallas import tpu as pltpu
from jax.sharding import PartitionSpec as P


SHARE = 0.1
BETA_SCALE = 0.5
BF16 = jnp.bfloat16
F32 = jnp.float32


def vmem_of(layers):
    return min(60, 14 + 6 * layers) << 20


def swapped(x, mask):
    return lax.ppermute(x, "dom", [(i, i ^ mask) for i in range(lax.axis_size("dom"))])


def every_piece(x):
    n = lax.axis_size("segment")
    return [x] + [lax.ppermute(x, "segment", [(i, (i + k) % n) for i in range(n)]) for k in range(1, n)]


def beta_of(k):
    return math.log(BETA_SCALE / (k + 1.0) + 1.0)


def mm(a, b):
    return jnp.dot(a, b, preferred_element_type=F32)


def mm_nt(a, b):
    return lax.dot_general(a, b, (((1,), (1,)), ((), ())), preferred_element_type=F32)


def mm_tn(a, b):
    return lax.dot_general(a, b, (((0,), (0,)), ((), ())), preferred_element_type=F32)


def place_of(seg, k, n):
    return lax.rem(seg - k + n, n)


def in_hbm(x):
    return pltpu.with_memory_space_constraint(x, pltpu.HBM)


def pack_call(scalars, feats, adj, couple, send_rows, cot, layers):
    rows, width = feats.shape
    piece = rows // layers
    picked = send_rows.shape[1]

    def body(sc, feats_r, adj_r, couple_r, sr_r, cot_r, fwd_o, cot_o, sr_s, sems):
        at = pl.ds(pl.multiple_of(sc[0] * piece, piece), piece)
        split = adj_r.shape[1]
        copies = [
            pltpu.make_async_copy(feats_r.at[at, :], fwd_o.at[:piece, :], sems.at[0]),
            pltpu.make_async_copy(adj_r.at[at, :], fwd_o.at[piece : 2 * piece, :split], sems.at[1]),
            pltpu.make_async_copy(couple_r.at[at, :], fwd_o.at[piece : 2 * piece, split:], sems.at[2]),
            pltpu.make_async_copy(cot_r.at[at, :], cot_o, sems.at[3]),
        ]
        sr_copy = pltpu.make_async_copy(sr_r, sr_s, sems.at[4])
        sr_copy.start()
        for c in copies:
            c.start()
        fwd_o[2 * piece :, picked:] = jnp.zeros((16, width - picked), BF16)
        sr_copy.wait()
        fwd_o[2 * piece :, :picked] = jnp.broadcast_to(sr_s[...].astype(F32), (16, picked)).astype(BF16)
        for c in copies:
            c.wait()

    vm = pl.BlockSpec(memory_space=pltpu.VMEM)
    hbm = pl.BlockSpec(memory_space=pltpu.HBM)
    return pl.pallas_call(
        body,
        out_shape=(
            jax.ShapeDtypeStruct((2 * piece + 16, width), BF16),
            jax.ShapeDtypeStruct((piece, width), BF16),
        ),
        in_specs=[pl.BlockSpec(memory_space=pltpu.SMEM), hbm, hbm, hbm, hbm, hbm],
        out_specs=(vm, vm),
        scratch_shapes=[pltpu.VMEM(send_rows.shape, jnp.int32), pltpu.SemaphoreType.DMA((5,))],
        compiler_params=pltpu.CompilerParams(vmem_limit_bytes=4 << 20),
        name="pack",
    )(scalars, *[in_hbm(a) for a in (feats, adj, couple, send_rows, cot)])


def picks_of(sr, rows):
    ids = lax.broadcasted_iota(jnp.int32, (rows, sr.shape[1]), 0).astype(F32)
    return (ids == sr).astype(F32).astype(BF16)


def mixed_of(agg, first):
    return ((1.0 - SHARE) * agg + SHARE * first.astype(F32)).astype(BF16)


def activate(mixed, w, k):
    beta = beta_of(k)
    pre = (1.0 - beta) * mixed.astype(F32) + beta * mm(mixed, w)
    sig = 1.0 / (1.0 + jnp.exp(-pre))
    out = pre * sig
    return sig + out * (1.0 - sig), out.astype(BF16)


def own_part_call(scalars, feats, adj, couple, send_rows, near, far, w_pieces):
    layers = len(w_pieces)
    rows, width = feats.shape
    piece = rows // layers
    bound = couple.shape[1] // 2

    def body(sc, feats_r, adj_r, couple_r, sr_r, *refs):
        got_r = [refs[g * layers : (g + 1) * layers] for g in range(2)]
        w_r = refs[2 * layers : 3 * layers]
        outs = refs[3 * layers :]
        x_o, own_o, near_o, far_o, cp_o, pick_o, agg_o, mix_o, slope_o, x1_o, w_o = outs[:11]
        ac_s, couple_s, sr_s, sems = outs[11:]
        seg = sc[0]
        copies = [
            pltpu.make_async_copy(sr_r, sr_s, sems.at[0]),
            pltpu.make_async_copy(couple_r, couple_s, sems.at[1]),
            pltpu.make_async_copy(feats_r, x_o.at[0], sems.at[2]),
            pltpu.make_async_copy(adj_r, own_o.at[0], sems.at[3]),
            pltpu.make_async_copy(w_r[0], w_o.at[seg], sems.at[4]),
        ]
        for c in copies:
            c.start()
        for g in range(2):
            for k in range(layers):
                at = pl.ds(pl.multiple_of(place_of(seg, k, layers) * piece, piece), piece)
                x_o[g + 1, at, :] = got_r[g][k][:piece, :]
                own_o[g + 1, at, :] = got_r[g][k][piece : 2 * piece, :rows]
                ac_s[g, at, :] = got_r[g][k][piece : 2 * piece, rows:]
        for k in range(1, layers):
            w_o[place_of(seg, k, layers)] = w_r[k][...]
        for c in copies:
            c.wait()
        picks = [picks_of(sr_s[...].astype(F32), rows)]
        for g in range(2):
            picks.append(picks_of(got_r[g][0][2 * piece : 2 * piece + 1, : 2 * bound].astype(F32), rows))
        near_o[0] = mm_nt(couple_s[:, :bound], picks[1][:, :bound]).astype(BF16)
        far_o[0] = mm_nt(couple_s[:, bound:], picks[2][:, bound:]).astype(BF16)
        near_o[1] = mm_nt(ac_s[0, :, :bound], picks[0][:, :bound]).astype(BF16)
        far_o[1] = mm_nt(ac_s[1, :, bound:], picks[0][:, bound:]).astype(BF16)
        cp_o[0] = ac_s[0, :, bound:]
        cp_o[1] = ac_s[1, :, :bound]
        pick_o[0] = picks[1][:, bound:]
        pick_o[1] = picks[2][:, :bound]
        agg_o[0] = mm(own_o[1], x_o[1]) + mm(near_o[1], x_o[0])
        agg_o[1] = mm(own_o[2], x_o[2]) + mm(far_o[1], x_o[0])
        agg = mm(own_o[0], x_o[0]) + mm(near_o[0], x_o[1]) + mm(far_o[0], x_o[2])
        mixed = mixed_of(agg, x_o[0])
        mix_o[...] = mixed
        slope_o[...], x1_o[...] = activate(mixed, w_o[0], 0)

    hbm = pl.BlockSpec(memory_space=pltpu.HBM)
    vm = pl.BlockSpec(memory_space=pltpu.VMEM)
    sds = jax.ShapeDtypeStruct
    return pl.pallas_call(
        body,
        out_shape=(
            sds((3, rows, width), BF16),
            sds((3, rows, rows), BF16),
            sds((2, rows, rows), BF16),
            sds((2, rows, rows), BF16),
            sds((2, rows, bound), BF16),
            sds((2, rows, bound), BF16),
            sds((2, rows, width), F32),
            sds((rows, width), BF16),
            sds((rows, width), F32),
            sds((rows, width), BF16),
            sds((layers, width, width), BF16),
        ),
        in_specs=[pl.BlockSpec(memory_space=pltpu.SMEM)] + [hbm] * 4 + [vm] * (2 * layers) + [hbm] + [vm] * (layers - 1),
        out_specs=(vm,) * 11,
        scratch_shapes=[
            pltpu.VMEM((2, rows, 2 * bound), BF16),
            pltpu.VMEM((rows, 2 * bound), BF16),
            pltpu.VMEM(send_rows.shape, jnp.int32),
            pltpu.SemaphoreType.DMA((5,)),
        ],
        compiler_params=pltpu.CompilerParams(vmem_limit_bytes=vmem_of(layers)),
        name="own_part",
    )(
        scalars,
        *[in_hbm(a) for a in (feats, adj, couple, send_rows)],
        *near,
        *far,
        in_hbm(w_pieces[0]),
        *w_pieces[1:],
    )


def rest_part_call(scalars, diag, part):
    x, _, _, _, cp, pick, agg, _, _, _, w = part
    layers = w.shape[0]
    _, rows, width = x.shape
    piece = rows // layers
    bound = cp.shape[2]

    def body(sc, *refs):
        got_r = refs[:layers]
        x_r, cp_r, pick_r, agg_r, w_r, x3_o, own3_o, near_o, far_o, mix_o, slope_o, x1_o, ac_s = refs[layers:]
        seg = sc[0]
        for k in range(layers):
            at = pl.ds(pl.multiple_of(place_of(seg, k, layers) * piece, piece), piece)
            x3_o[at, :] = got_r[k][:piece, :]
            own3_o[at, :] = got_r[k][piece : 2 * piece, :rows]
            ac_s[at, :] = got_r[k][piece : 2 * piece, rows:]
        picks = picks_of(got_r[0][2 * piece : 2 * piece + 1, : 2 * bound].astype(F32), rows)
        far_o[0] = mm_nt(cp_r[0], picks[:, bound:]).astype(BF16)
        near_o[0] = mm_nt(cp_r[1], picks[:, :bound]).astype(BF16)
        near_o[1] = mm_nt(ac_s[:, :bound], pick_r[1]).astype(BF16)
        far_o[1] = mm_nt(ac_s[:, bound:], pick_r[0]).astype(BF16)
        for g in range(3):
            if g == 0:
                sums = agg_r[0] + mm(far_o[0], x3_o[...])
            elif g == 1:
                sums = agg_r[1] + mm(near_o[0], x3_o[...])
            else:
                sums = mm(own3_o[...], x3_o[...]) + mm(near_o[1], x_r[2]) + mm(far_o[1], x_r[1])
            mixed = mixed_of(sums, x_r[g + 1] if g < 2 else x3_o[...])
            mix_o[g] = mixed
            slope_o[g], x1_o[g] = activate(mixed, w_r[0], 0)

    vm = pl.BlockSpec(memory_space=pltpu.VMEM)
    sds = jax.ShapeDtypeStruct
    return pl.pallas_call(
        body,
        out_shape=(
            sds((rows, width), BF16),
            sds((rows, rows), BF16),
            sds((2, rows, rows), BF16),
            sds((2, rows, rows), BF16),
            sds((3, rows, width), BF16),
            sds((3, rows, width), F32),
            sds((3, rows, width), BF16),
        ),
        in_specs=[pl.BlockSpec(memory_space=pltpu.SMEM)] + [vm] * (5 + layers),
        out_specs=(vm,) * 7,
        scratch_shapes=[pltpu.VMEM((rows, 2 * bound), BF16)],
        compiler_params=pltpu.CompilerParams(vmem_limit_bytes=vmem_of(layers)),
        name="rest_part",
    )(scalars, *diag, x, cp, pick, agg, w)


def blocks_at(own, near, far, own3, near3, far3):
    return (
        lambda g: own[g] if g < 3 else own3[...],
        lambda g: (near[0], near[1], near3[0], near3[1])[g],
        lambda g: (far[0], far3[0], far[1], far3[1])[g],
    )


def later_layers_call(scalars, part, rest):
    x, own, near, far, _, _, _, _, _, x1, w = part
    x3, own3, near3, far3, _, _, x1_rest = rest
    layers = w.shape[0]
    rows, width = x.shape[1:]

    def body(sc, x_r, own_r, near_r, far_r, x1_r, w_r, x3_r, own3_r, near3_r, far3_r, x1n_r, acts_o, mix_o, slope_o, xa_s, xb_s):
        seg = sc[0]
        own_at, near_at, far_at = blocks_at(own_r, near_r, far_r, own3_r, near3_r, far3_r)

        @pl.when(seg == 0)
        def _():
            acts_o[...] = x1_r[...]

        def src(g):
            return x1n_r[g - 1] if g else x1_r[...]

        for k in range(1, layers):
            dst = (xa_s, xb_s)[k % 2]
            for g in range(4):
                agg = mm(own_at(g), src(g)) + mm(near_at(g), src(g ^ 1)) + mm(far_at(g), src(g ^ 2))
                mixed = mixed_of(agg, x_r[g] if g < 3 else x3_r[...])
                mix_o[k - 1, g] = mixed
                slope_o[k - 1, g], out = activate(mixed, w_r[k], k)
                if k + 1 < layers:
                    dst[g] = out
                if g == 0:

                    @pl.when(seg == k)
                    def _():
                        acts_o[...] = out

            def src(g, dst=dst):
                return dst[g]

    vm = pl.BlockSpec(memory_space=pltpu.VMEM)
    return pl.pallas_call(
        body,
        out_shape=(
            jax.ShapeDtypeStruct((rows, width), BF16),
            jax.ShapeDtypeStruct((layers - 1, 4, rows, width), BF16),
            jax.ShapeDtypeStruct((layers - 1, 4, rows, width), F32),
        ),
        in_specs=[pl.BlockSpec(memory_space=pltpu.SMEM)] + [vm] * 11,
        out_specs=(vm,) * 3,
        scratch_shapes=[pltpu.VMEM((4, rows, width), BF16)] * 2,
        compiler_params=pltpu.CompilerParams(vmem_limit_bytes=vmem_of(layers)),
        name="later_layers",
    )(scalars, x, own, near, far, x1, w, x3, own3, near3, far3, x1_rest)


def backward_call(scalars, cot, got, part, rest, later_mix, later_slope):
    _, own, near, far, _, _, _, mix, slope, _, w = part
    _, own3, near3, far3, mix_rest, slope_rest, _ = rest
    layers = w.shape[0]
    rows, width = cot.shape
    piece = rows // layers
    n_dom = lax.axis_size("dom")
    others = n_dom // 4
    out_rows = width // n_dom
    half = width // 2

    def body(sc, cot_r, *refs):
        got_r = [refs[g * layers : (g + 1) * layers] for g in range(3)]
        own_r, near_r, far_r, mix_r, slope_r, w_r, own3_r, near3_r, far3_r, mixn_r, slopen_r, later_mix_r, later_slope_r = refs[
            3 * layers : 3 * layers + 13
        ]
        outs = refs[3 * layers + 13 :]
        dpre_o, carry_o, mine_o = outs[:3]
        send_o = outs[3 : 2 + others]
        up_s, dmix_s, part_s = outs[2 + others :]
        seg, low, high, place = sc[0], sc[1], sc[2], sc[3]
        own_at, near_at, far_at = blocks_at(own_r, near_r, far_r, own3_r, near3_r, far3_r)
        for g in range(3):
            for k in range(layers):
                at = pl.ds(pl.multiple_of(place_of(seg, k, layers) * piece, piece), piece)
                up_s[g + 1, at, :] = got_r[g][k][...]
        up_s[0] = cot_r[...]
        if layers == 1:
            carry_o[...] = jnp.zeros((rows, width), F32)
        for k in range(layers - 1, -1, -1):
            beta = beta_of(k)
            for g in range(4):
                slope_now = later_slope_r[k - 1, g] if k else (slopen_r[g - 1] if g else slope_r[...])
                dpre = (up_s[g].astype(F32) * slope_now).astype(BF16)
                dpre_o[pl.ds(g * rows, rows), :] = dpre
                if k:
                    dmix = ((1.0 - beta) * dpre.astype(F32) + beta * mm_nt(dpre, w_r[k])).astype(BF16)
                    dmix_s[g] = dmix
                    if g == 0:
                        carry_o[...] = SHARE * dmix.astype(F32) + (carry_o[...] if k + 1 < layers else 0.0)

            @pl.when(seg == k)
            def _():
                at = pl.ds(pl.multiple_of(high * half, half), half)
                part = jnp.zeros((half, width), F32)
                for g in range(4):
                    chosen = later_mix_r[k - 1, g, :, at] if k else (mixn_r[g - 1, :, at] if g else mix_r[:, at])
                    part = part + mm_tn(chosen, dpre_o[pl.ds(g * rows, rows), :])
                part_s[...] = beta * part

            if k:
                for g in range(4):
                    up_s[g] = (
                        (1.0 - SHARE)
                        * (
                            mm_tn(own_at(g), dmix_s[g])
                            + mm_tn(near_at(g ^ 1), dmix_s[g ^ 1])
                            + mm_tn(far_at(g ^ 2), dmix_s[g ^ 2])
                        )
                    ).astype(BF16)

        def block(m):
            at = (place ^ m) * (2 * out_rows) + low * out_rows
            return part_s[pl.ds(pl.multiple_of(at, out_rows), out_rows), :]

        mine_o[...] = block(0)
        for m in range(1, others):
            send_o[m - 1][...] = block(m).astype(BF16)

    vm = pl.BlockSpec(memory_space=pltpu.VMEM)
    sds = jax.ShapeDtypeStruct
    got_out = pl.pallas_call(
        body,
        out_shape=(sds((4 * rows, width), BF16), sds((rows, width), F32), sds((out_rows, width), F32))
        + tuple(sds((out_rows, width), BF16) for _ in range(1, others)),
        in_specs=[pl.BlockSpec(memory_space=pltpu.SMEM)] + [vm] * (1 + 3 * layers + 13),
        out_specs=(vm,) * (2 + others),
        scratch_shapes=[
            pltpu.VMEM((4, rows, width), BF16),
            pltpu.VMEM((4, rows, width), BF16),
            pltpu.VMEM((half, width), F32),
        ],
        compiler_params=pltpu.CompilerParams(vmem_limit_bytes=vmem_of(layers)),
        name="backward",
    )(
        scalars,
        cot,
        *[p for g in got for p in g],
        own,
        near,
        far,
        mix,
        slope,
        w,
        own3,
        near3,
        far3,
        mix_rest,
        slope_rest,
        later_mix,
        later_slope,
    )
    return got_out[0], got_out[1], got_out[2], got_out[3:]


def feat_call(scalars, dpre, carry, part):
    _, own, near, far, _, _, _, _, _, _, w = part
    layers = w.shape[0]
    rows, width = carry.shape
    cols = width // layers
    beta = beta_of(0)
    sliced = cols % 128 == 0
    kept = cols if sliced else width

    def body(sc, dpre_r, carry_r, own_r, near_r, far_r, w_r, feat_o):
        at = pl.ds(pl.multiple_of(sc[0] * cols, cols), cols) if sliced else slice(None)
        w_rows = w_r[0, at, :]
        dmix = []
        for g in range(3):
            d_at = pl.ds(g * rows, rows)
            through = mm_nt(dpre_r[d_at, :], w_rows)
            dmix.append(((1.0 - beta) * dpre_r[d_at, at].astype(F32) + beta * through).astype(BF16))
        sums = mm_tn(own_r[0], dmix[0]) + mm_tn(near_r[1], dmix[1]) + mm_tn(far_r[1], dmix[2])
        feat_o[...] = (1.0 - SHARE) * sums + (carry_r[:, at] + SHARE * dmix[0].astype(F32))

    vm = pl.BlockSpec(memory_space=pltpu.VMEM)
    feat = pl.pallas_call(
        body,
        out_shape=jax.ShapeDtypeStruct((rows, kept), F32),
        in_specs=[pl.BlockSpec(memory_space=pltpu.SMEM)] + [vm] * 6,
        out_specs=vm,
        compiler_params=pltpu.CompilerParams(vmem_limit_bytes=vmem_of(layers)),
        name="feat",
    )(scalars, dpre, carry, own, near, far, w)
    return feat if sliced else lax.dynamic_slice_in_dim(feat, scalars[0] * cols, cols, 1)


def step(feats, adj, couple, send_rows, weights, cot):
    seg = lax.axis_index("segment")
    dom = lax.axis_index("dom")
    layers = lax.axis_size("segment")
    n_dom = lax.axis_size("dom")
    top = n_dom // 2
    others = n_dom // 4
    place = (dom // 2) % others
    scalars = jnp.stack([seg, dom & 1, dom // top, place]).astype(jnp.int32)

    fwd_mine, cot_mine = pack_call(scalars, feats, adj, couple, send_rows, cot, layers)
    far_fwd = swapped(fwd_mine, top)
    near_fwd = swapped(fwd_mine, 1)
    near_cot = swapped(cot_mine, 1)
    w_pieces = every_piece(weights)
    near_fwd = every_piece(near_fwd)
    diag_fwd = swapped(far_fwd, 1)
    far_fwd = every_piece(far_fwd)
    far_cot = swapped(cot_mine, top)
    near_cot = every_piece(near_cot)
    part = own_part_call(scalars, feats, adj, couple, send_rows, near_fwd, far_fwd, w_pieces)
    diag_fwd = every_piece(diag_fwd)
    diag_cot = swapped(far_cot, 1)
    far_cot = every_piece(far_cot)
    rest = rest_part_call(scalars, diag_fwd, part)
    diag_cot = every_piece(diag_cot)
    acts, later_mix, later_slope = later_layers_call(scalars, part, rest)
    dpre, carry, wgrad, sends = backward_call(
        scalars, cot, [near_cot, far_cot, diag_cot], part, rest, later_mix, later_slope
    )
    for m in range(others - 1, 0, -1):
        wgrad = wgrad + swapped(sends[m - 1], 2 * m).astype(F32)
    feat = feat_call(scalars, dpre, carry, part)
    return (acts[None], wgrad[None], feat)


def solution(mesh):
    in_specs = (
        P("dom", None),
        P("dom", None),
        P("dom", None),
        P("dom", None),
        P("segment", None),
        P("dom", None),
    )
    out_specs = (P("segment", "dom", None), P("segment", "dom", None), P("dom", "segment"))
    return jax.shard_map(step, mesh=mesh, in_specs=in_specs, out_specs=out_specs, check_vma=False)
```

```python
import math

import jax
import jax.numpy as jnp
from jax import lax
from jax.experimental import pallas as pl
from jax.experimental.pallas import tpu as pltpu
from jax.sharding import PartitionSpec as P


SHARE = 0.1
BETA_SCALE = 0.5
BF16 = jnp.bfloat16
F32 = jnp.float32


def swapped(x, mask):
    return lax.ppermute(x, "dom", [(i, i ^ mask) for i in range(lax.axis_size("dom"))])


def every_piece(x):
    n = lax.axis_size("segment")
    return [x] + [lax.ppermute(x, "segment", [(i, (i + k) % n) for i in range(n)]) for k in range(1, n)]


def beta_of(k):
    return math.log(BETA_SCALE / (k + 1.0) + 1.0)


def mm(a, b):
    return jnp.dot(a, b, preferred_element_type=F32)


def mm_nt(a, b):
    return lax.dot_general(a, b, (((1,), (1,)), ((), ())), preferred_element_type=F32)


def mm_tn(a, b):
    return lax.dot_general(a, b, (((0,), (0,)), ((), ())), preferred_element_type=F32)


def place_of(seg, k, n):
    return lax.rem(seg - k + n, n)


def in_hbm(x):
    return pltpu.with_memory_space_constraint(x, pltpu.HBM)


def call(body, out_shape, ins, scratch=(), vmem=20):
    spaces = {"s": pltpu.SMEM, "h": pltpu.HBM, "v": pltpu.VMEM}
    specs = [pl.BlockSpec(memory_space=spaces[m]) for _, m in ins]
    arrays = [in_hbm(a) if m == "h" else a for a, m in ins]
    return pl.pallas_call(
        body,
        out_shape=tuple(out_shape),
        in_specs=specs,
        out_specs=tuple(pl.BlockSpec(memory_space=pltpu.VMEM) for _ in out_shape),
        scratch_shapes=list(scratch),
        compiler_params=pltpu.CompilerParams(vmem_limit_bytes=vmem << 20),
    )(*arrays)


sds = jax.ShapeDtypeStruct


def pack_call(scalars, feats, adj, couple, send_rows, cot, layers):
    rows, width = feats.shape
    piece = rows // layers
    picked = send_rows.shape[1]

    def body(sc, feats_r, adj_r, couple_r, sr_r, cot_r, ac_o, feats_o, cot_o, sr_s, sems):
        at = pl.ds(pl.multiple_of(sc[0] * piece, piece), piece)
        split = adj_r.shape[1]
        copies = [
            pltpu.make_async_copy(adj_r.at[at, :], ac_o.at[:piece, :split], sems.at[1]),
            pltpu.make_async_copy(couple_r.at[at, :], ac_o.at[:piece, split:], sems.at[2]),
            pltpu.make_async_copy(feats_r.at[at, :], feats_o, sems.at[0]),
            pltpu.make_async_copy(cot_r.at[at, :], cot_o, sems.at[3]),
        ]
        sr_copy = pltpu.make_async_copy(sr_r, sr_s, sems.at[4])
        sr_copy.start()
        for c in copies:
            c.start()
        ac_o[piece:, picked:] = jnp.zeros((8, width - picked), BF16)
        sr_copy.wait()
        ac_o[piece:, :picked] = jnp.broadcast_to(sr_s[...].astype(F32), (8, picked)).astype(BF16)
        for c in copies:
            c.wait()

    return call(
        body,
        (sds((piece + 8, width), BF16), sds((piece, width), BF16), sds((piece, width), BF16)),
        [(scalars, "s"), (feats, "h"), (adj, "h"), (couple, "h"), (send_rows, "h"), (cot, "h")],
        [pltpu.VMEM(send_rows.shape, jnp.int32), pltpu.SemaphoreType.DMA((5,))],
        4,
    )


def picks_of(sr, rows):
    ids = lax.broadcasted_iota(jnp.int32, (rows, sr.shape[1]), 0).astype(F32)
    return (ids == sr).astype(F32).astype(BF16)


def mixed_of(agg, first):
    return ((1.0 - SHARE) * agg + SHARE * first.astype(F32)).astype(BF16)


def activate(mixed, w, k):
    beta = beta_of(k)
    pre = (1.0 - beta) * mixed.astype(F32) + beta * mm(mixed, w)
    sig = 1.0 / (1.0 + jnp.exp(-pre))
    out = pre * sig
    return sig + out * (1.0 - sig), out.astype(BF16)


def piece_slice(seg, k, layers, piece):
    return pl.ds(pl.multiple_of(place_of(seg, k, layers) * piece, piece), piece)


def prep_call(scalars, feats, adj, couple, send_rows, w_pieces):
    layers = len(w_pieces)
    rows, width = feats.shape

    def body(sc, feats_r, adj_r, couple_r, sr_r, *refs):
        w_r = refs[:layers]
        x_o, own_o, couple_o, pick_o, agg_o, w_o, sr_s, sems = refs[layers:]
        seg = sc[0]
        copies = [
            pltpu.make_async_copy(sr_r, sr_s, sems.at[0]),
            pltpu.make_async_copy(couple_r, couple_o, sems.at[1]),
            pltpu.make_async_copy(feats_r, x_o, sems.at[2]),
            pltpu.make_async_copy(adj_r, own_o, sems.at[3]),
            pltpu.make_async_copy(w_r[0], w_o.at[seg], sems.at[4]),
        ]
        for c in copies:
            c.start()
        for k in range(1, layers):
            w_o[place_of(seg, k, layers)] = w_r[k][...]
        for c in copies:
            c.wait()
        pick_o[...] = picks_of(sr_s[...].astype(F32), rows)
        agg_o[...] = mm(own_o[...], x_o[...])

    return call(
        body,
        (
            sds((rows, width), BF16),
            sds((rows, rows), BF16),
            sds(couple.shape[:0] + (rows, couple.shape[1]), BF16),
            sds((rows, send_rows.shape[1]), BF16),
            sds((rows, width), F32),
            sds((layers, width, width), BF16),
        ),
        [(scalars, "s"), (feats, "h"), (adj, "h"), (couple, "h"), (send_rows, "h"), (w_pieces[0], "h")]
        + [(w, "v") for w in w_pieces[1:]],
        [pltpu.VMEM(send_rows.shape, jnp.int32), pltpu.SemaphoreType.DMA((5,))],
        8 + 2 * layers,
    )


def blocks_call(scalars, near, far, couple, pick):
    layers = len(near)
    rows = couple.shape[0]
    piece = rows // layers
    bound = couple.shape[1] // 2

    def body(sc, couple_r, pick_r, *refs):
        got_r = [refs[g * layers : (g + 1) * layers] for g in range(2)]
        own_o, near_o, far_o, cp_o, pick_o, ac_s = refs[2 * layers :]
        seg = sc[0]
        picks = [pick_r[...]]
        for g in range(2):
            for k in range(layers):
                at = piece_slice(seg, k, layers, piece)
                own_o[g, at, :] = got_r[g][k][:piece, :rows]
                ac_s[g, at, :] = got_r[g][k][:piece, rows:]
            picks.append(picks_of(got_r[g][0][piece : piece + 1, : 2 * bound].astype(F32), rows))
        near_o[0] = mm_nt(couple_r[:, :bound], picks[1][:, :bound]).astype(BF16)
        far_o[0] = mm_nt(couple_r[:, bound:], picks[2][:, bound:]).astype(BF16)
        near_o[1] = mm_nt(ac_s[0, :, :bound], picks[0][:, :bound]).astype(BF16)
        far_o[1] = mm_nt(ac_s[1, :, bound:], picks[0][:, bound:]).astype(BF16)
        cp_o[0] = ac_s[0, :, bound:]
        cp_o[1] = ac_s[1, :, :bound]
        pick_o[0] = picks[1][:, bound:]
        pick_o[1] = picks[2][:, :bound]

    return call(
        body,
        (sds((2, rows, rows), BF16),) * 3 + (sds((2, rows, bound), BF16),) * 2,
        [(scalars, "s"), (couple, "v"), (pick, "v")] + [(a, "v") for a in (*near, *far)],
        [pltpu.VMEM((2, rows, 2 * bound), BF16)],
        8,
    )


def own_call(scalars, near, far, diag, prep, blocks):
    x, _, _, _, agg, w = prep
    own12, near01, far02, cp, pick = blocks
    layers = len(near)
    rows, width = x.shape
    piece = rows // layers
    bound = cp.shape[2]

    def body(sc, x_r, agg_r, w_r, own12_r, near01_r, far02_r, cp_r, pick_r, *refs):
        got_r = [refs[g * layers : (g + 1) * layers] for g in range(3)]
        x12_o, mix_o, slope_o, x1_o, sums_o, own3_o, near23_o, far13_o, ac_s = refs[3 * layers :]
        seg = sc[0]
        for k in range(layers):
            at = piece_slice(seg, k, layers, piece)
            x12_o[0, at, :] = got_r[0][k][...]
            x12_o[1, at, :] = got_r[1][k][...]
            own3_o[at, :] = got_r[2][k][:piece, :rows]
            ac_s[at, :] = got_r[2][k][:piece, rows:]
        mixed = mixed_of(agg_r[...] + mm(near01_r[0], x12_o[0]) + mm(far02_r[0], x12_o[1]), x_r[...])
        mix_o[...] = mixed
        slope_o[...], x1_o[...] = activate(mixed, w_r[0], 0)
        picks = picks_of(got_r[2][0][piece : piece + 1, : 2 * bound].astype(F32), rows)
        far13_o[0] = mm_nt(cp_r[0], picks[:, bound:]).astype(BF16)
        near23_o[0] = mm_nt(cp_r[1], picks[:, :bound]).astype(BF16)
        near23_o[1] = mm_nt(ac_s[:, :bound], pick_r[1]).astype(BF16)
        far13_o[1] = mm_nt(ac_s[:, bound:], pick_r[0]).astype(BF16)
        sums_o[0] = mm(own12_r[0], x12_o[0]) + mm(near01_r[1], x_r[...])
        sums_o[1] = mm(own12_r[1], x12_o[1]) + mm(far02_r[1], x_r[...])
        sums_o[2] = mm(near23_o[1], x12_o[1]) + mm(far13_o[1], x12_o[0])

    return call(
        body,
        (
            sds((2, rows, width), BF16),
            sds((rows, width), BF16),
            sds((rows, width), F32),
            sds((rows, width), BF16),
            sds((3, rows, width), F32),
            sds((rows, rows), BF16),
            sds((2, rows, rows), BF16),
            sds((2, rows, rows), BF16),
        ),
        [(scalars, "s")]
        + [(a, "v") for a in (x, agg, w, own12, near01, far02, cp, pick, *near, *far, *diag)],
        [pltpu.VMEM((rows, 2 * bound), BF16)],
        16,
    )


def rest_call(scalars, diag, prep, own):
    x12, _, _, _, sums, own3, near23, far13 = own
    w = prep[-1]
    layers = len(diag)
    _, rows, width = x12.shape
    piece = rows // layers

    def body(sc, x12_r, sums_r, own3_r, near23_r, far13_r, w_r, *refs):
        got_r = refs[:layers]
        x3_o, mix_o, slope_o, x1_o = refs[layers:]
        seg = sc[0]
        for k in range(layers):
            x3_o[piece_slice(seg, k, layers, piece), :] = got_r[k][...]
        for g in range(3):
            blk = (far13_r[0], near23_r[0], own3_r[...])[g]
            agg = sums_r[g] + mm(blk, x3_o[...])
            mixed = mixed_of(agg, x12_r[g] if g < 2 else x3_o[...])
            mix_o[g] = mixed
            slope_o[g], x1_o[g] = activate(mixed, w_r[0], 0)

    return call(
        body,
        (
            sds((rows, width), BF16),
            sds((3, rows, width), BF16),
            sds((3, rows, width), F32),
            sds((3, rows, width), BF16),
        ),
        [(scalars, "s")] + [(a, "v") for a in (x12, sums, own3, near23, far13, w, *diag)],
        vmem=16,
    )


def matrix_of(prep, blocks, own):
    arrays = (prep[1], blocks[0], own[5], blocks[1], own[6], blocks[2], own[7])

    def readers(refs):
        own0, own12, own3, near01, near23, far02, far13 = refs
        return (
            lambda g: own0[...] if g == 0 else own3[...] if g == 3 else own12[g - 1],
            lambda g: (near01, near23)[g // 2][g % 2],
            lambda g: (far02, far13)[g % 2][g // 2],
        )

    return arrays, readers


def later_call(scalars, prep, own, rest, matrix):
    arrays, readers = matrix
    x, w = prep[0], prep[-1]
    layers = w.shape[0]
    rows, width = x.shape
    m = len(arrays)

    def body(sc, x_r, x12_r, x3_r, x1_r, x1n_r, w_r, *refs):
        own_at, near_at, far_at = readers(refs[:m])
        acts_o, mix_o, slope_o, xa_s, xb_s = refs[m:]
        seg = sc[0]
        first = (lambda: x_r[...], lambda: x12_r[0], lambda: x12_r[1], lambda: x3_r[...])

        @pl.when(seg == 0)
        def _():
            acts_o[...] = x1_r[...]

        def src(g):
            return x1n_r[g - 1] if g else x1_r[...]

        for k in range(1, layers):
            dst = (xa_s, xb_s)[k % 2]
            for g in range(4):
                agg = mm(own_at(g), src(g)) + mm(near_at(g), src(g ^ 1)) + mm(far_at(g), src(g ^ 2))
                mixed = mixed_of(agg, first[g]())
                mix_o[k - 1, g] = mixed
                slope_o[k - 1, g], out = activate(mixed, w_r[k], k)
                if k + 1 < layers:
                    dst[g] = out
                if g == 0:

                    @pl.when(seg == k)
                    def _():
                        acts_o[...] = out

            def src(g, dst=dst):
                return dst[g]

    return call(
        body,
        (
            sds((rows, width), BF16),
            sds((layers - 1, 4, rows, width), BF16),
            sds((layers - 1, 4, rows, width), F32),
        ),
        [(scalars, "s")] + [(a, "v") for a in (x, own[0], rest[0], own[3], rest[3], w, *arrays)],
        [pltpu.VMEM((4, rows, width), BF16)] * 2,
        min(60, 14 + 6 * layers),
    )


def dmix_of(dpre, w, k):
    beta = beta_of(k)
    return ((1.0 - beta) * dpre.astype(F32) + beta * mm_nt(dpre, w)).astype(BF16)


def back_start_call(scalars, cot, near, far, w, later_slope, matrix):
    arrays, readers = matrix
    layers = w.shape[0]
    rows, width = cot.shape
    piece = rows // layers
    m = len(arrays)
    last = layers - 1

    def body(sc, cot_r, w_r, slope_r, *refs):
        own_at, near_at, far_at = readers(refs[:m])
        got_r = [refs[m + g * layers : m + (g + 1) * layers] for g in range(2)]
        dpre_o, sums_o, carry_o, up_s = refs[m + 2 * layers :]
        seg = sc[0]
        for g in range(2):
            for k in range(layers):
                up_s[g, piece_slice(seg, k, layers, piece), :] = got_r[g][k][...]
        dmix = []
        for g in range(3):
            up = up_s[g - 1] if g else cot_r[...]
            dpre = (up.astype(F32) * slope_r[last - 1, g]).astype(BF16)
            dpre_o[pl.ds(g * rows, rows), :] = dpre
            dmix.append(dmix_of(dpre, w_r[last], last))
        carry_o[...] = SHARE * dmix[0].astype(F32)
        sums_o[0] = mm_tn(own_at(0), dmix[0]) + mm_tn(near_at(1), dmix[1]) + mm_tn(far_at(2), dmix[2])
        sums_o[1] = mm_tn(own_at(1), dmix[1]) + mm_tn(near_at(0), dmix[0])
        sums_o[2] = mm_tn(own_at(2), dmix[2]) + mm_tn(far_at(0), dmix[0])
        sums_o[3] = mm_tn(near_at(2), dmix[2]) + mm_tn(far_at(1), dmix[1])

    return call(
        body,
        (sds((3 * rows, width), BF16), sds((4, rows, width), F32), sds((rows, width), F32)),
        [(scalars, "s")] + [(a, "v") for a in (cot, w, later_slope, *arrays, *near, *far)],
        [pltpu.VMEM((2, rows, width), BF16)],
        min(60, 14 + 6 * layers),
    )


def back_call(scalars, diag, start, prep, own, rest, later_mix, later_slope, matrix):
    arrays, readers = matrix
    dpre_start, sums, carry = start
    mix, slope = own[1], own[2]
    mix_rest, slope_rest = rest[1], rest[2]
    w = prep[-1]
    layers = w.shape[0]
    rows, width = mix.shape
    piece = rows // layers
    n_dom = lax.axis_size("dom")
    others = n_dom // 4
    out_rows = width // n_dom
    half = width // 2
    m = len(arrays)
    last = layers - 1

    def body(sc, dps_r, sums_r, carry_r, mix_r, slope_r, mixn_r, slopen_r, later_mix_r, later_slope_r, w_r, *refs):
        own_at, near_at, far_at = readers(refs[:m])
        got_r = refs[m : m + layers]
        outs = refs[m + layers :]
        dpre_o, carry_o, mine_o = outs[:3]
        send_o = outs[3 : 2 + others]
        up_s, dmix_s, part_s = outs[2 + others :]
        seg, low, high, place = sc[0], sc[1], sc[2], sc[3]
        for k in range(layers):
            up_s[3, piece_slice(seg, k, layers, piece), :] = got_r[k][...]

        def weight_part(k, dpre_at):
            at = pl.ds(pl.multiple_of(high * half, half), half)
            part = None
            for g in range(4):
                chosen = later_mix_r[k - 1, g, :, at] if k else (mixn_r[g - 1, :, at] if g else mix_r[:, at])
                one = mm_tn(chosen, dpre_at(g))
                part = one if part is None else part + one
            part_s[...] = beta_of(k) * part

        dpre = (up_s[3].astype(F32) * later_slope_r[last - 1, 3]).astype(BF16)
        dpre_o[pl.ds(3 * rows, rows), :] = dpre
        dmix = dmix_of(dpre, w_r[last], last)
        extra = (None, mm_tn(far_at(3), dmix), mm_tn(near_at(3), dmix), mm_tn(own_at(3), dmix))
        for g in range(4):
            total = sums_r[g] if g == 0 else sums_r[g] + extra[g]
            up_s[g] = ((1.0 - SHARE) * total).astype(BF16)

        @pl.when(seg == last)
        def _():
            weight_part(last, lambda g: dps_r[pl.ds(g * rows, rows), :] if g < 3 else dpre_o[pl.ds(g * rows, rows), :])

        carry_o[...] = carry_r[...]
        for k in range(last - 1, -1, -1):
            for g in range(4):
                slope_now = later_slope_r[k - 1, g] if k else (slopen_r[g - 1] if g else slope_r[...])
                dpre = (up_s[g].astype(F32) * slope_now).astype(BF16)
                dpre_o[pl.ds(g * rows, rows), :] = dpre
                if k:
                    dmix = dmix_of(dpre, w_r[k], k)
                    dmix_s[g] = dmix
                    if g == 0:
                        carry_o[...] = SHARE * dmix.astype(F32) + carry_o[...]

            @pl.when(seg == k)
            def _():
                weight_part(k, lambda g: dpre_o[pl.ds(g * rows, rows), :])

            if k:
                for g in range(4):
                    total = (
                        mm_tn(own_at(g), dmix_s[g])
                        + mm_tn(near_at(g ^ 1), dmix_s[g ^ 1])
                        + mm_tn(far_at(g ^ 2), dmix_s[g ^ 2])
                    )
                    up_s[g] = ((1.0 - SHARE) * total).astype(BF16)

        def block(b):
            at = (place ^ b) * (2 * out_rows) + low * out_rows
            return part_s[pl.ds(pl.multiple_of(at, out_rows), out_rows), :]

        mine_o[...] = block(0)
        for b in range(1, others):
            send_o[b - 1][...] = block(b).astype(BF16)

    got = call(
        body,
        (sds((4 * rows, width), BF16), sds((rows, width), F32), sds((out_rows, width), F32))
        + tuple(sds((out_rows, width), BF16) for _ in range(1, others)),
        [(scalars, "s")]
        + [
            (a, "v")
            for a in (
                dpre_start,
                sums,
                carry,
                mix,
                slope,
                mix_rest,
                slope_rest,
                later_mix,
                later_slope,
                w,
                *arrays,
                *diag,
            )
        ],
        [
            pltpu.VMEM((4, rows, width), BF16),
            pltpu.VMEM((4, rows, width), BF16),
            pltpu.VMEM((half, width), F32),
        ],
        min(60, 14 + 6 * layers),
    )
    return got[0], got[1], got[2], got[3:]


def feat_call(scalars, dpre, carry, w, matrix):
    arrays, readers = matrix
    layers = w.shape[0]
    rows, width = carry.shape
    cols = width // layers
    sliced = cols % 128 == 0
    kept = cols if sliced else width
    m = len(arrays)
    beta = beta_of(0)

    def body(sc, dpre_r, carry_r, w_r, *refs):
        own_at, near_at, far_at = readers(refs[:m])
        feat_o = refs[m]
        at = pl.ds(pl.multiple_of(sc[0] * cols, cols), cols) if sliced else slice(None)
        w_rows = w_r[0, at, :]
        dmix = []
        for g in range(3):
            d_at = pl.ds(g * rows, rows)
            through = mm_nt(dpre_r[d_at, :], w_rows)
            dmix.append(((1.0 - beta) * dpre_r[d_at, at].astype(F32) + beta * through).astype(BF16))
        sums = mm_tn(own_at(0), dmix[0]) + mm_tn(near_at(1), dmix[1]) + mm_tn(far_at(2), dmix[2])
        feat_o[...] = (1.0 - SHARE) * sums + (carry_r[:, at] + SHARE * dmix[0].astype(F32))

    (feat,) = call(
        body,
        (sds((rows, kept), F32),),
        [(scalars, "s")] + [(a, "v") for a in (dpre, carry, w, *arrays)],
        vmem=12,
    )
    return feat if sliced else lax.dynamic_slice_in_dim(feat, scalars[0] * cols, cols, 1)


def step(feats, adj, couple, send_rows, weights, cot):
    seg = lax.axis_index("segment")
    dom = lax.axis_index("dom")
    layers = lax.axis_size("segment")
    n_dom = lax.axis_size("dom")
    top = n_dom // 2
    others = n_dom // 4
    place = (dom // 2) % others
    scalars = jnp.stack([seg, dom & 1, dom // top, place]).astype(jnp.int32)

    ac_mine, f_mine, cot_mine = pack_call(scalars, feats, adj, couple, send_rows, cot, layers)
    far_ac = swapped(ac_mine, top)
    near_ac = swapped(ac_mine, 1)
    w_pieces = every_piece(weights)
    prep = prep_call(scalars, feats, adj, couple, send_rows, w_pieces)
    far_f = swapped(f_mine, top)
    near_f = swapped(f_mine, 1)
    near_cot = swapped(cot_mine, 1)
    near_acs = every_piece(near_ac)
    diag_ac = swapped(far_ac, 1)
    far_acs = every_piece(far_ac)
    near_fs = every_piece(near_f)
    blocks = blocks_call(scalars, near_acs, far_acs, prep[2], prep[3])
    far_cot = swapped(cot_mine, top)
    diag_acs = every_piece(diag_ac)
    diag_f = swapped(far_f, 1)
    far_fs = every_piece(far_f)
    near_cots = every_piece(near_cot)
    own = own_call(scalars, near_fs, far_fs, diag_acs, prep, blocks)
    diag_fs = every_piece(diag_f)
    diag_cot = swapped(far_cot, 1)
    far_cots = every_piece(far_cot)
    matrix = matrix_of(prep, blocks, own)
    rest = rest_call(scalars, diag_fs, prep, own)
    acts, later_mix, later_slope = later_call(scalars, prep, own, rest, matrix)
    diag_cots = every_piece(diag_cot)
    start = back_start_call(scalars, cot, near_cots, far_cots, prep[-1], later_slope, matrix)
    dpre, carry, wgrad, sends = back_call(
        scalars, diag_cots, start, prep, own, rest, later_mix, later_slope, matrix
    )
    for m in range(others - 1, 0, -1):
        wgrad = wgrad + swapped(sends[m - 1], 2 * m).astype(F32)
    feat = feat_call(scalars, dpre, carry, prep[-1], matrix)
    return (acts[None], wgrad[None], feat)


def solution(mesh):
    in_specs = (
        P("dom", None),
        P("dom", None),
        P("dom", None),
        P("dom", None),
        P("segment", None),
        P("dom", None),
    )
    out_specs = (P("segment", "dom", None), P("segment", "dom", None), P("dom", "segment"))
    return jax.shard_map(step, mesh=mesh, in_specs=in_specs, out_specs=out_specs, check_vma=False)
```

```python
import math

import jax
import jax.numpy as jnp
from jax import lax
from jax.experimental import pallas as pl
from jax.experimental.pallas import tpu as pltpu
from jax.sharding import PartitionSpec as P


SHARE = 0.1
BETA_SCALE = 0.5
BF16 = jnp.bfloat16
F32 = jnp.float32


def swapped(x, mask):
    return lax.ppermute(x, "dom", [(i, i ^ mask) for i in range(lax.axis_size("dom"))])


def every_piece(x):
    n = lax.axis_size("segment")
    return [x] + [lax.ppermute(x, "segment", [(i, (i + k) % n) for i in range(n)]) for k in range(1, n)]


def beta_of(k):
    return math.log(BETA_SCALE / (k + 1.0) + 1.0)


def mm(a, b):
    return jnp.dot(a, b, preferred_element_type=F32)


def mm_nt(a, b):
    return lax.dot_general(a, b, (((1,), (1,)), ((), ())), preferred_element_type=F32)


def mm_tn(a, b):
    return lax.dot_general(a, b, (((0,), (0,)), ((), ())), preferred_element_type=F32)


def position():
    n = lax.axis_size("dom")
    dom = lax.axis_index("dom")
    return lax.axis_index("segment"), lax.rem(dom, 2), lax.div(dom, n // 2), lax.rem(lax.div(dom, 2), n // 4)


def place_of(seg, k, n):
    return lax.rem(seg - k + n, n)


def in_hbm(x):
    return pltpu.with_memory_space_constraint(x, pltpu.HBM)


def call(body, out_shape, ins, scratch=(), vmem=20):
    spaces = {"h": pltpu.HBM, "v": pltpu.VMEM}
    specs = [pl.BlockSpec(memory_space=spaces[m]) for _, m in ins]
    arrays = [in_hbm(a) if m == "h" else a for a, m in ins]
    return pl.pallas_call(
        body,
        out_shape=tuple(out_shape),
        in_specs=specs,
        out_specs=tuple(pl.BlockSpec(memory_space=pltpu.VMEM) for _ in out_shape),
        scratch_shapes=list(scratch),
        compiler_params=pltpu.CompilerParams(vmem_limit_bytes=vmem << 20),
    )(*arrays)


sds = jax.ShapeDtypeStruct


def pack_call(feats, adj, couple, send_rows, cot, layers):
    rows, width = feats.shape
    piece = rows // layers
    picked = send_rows.shape[1]

    def body(feats_r, adj_r, couple_r, sr_r, cot_r, fwd_o, cot_o, sr_s, sems):
        at = pl.ds(pl.multiple_of(lax.axis_index("segment") * piece, piece), piece)
        split = adj_r.shape[1]
        copies = [
            pltpu.make_async_copy(adj_r.at[at, :], fwd_o.at[:piece, :split], sems.at[1]),
            pltpu.make_async_copy(couple_r.at[at, :], fwd_o.at[:piece, split:], sems.at[2]),
            pltpu.make_async_copy(feats_r.at[at, :], fwd_o.at[piece : 2 * piece, :], sems.at[0]),
            pltpu.make_async_copy(cot_r.at[at, :], cot_o, sems.at[3]),
        ]
        sr_copy = pltpu.make_async_copy(sr_r, sr_s, sems.at[4])
        sr_copy.start()
        for c in copies:
            c.start()
        fwd_o[2 * piece :, picked:] = jnp.zeros((8, width - picked), BF16)
        sr_copy.wait()
        fwd_o[2 * piece :, :picked] = jnp.broadcast_to(sr_s[...].astype(F32), (8, picked)).astype(BF16)
        for c in copies:
            c.wait()

    return call(
        body,
        (sds((2 * piece + 8, width), BF16), sds((piece, width), BF16)),
        [(feats, "h"), (adj, "h"), (couple, "h"), (send_rows, "h"), (cot, "h")],
        [pltpu.VMEM(send_rows.shape, jnp.int32), pltpu.SemaphoreType.DMA((5,))],
        4,
    )


def picks_of(sr, rows):
    ids = lax.broadcasted_iota(jnp.int32, (rows, sr.shape[1]), 0).astype(F32)
    return (ids == sr).astype(F32).astype(BF16)


def scaled(first):
    return SHARE * first.astype(F32)


def mixed_of(agg, first_scaled):
    return ((1.0 - SHARE) * agg + first_scaled).astype(BF16)


def activate(mixed, w, k):
    beta = beta_of(k)
    half = (0.5 - 0.5 * beta) * mixed.astype(F32) + (0.5 * beta) * mm(mixed, w)
    t = jnp.tanh(half)
    up = 1.0 + t
    return up * (1.0 + half * (1.0 - t)), (half * up).astype(BF16)


def along(dim, *parts):
    return jnp.concatenate(parts, axis=dim)


def piece_slice(seg, k, layers, piece):
    return pl.ds(pl.multiple_of(place_of(seg, k, layers) * piece, piece), piece)


def prep_call(feats, adj, couple, send_rows):
    rows, width = feats.shape

    def body(feats_r, adj_r, couple_r, sr_r, x_o, own_o, couple_o, pick_o, agg_o, sr_s, sems):
        copies = [
            pltpu.make_async_copy(sr_r, sr_s, sems.at[0]),
            pltpu.make_async_copy(couple_r, couple_o, sems.at[1]),
            pltpu.make_async_copy(feats_r, x_o, sems.at[2]),
            pltpu.make_async_copy(adj_r, own_o, sems.at[3]),
        ]
        for c in copies:
            c.start()
        for c in copies:
            c.wait()
        pick_o[...] = picks_of(sr_s[...].astype(F32), rows)
        agg_o[...] = mm(own_o[...], x_o[...])

    return call(
        body,
        (
            sds((rows, width), BF16),
            sds((rows, rows), BF16),
            sds((rows, couple.shape[1]), BF16),
            sds((rows, send_rows.shape[1]), BF16),
            sds((rows, width), F32),
        ),
        [(feats, "h"), (adj, "h"), (couple, "h"), (send_rows, "h")],
        [pltpu.VMEM(send_rows.shape, jnp.int32), pltpu.SemaphoreType.DMA((4,))],
        8,
    )


def own_call(near, far, w_pieces, prep):
    x, _, couple, pick, agg = prep
    layers = len(near)
    rows, width = x.shape
    piece = rows // layers
    bound = couple.shape[1] // 2

    def body(x_r, couple_r, pick_r, agg_r, *refs):
        got_r = [refs[g * layers : (g + 1) * layers] for g in range(2)]
        w_r = refs[2 * layers : 3 * layers]
        outs = refs[3 * layers :]
        x12_o, mix_o, slope_o, x1_o, sums_o, own12_o, near01_o, far02_o, cp_o, pick_o, w_o, first_o, ac_s, sem = outs
        seg = lax.axis_index("segment")
        w_copy = pltpu.make_async_copy(w_r[0], w_o.at[seg], sem)
        w_copy.start()
        for k in range(1, layers):
            w_o[place_of(seg, k, layers)] = w_r[k][...]
        picks = []
        for g in range(2):
            for k in range(layers):
                at = piece_slice(seg, k, layers, piece)
                own12_o[g, at, :] = got_r[g][k][:piece, :rows]
                ac_s[g, at, :] = got_r[g][k][:piece, rows:]
                x12_o[g, at, :] = got_r[g][k][piece : 2 * piece, :]
            picks.append(picks_of(got_r[g][0][2 * piece : 2 * piece + 1, : 2 * bound].astype(F32), rows))
        near01_o[0] = mm_nt(couple_r[:, :bound], picks[0][:, :bound]).astype(BF16)
        far02_o[0] = mm_nt(couple_r[:, bound:], picks[1][:, bound:]).astype(BF16)
        near01_o[1] = mm_nt(ac_s[0, :, :bound], pick_r[:, :bound]).astype(BF16)
        far02_o[1] = mm_nt(ac_s[1, :, bound:], pick_r[:, bound:]).astype(BF16)
        cp_o[0] = ac_s[0, :, bound:]
        cp_o[1] = ac_s[1, :, :bound]
        pick_o[0] = picks[0][:, bound:]
        pick_o[1] = picks[1][:, :bound]
        sums_o[0] = mm(along(1, own12_o[0], near01_o[1]), along(0, x12_o[0], x_r[...]))
        sums_o[1] = mm(along(1, own12_o[1], far02_o[1]), along(0, x12_o[1], x_r[...]))
        first_o[0] = scaled(x_r[...])
        first_o[1] = scaled(x12_o[0])
        first_o[2] = scaled(x12_o[1])
        w_copy.wait()
        agg = agg_r[...] + mm(along(1, near01_o[0], far02_o[0]), along(0, x12_o[0], x12_o[1]))
        mixed = mixed_of(agg, first_o[0])
        mix_o[...] = mixed
        slope_o[...], x1_o[...] = activate(mixed, w_o[0], 0)

    return call(
        body,
        (
            sds((2, rows, width), BF16),
            sds((rows, width), BF16),
            sds((rows, width), F32),
            sds((rows, width), BF16),
            sds((2, rows, width), F32),
            sds((2, rows, rows), BF16),
            sds((2, rows, rows), BF16),
            sds((2, rows, rows), BF16),
            sds((2, rows, bound), BF16),
            sds((2, rows, bound), BF16),
            sds((layers, width, width), BF16),
            sds((3, rows, width), F32),
        ),
        [(a, "v") for a in (x, couple, pick, agg, *near, *far)]
        + [(w_pieces[0], "h")]
        + [(w, "v") for w in w_pieces[1:]],
        [pltpu.VMEM((2, rows, 2 * bound), BF16), pltpu.SemaphoreType.DMA],
        14 + 2 * layers,
    )


def rest_call(diag, own):
    x12, _, _, _, sums, _, _, _, cp, pick, w, first = own
    layers = len(diag)
    _, rows, width = x12.shape
    piece = rows // layers
    bound = cp.shape[2]

    def body(x12_r, sums_r, cp_r, pick_r, w_r, first_r, *refs):
        got_r = refs[:layers]
        first3_o, x3_s, mix_o, slope_o, x1_o, own3_o, near23_o, far13_o, ac_s = (refs[layers], refs[-1], *refs[layers + 1 : -1])
        seg = lax.axis_index("segment")
        for k in range(layers):
            at = piece_slice(seg, k, layers, piece)
            own3_o[at, :] = got_r[k][:piece, :rows]
            ac_s[at, :] = got_r[k][:piece, rows:]
            x3_s[at, :] = got_r[k][piece : 2 * piece, :]
        first3_o[...] = scaled(x3_s[...])
        picks = picks_of(got_r[0][2 * piece : 2 * piece + 1, : 2 * bound].astype(F32), rows)
        far13_o[0] = mm_nt(cp_r[0], picks[:, bound:]).astype(BF16)
        near23_o[0] = mm_nt(cp_r[1], picks[:, :bound]).astype(BF16)
        near23_o[1] = mm_nt(ac_s[:, :bound], pick_r[1]).astype(BF16)
        far13_o[1] = mm_nt(ac_s[:, bound:], pick_r[0]).astype(BF16)
        for g in range(3):
            if g < 2:
                agg = sums_r[g] + mm((far13_o, near23_o)[g][0], x3_s[...])
            else:
                agg = mm(along(1, own3_o[...], near23_o[1], far13_o[1]), along(0, x3_s[...], x12_r[1], x12_r[0]))
            mixed = mixed_of(agg, first_r[g + 1] if g < 2 else first3_o[...])
            mix_o[g] = mixed
            slope_o[g], x1_o[g] = activate(mixed, w_r[0], 0)

    return call(
        body,
        (
            sds((rows, width), F32),
            sds((3, rows, width), BF16),
            sds((3, rows, width), F32),
            sds((3, rows, width), BF16),
            sds((rows, rows), BF16),
            sds((2, rows, rows), BF16),
            sds((2, rows, rows), BF16),
        ),
        [(a, "v") for a in (x12, sums, cp, pick, w, first, *diag)],
        [pltpu.VMEM((rows, 2 * bound), BF16), pltpu.VMEM((rows, width), BF16)],
        16,
    )


def matrix_of(prep, own, rest):
    arrays = (prep[1], own[5], rest[4], own[6], rest[5], own[7], rest[6])

    def readers(refs):
        own0, own12, own3, near01, near23, far02, far13 = refs
        return (
            lambda g: own0[...] if g == 0 else own3[...] if g == 3 else own12[g - 1],
            lambda g: (near01, near23)[g // 2][g % 2],
            lambda g: (far02, far13)[g % 2][g // 2],
        )

    return arrays, readers


def later_call(w, own, rest, matrix):
    arrays, readers = matrix
    layers = w.shape[0]
    rows, width = own[1].shape
    m = len(arrays)

    def body(first_r, first3_r, x1_r, x1n_r, w_r, *refs):
        own_at, near_at, far_at = readers(refs[:m])
        acts_o, mix_o, slope_o, xa_s, xb_s = refs[m:]
        seg = lax.axis_index("segment")

        @pl.when(seg == 0)
        def _():
            acts_o[...] = x1_r[...]

        def src(g):
            return x1n_r[g - 1] if g else x1_r[...]

        for k in range(1, layers):
            dst = (xa_s, xb_s)[k % 2]
            for g in range(4):
                agg = mm(along(1, own_at(g), near_at(g), far_at(g)), along(0, src(g), src(g ^ 1), src(g ^ 2)))
                mixed = mixed_of(agg, first_r[g] if g < 3 else first3_r[...])
                mix_o[k - 1, g] = mixed
                slope_o[k - 1, g], out = activate(mixed, w_r[k], k)
                if k + 1 < layers:
                    dst[g] = out
                if g == 0:

                    @pl.when(seg == k)
                    def _():
                        acts_o[...] = out

            def src(g, dst=dst):
                return dst[g]

    return call(
        body,
        (
            sds((rows, width), BF16),
            sds((layers - 1, 4, rows, width), BF16),
            sds((layers - 1, 4, rows, width), F32),
        ),
        [(a, "v") for a in (own[-1], rest[0], own[3], rest[3], w, *arrays)],
        [pltpu.VMEM((4, rows, width), BF16)] * 2,
        min(60, 14 + 6 * layers),
    )


def dmix_of(dpre, w, k):
    beta = beta_of(k)
    return ((1.0 - beta) * dpre.astype(F32) + beta * mm_nt(dpre, w)).astype(BF16)


def back_start_call(cot, near, far, w, later_slope, matrix):
    arrays, readers = matrix
    layers = w.shape[0]
    rows, width = cot.shape
    piece = rows // layers
    m = len(arrays)
    last = layers - 1

    def body(cot_r, w_r, slope_r, *refs):
        own_at, near_at, far_at = readers(refs[:m])
        got_r = [refs[m + g * layers : m + (g + 1) * layers] for g in range(2)]
        dpre_o, sums_o, carry_o, up_s = refs[m + 2 * layers :]
        seg = lax.axis_index("segment")
        for g in range(2):
            for k in range(layers):
                up_s[g, piece_slice(seg, k, layers, piece), :] = got_r[g][k][...]
        dmix = []
        for g in range(3):
            up = up_s[g - 1] if g else cot_r[...]
            dpre = ((0.5 * up).astype(F32) * slope_r[last - 1, g]).astype(BF16)
            dpre_o[pl.ds(g * rows, rows), :] = dpre
            dmix.append(dmix_of(dpre, w_r[last], last))
        carry_o[...] = SHARE * dmix[0].astype(F32)
        sums_o[0] = mm_tn(along(0, own_at(0), near_at(1), far_at(2)), along(0, *dmix))
        sums_o[1] = mm_tn(along(0, near_at(0), own_at(1)), along(0, dmix[0], dmix[1]))
        sums_o[2] = mm_tn(along(0, far_at(0), own_at(2)), along(0, dmix[0], dmix[2]))
        sums_o[3] = mm_tn(along(0, far_at(1), near_at(2)), along(0, dmix[1], dmix[2]))

    return call(
        body,
        (sds((3 * rows, width), BF16), sds((4, rows, width), F32), sds((rows, width), F32)),
        [(a, "v") for a in (cot, w, later_slope, *arrays, *near, *far)],
        [pltpu.VMEM((2, rows, width), BF16)],
        min(60, 14 + 6 * layers),
    )


def back_call(diag, start, w, own, rest, later_mix, later_slope, matrix):
    arrays, readers = matrix
    dpre_start, sums, carry = start
    mix, slope = own[1], own[2]
    mix_rest, slope_rest = rest[1], rest[2]
    layers = w.shape[0]
    rows, width = mix.shape
    piece = rows // layers
    n_dom = lax.axis_size("dom")
    others = n_dom // 4
    out_rows = width // n_dom
    half = width // 2
    m = len(arrays)
    last = layers - 1

    def body(dps_r, sums_r, carry_r, mix_r, slope_r, mixn_r, slopen_r, later_mix_r, later_slope_r, w_r, *refs):
        own_at, near_at, far_at = readers(refs[:m])
        got_r = refs[m : m + layers]
        outs = refs[m + layers :]
        dpre_o, carry_o, mine_o = outs[:3]
        send_o = outs[3 : 2 + others]
        up_s, dmix_s, part_s = outs[2 + others :]
        seg, low, high, place = position()
        for k in range(layers):
            up_s[3, piece_slice(seg, k, layers, piece), :] = got_r[k][...]

        def weight_part(k, dpre_at):
            at = pl.ds(pl.multiple_of(high * half, half), half)
            chosen = [later_mix_r[k - 1, g, :, at] if k else (mixn_r[g - 1, :, at] if g else mix_r[:, at]) for g in range(4)]
            part_s[...] = beta_of(k) * mm_tn(along(0, *chosen), along(0, *[dpre_at(g) for g in range(4)]))

        dpre = ((0.5 * up_s[3]).astype(F32) * later_slope_r[last - 1, 3]).astype(BF16)
        dpre_o[pl.ds(3 * rows, rows), :] = dpre
        dmix = dmix_of(dpre, w_r[last], last)
        extra = (None, mm_tn(far_at(3), dmix), mm_tn(near_at(3), dmix), mm_tn(own_at(3), dmix))
        for g in range(4):
            total = sums_r[g] if g == 0 else sums_r[g] + extra[g]
            up_s[g] = ((0.5 - 0.5 * SHARE) * total).astype(BF16)

        @pl.when(seg == last)
        def _():
            weight_part(last, lambda g: dps_r[pl.ds(g * rows, rows), :] if g < 3 else dpre_o[pl.ds(g * rows, rows), :])

        carry_o[...] = carry_r[...]
        for k in range(last - 1, -1, -1):
            for g in range(4):
                slope_now = later_slope_r[k - 1, g] if k else (slopen_r[g - 1] if g else slope_r[...])
                dpre = (up_s[g].astype(F32) * slope_now).astype(BF16)
                dpre_o[pl.ds(g * rows, rows), :] = dpre
                if k:
                    dmix = dmix_of(dpre, w_r[k], k)
                    dmix_s[g] = dmix
                    if g == 0:
                        carry_o[...] = SHARE * dmix.astype(F32) + carry_o[...]

            @pl.when(seg == k)
            def _():
                weight_part(k, lambda g: dpre_o[pl.ds(g * rows, rows), :])

            if k:
                for g in range(4):
                    total = mm_tn(
                        along(0, own_at(g), near_at(g ^ 1), far_at(g ^ 2)), along(0, dmix_s[g], dmix_s[g ^ 1], dmix_s[g ^ 2])
                    )
                    up_s[g] = ((0.5 - 0.5 * SHARE) * total).astype(BF16)

        def block(b):
            at = (place ^ b) * (2 * out_rows) + low * out_rows
            return part_s[pl.ds(pl.multiple_of(at, out_rows), out_rows), :]

        mine_o[...] = block(0)
        for b in range(1, others):
            send_o[b - 1][...] = block(b).astype(BF16)

    got = call(
        body,
        (sds((4 * rows, width), BF16), sds((rows, width), F32), sds((out_rows, width), F32))
        + tuple(sds((out_rows, width), BF16) for _ in range(1, others)),
        [
            (a, "v")
            for a in (
                dpre_start,
                sums,
                carry,
                mix,
                slope,
                mix_rest,
                slope_rest,
                later_mix,
                later_slope,
                w,
                *arrays,
                *diag,
            )
        ],
        [
            pltpu.VMEM((4, rows, width), BF16),
            pltpu.VMEM((4, rows, width), BF16),
            pltpu.VMEM((half, width), F32),
        ],
        min(60, 14 + 6 * layers),
    )
    return got[0], got[1], got[2], got[3:]


def feat_call(dpre, carry, w, matrix):
    arrays, readers = matrix
    layers = w.shape[0]
    rows, width = carry.shape
    cols = width // layers
    sliced = cols % 128 == 0
    kept = cols if sliced else width
    m = len(arrays)
    beta = beta_of(0)

    def body(dpre_r, carry_r, w_r, *refs):
        own_at, near_at, far_at = readers(refs[:m])
        feat_o = refs[m]
        at = pl.ds(pl.multiple_of(lax.axis_index("segment") * cols, cols), cols) if sliced else slice(None)
        w_rows = w_r[0, at, :]
        dmix = []
        for g in range(3):
            d_at = pl.ds(g * rows, rows)
            through = mm_nt(dpre_r[d_at, :], w_rows)
            dmix.append(((1.0 - beta) * dpre_r[d_at, at].astype(F32) + beta * through).astype(BF16))
        sums = mm_tn(along(0, own_at(0), near_at(1), far_at(2)), along(0, *dmix))
        feat_o[...] = (1.0 - SHARE) * sums + (carry_r[:, at] + SHARE * dmix[0].astype(F32))

    (feat,) = call(body, (sds((rows, kept), F32),), [(a, "v") for a in (dpre, carry, w, *arrays)], vmem=12)
    return feat if sliced else lax.dynamic_slice_in_dim(feat, lax.axis_index("segment") * cols, cols, 1)


def step(feats, adj, couple, send_rows, weights, cot):
    layers = lax.axis_size("segment")
    n_dom = lax.axis_size("dom")
    top = n_dom // 2
    others = n_dom // 4

    fwd_mine, cot_mine = pack_call(feats, adj, couple, send_rows, cot, layers)
    far = swapped(fwd_mine, top)
    near = swapped(fwd_mine, 1)
    w_pieces = every_piece(weights)
    prep = prep_call(feats, adj, couple, send_rows)
    nears = every_piece(near)
    diag = swapped(far, 1)
    fars = every_piece(far)
    far_cot = swapped(cot_mine, top)
    own = own_call(nears, fars, w_pieces, prep)
    diags = every_piece(diag)
    near_cot = swapped(cot_mine, 1)
    rest = rest_call(diags, own)
    diag_cot = swapped(far_cot, 1)
    far_cots = every_piece(far_cot)
    near_cots = every_piece(near_cot)
    matrix = matrix_of(prep, own, rest)
    w = own[-2]
    acts, later_mix, later_slope = later_call(w, own, rest, matrix)
    diag_cots = every_piece(diag_cot)
    start = back_start_call(cot, near_cots, far_cots, w, later_slope, matrix)
    dpre, carry, wgrad, sends = back_call(diag_cots, start, w, own, rest, later_mix, later_slope, matrix
    )
    for m in range(1, others):
        wgrad = wgrad + swapped(sends[m - 1], 2 * m).astype(F32)
    feat = feat_call(dpre, carry, w, matrix)
    return (acts[None], wgrad[None], feat)


def solution(mesh):
    in_specs = (
        P("dom", None),
        P("dom", None),
        P("dom", None),
        P("dom", None),
        P("segment", None),
        P("dom", None),
    )
    out_specs = (P("segment", "dom", None), P("segment", "dom", None), P("dom", "segment"))
    return jax.shard_map(step, mesh=mesh, in_specs=in_specs, out_specs=out_specs, check_vma=False)
```

```python
import math

import jax
import jax.numpy as jnp
from jax import lax
from jax.experimental import pallas as pl
from jax.experimental.pallas import tpu as pltpu
from jax.sharding import PartitionSpec as P


SHARE = 0.1
BETA_SCALE = 0.5
BF16 = jnp.bfloat16
F32 = jnp.float32


def swapped(x, mask):
    return lax.ppermute(x, "dom", [(i, i ^ mask) for i in range(lax.axis_size("dom"))])


def every_piece(x):
    n = lax.axis_size("segment")
    return [x] + [lax.ppermute(x, "segment", [(i, (i + k) % n) for i in range(n)]) for k in range(1, n)]


def beta_of(k):
    return math.log(BETA_SCALE / (k + 1.0) + 1.0)


def mm(a, b):
    return jnp.dot(a, b, preferred_element_type=F32)


def mm_nt(a, b):
    return lax.dot_general(a, b, (((1,), (1,)), ((), ())), preferred_element_type=F32)


def mm_tn(a, b):
    return lax.dot_general(a, b, (((0,), (0,)), ((), ())), preferred_element_type=F32)


def position():
    n = lax.axis_size("dom")
    dom = lax.axis_index("dom")
    return lax.axis_index("segment"), lax.rem(dom, 2), lax.div(dom, n // 2), lax.rem(lax.div(dom, 2), n // 4)


def place_of(seg, k, n):
    return lax.rem(seg - k + n, n)


def in_hbm(x):
    return pltpu.with_memory_space_constraint(x, pltpu.HBM)


def call(body, out_shape, ins, scratch=(), vmem=20):
    spaces = {"h": pltpu.HBM, "v": pltpu.VMEM}
    specs = [pl.BlockSpec(memory_space=spaces[m]) for _, m in ins]
    arrays = [in_hbm(a) if m == "h" else a for a, m in ins]
    return pl.pallas_call(
        body,
        out_shape=tuple(out_shape),
        in_specs=specs,
        out_specs=tuple(pl.BlockSpec(memory_space=pltpu.VMEM) for _ in out_shape),
        scratch_shapes=list(scratch),
        compiler_params=pltpu.CompilerParams(vmem_limit_bytes=vmem << 20),
    )(*arrays)


sds = jax.ShapeDtypeStruct


def pack_call(feats, adj, couple, cot, layers):
    rows, width = feats.shape
    piece = rows // layers

    def body(feats_r, adj_r, couple_r, cot_r, fwd_o, cot_o, sems):
        at = pl.ds(pl.multiple_of(lax.axis_index("segment") * piece, piece), piece)
        split = adj_r.shape[1]
        copies = [
            pltpu.make_async_copy(adj_r.at[at, :], fwd_o.at[:piece, :split], sems.at[0]),
            pltpu.make_async_copy(couple_r.at[at, :], fwd_o.at[:piece, split:], sems.at[1]),
            pltpu.make_async_copy(feats_r.at[at, :], fwd_o.at[piece:, :], sems.at[2]),
            pltpu.make_async_copy(cot_r.at[at, :], cot_o, sems.at[3]),
        ]
        for c in copies:
            c.start()
        for c in copies:
            c.wait()

    return call(
        body,
        (sds((2 * piece, width), BF16), sds((piece, width), BF16)),
        [(feats, "h"), (adj, "h"), (couple, "h"), (cot, "h")],
        [pltpu.SemaphoreType.DMA((4,))],
        4,
    )


def picks_of(sr, rows):
    ids = lax.broadcasted_iota(jnp.int32, (rows, sr.shape[1]), 0).astype(F32)
    return (ids == sr).astype(F32).astype(BF16)


def scaled(first):
    return SHARE * first.astype(F32)


def mixed_of(agg, first_scaled):
    return ((1.0 - SHARE) * agg + first_scaled).astype(BF16)


def activate(mixed, through, k):
    beta = beta_of(k)
    half = (0.5 - 0.5 * beta) * mixed.astype(F32) + (0.5 * beta) * through
    t = jnp.tanh(half)
    up = 1.0 + t
    return up * (1.0 + half * (1.0 - t)), (half * up).astype(BF16)


def along(dim, *parts):
    return jnp.concatenate(parts, axis=dim)


def piece_slice(seg, k, layers, piece):
    return pl.ds(pl.multiple_of(place_of(seg, k, layers) * piece, piece), piece)


def prep_call(feats, adj, couple, send_rows):
    rows, width = feats.shape

    def body(feats_r, adj_r, couple_r, sr_r, x_o, own_o, couple_o, pick_o, agg_o, sr_s, sems):
        copies = [
            pltpu.make_async_copy(sr_r, sr_s, sems.at[0]),
            pltpu.make_async_copy(couple_r, couple_o, sems.at[1]),
            pltpu.make_async_copy(feats_r, x_o, sems.at[2]),
            pltpu.make_async_copy(adj_r, own_o, sems.at[3]),
        ]
        for c in copies:
            c.start()
        for c in copies:
            c.wait()
        pick_o[...] = picks_of(sr_s[...].astype(F32), rows)
        agg_o[...] = mm(own_o[...], x_o[...])

    return call(
        body,
        (
            sds((rows, width), BF16),
            sds((rows, rows), BF16),
            sds((rows, couple.shape[1]), BF16),
            sds((rows, send_rows.shape[1]), BF16),
            sds((rows, width), F32),
        ),
        [(feats, "h"), (adj, "h"), (couple, "h"), (send_rows, "h")],
        [pltpu.VMEM(send_rows.shape, jnp.int32), pltpu.SemaphoreType.DMA((4,))],
        8,
    )


def own_call(near, far, near_sr, far_sr, w_pieces, prep):
    x, _, couple, pick, agg = prep
    layers = len(near)
    rows, width = x.shape
    piece = rows // layers
    bound = couple.shape[1] // 2

    def body(x_r, couple_r, pick_r, agg_r, near_sr_r, far_sr_r, *refs):
        got_r = [refs[g * layers : (g + 1) * layers] for g in range(2)]
        w_r = refs[2 * layers : 3 * layers]
        outs = refs[3 * layers :]
        x12_o, mix_o, slope_o, x1_o, sums_o, own12_o, near01_o, far02_o, cp_o, pick_o, w_o, first_o, wt_o, ac_s, sem = outs
        seg = lax.axis_index("segment")
        w_copy = pltpu.make_async_copy(w_r[0], w_o.at[seg], sem)
        w_copy.start()
        for k in range(1, layers):
            w_o[place_of(seg, k, layers)] = w_r[k][...]
        picks = []
        for g in range(2):
            for k in range(layers):
                at = piece_slice(seg, k, layers, piece)
                own12_o[g, at, :] = got_r[g][k][:piece, :rows]
                ac_s[g, at, :] = got_r[g][k][:piece, rows:]
                x12_o[g, at, :] = got_r[g][k][piece : 2 * piece, :]
            picks.append(picks_of((near_sr_r, far_sr_r)[g][...].astype(F32), rows))
        near01_o[0] = mm_nt(couple_r[:, :bound], picks[0][:, :bound]).astype(BF16)
        far02_o[0] = mm_nt(couple_r[:, bound:], picks[1][:, bound:]).astype(BF16)
        near01_o[1] = mm_nt(ac_s[0, :, :bound], pick_r[:, :bound]).astype(BF16)
        far02_o[1] = mm_nt(ac_s[1, :, bound:], pick_r[:, bound:]).astype(BF16)
        cp_o[0] = ac_s[0, :, bound:]
        cp_o[1] = ac_s[1, :, :bound]
        pick_o[0] = picks[0][:, bound:]
        pick_o[1] = picks[1][:, :bound]
        sums_o[0] = mm(along(1, own12_o[0], near01_o[1]), along(0, x12_o[0], x_r[...]))
        sums_o[1] = mm(along(1, own12_o[1], far02_o[1]), along(0, x12_o[1], x_r[...]))
        first_o[0] = scaled(x_r[...])
        first_o[1] = scaled(x12_o[0])
        first_o[2] = scaled(x12_o[1])
        w_copy.wait()
        for k in range(layers):
            wt_o[k] = w_o[k].T
        agg = agg_r[...] + mm(along(1, near01_o[0], far02_o[0]), along(0, x12_o[0], x12_o[1]))
        mixed = mixed_of(agg, first_o[0])
        mix_o[...] = mixed
        slope_o[...], x1_o[...] = activate(mixed, mm(mixed, w_o[0]), 0)

    return call(
        body,
        (
            sds((2, rows, width), BF16),
            sds((rows, width), BF16),
            sds((rows, width), F32),
            sds((rows, width), BF16),
            sds((2, rows, width), F32),
            sds((2, rows, rows), BF16),
            sds((2, rows, rows), BF16),
            sds((2, rows, rows), BF16),
            sds((2, rows, bound), BF16),
            sds((2, rows, bound), BF16),
            sds((layers, width, width), BF16),
            sds((3, rows, width), F32),
            sds((layers, width, width), BF16),
        ),
        [(a, "v") for a in (x, couple, pick, agg, near_sr, far_sr, *near, *far)]
        + [(w_pieces[0], "h")]
        + [(w, "v") for w in w_pieces[1:]],
        [pltpu.VMEM((2, rows, 2 * bound), BF16), pltpu.SemaphoreType.DMA],
        14 + 2 * layers,
    )


def rest_call(diag, diag_sr, own):
    x12, _, _, _, sums, _, _, _, cp, pick, w, first, _ = own
    layers = len(diag)
    _, rows, width = x12.shape
    piece = rows // layers
    bound = cp.shape[2]

    def body(x12_r, sums_r, cp_r, pick_r, w_r, first_r, sr_r, *refs):
        got_r = refs[:layers]
        first3_o, x3_s, mix_o, slope_o, x1_o, own3_o, near23_o, far13_o, ac_s = (refs[layers], refs[-1], *refs[layers + 1 : -1])
        seg = lax.axis_index("segment")
        for k in range(layers):
            at = piece_slice(seg, k, layers, piece)
            own3_o[at, :] = got_r[k][:piece, :rows]
            ac_s[at, :] = got_r[k][:piece, rows:]
            x3_s[at, :] = got_r[k][piece : 2 * piece, :]
        first3_o[...] = scaled(x3_s[...])
        picks = picks_of(sr_r[...].astype(F32), rows)
        far13_o[0] = mm_nt(cp_r[0], picks[:, bound:]).astype(BF16)
        near23_o[0] = mm_nt(cp_r[1], picks[:, :bound]).astype(BF16)
        near23_o[1] = mm_nt(ac_s[:, :bound], pick_r[1]).astype(BF16)
        far13_o[1] = mm_nt(ac_s[:, bound:], pick_r[0]).astype(BF16)
        for g in range(3):
            if g < 2:
                agg = sums_r[g] + mm((far13_o, near23_o)[g][0], x3_s[...])
            else:
                agg = mm(along(1, own3_o[...], near23_o[1], far13_o[1]), along(0, x3_s[...], x12_r[1], x12_r[0]))
            mixed = mixed_of(agg, first_r[g + 1] if g < 2 else first3_o[...])
            mix_o[g] = mixed
        through = mm(along(0, *[mix_o[g] for g in range(3)]), w_r[0])
        for g in range(3):
            slope_o[g], x1_o[g] = activate(mix_o[g], through[g * rows : (g + 1) * rows], 0)

    return call(
        body,
        (
            sds((rows, width), F32),
            sds((3, rows, width), BF16),
            sds((3, rows, width), F32),
            sds((3, rows, width), BF16),
            sds((rows, rows), BF16),
            sds((2, rows, rows), BF16),
            sds((2, rows, rows), BF16),
        ),
        [(a, "v") for a in (x12, sums, cp, pick, w, first, diag_sr, *diag)],
        [pltpu.VMEM((rows, 2 * bound), BF16), pltpu.VMEM((rows, width), BF16)],
        16,
    )


def matrix_of(prep, own, rest):
    arrays = (prep[1], own[5], rest[4], own[6], rest[5], own[7], rest[6])

    def readers(refs):
        own0, own12, own3, near01, near23, far02, far13 = refs
        return (
            lambda g: own0[...] if g == 0 else own3[...] if g == 3 else own12[g - 1],
            lambda g: (near01, near23)[g // 2][g % 2],
            lambda g: (far02, far13)[g % 2][g // 2],
        )

    return arrays, readers


def later_call(w, own, rest, matrix):
    arrays, readers = matrix
    layers = w.shape[0]
    rows, width = own[1].shape
    m = len(arrays)

    def body(first_r, first3_r, x1_r, x1n_r, w_r, *refs):
        own_at, near_at, far_at = readers(refs[:m])
        acts_o, mix_o, slope_o, xa_s, xb_s = refs[m:]
        seg = lax.axis_index("segment")

        @pl.when(seg == 0)
        def _():
            acts_o[...] = x1_r[...]

        def src(g):
            return x1n_r[g - 1] if g else x1_r[...]

        for k in range(1, layers):
            dst = (xa_s, xb_s)[k % 2]
            for g in range(4):
                agg = mm(along(1, own_at(g), near_at(g), far_at(g)), along(0, src(g), src(g ^ 1), src(g ^ 2)))
                mixed = mixed_of(agg, first_r[g] if g < 3 else first3_r[...])
                mix_o[k - 1, g] = mixed
            through = mm(along(0, *[mix_o[k - 1, g] for g in range(4)]), w_r[k])
            for g in range(4):
                slope_o[k - 1, g], out = activate(mix_o[k - 1, g], through[g * rows : (g + 1) * rows], k)
                if k + 1 < layers:
                    dst[g] = out
                if g == 0:

                    @pl.when(seg == k)
                    def _():
                        acts_o[...] = out

            def src(g, dst=dst):
                return dst[g]

    return call(
        body,
        (
            sds((rows, width), BF16),
            sds((layers - 1, 4, rows, width), BF16),
            sds((layers - 1, 4, rows, width), F32),
        ),
        [(a, "v") for a in (own[-2], rest[0], own[3], rest[3], w, *arrays)],
        [pltpu.VMEM((4, rows, width), BF16)] * 2,
        min(60, 14 + 6 * layers),
    )


def dmix_of(dpre, w_t, k):
    beta = beta_of(k)
    return ((1.0 - beta) * dpre.astype(F32) + beta * mm(dpre, w_t)).astype(BF16)


def back_start_call(cot, near, far, w, later_slope, matrix):
    arrays, readers = matrix
    layers = w.shape[0]
    rows, width = cot.shape
    piece = rows // layers
    m = len(arrays)
    last = layers - 1

    def body(cot_r, w_r, slope_r, *refs):
        own_at, near_at, far_at = readers(refs[:m])
        got_r = [refs[m + g * layers : m + (g + 1) * layers] for g in range(2)]
        dpre_o, sums_o, carry_o, up_s = refs[m + 2 * layers :]
        seg = lax.axis_index("segment")
        for g in range(2):
            for k in range(layers):
                up_s[g, piece_slice(seg, k, layers, piece), :] = got_r[g][k][...]
        dmix = []
        for g in range(3):
            up = up_s[g - 1] if g else cot_r[...]
            dpre = ((0.5 * up).astype(F32) * slope_r[last - 1, g]).astype(BF16)
            dpre_o[pl.ds(g * rows, rows), :] = dpre
            dmix.append(dmix_of(dpre, w_r[last], last))
        carry_o[...] = SHARE * dmix[0].astype(F32)
        sums_o[0] = mm_tn(along(0, own_at(0), near_at(1), far_at(2)), along(0, *dmix))
        sums_o[1] = mm_tn(along(0, near_at(0), own_at(1)), along(0, dmix[0], dmix[1]))
        sums_o[2] = mm_tn(along(0, far_at(0), own_at(2)), along(0, dmix[0], dmix[2]))
        sums_o[3] = mm_tn(along(0, far_at(1), near_at(2)), along(0, dmix[1], dmix[2]))

    return call(
        body,
        (sds((3 * rows, width), BF16), sds((4, rows, width), F32), sds((rows, width), F32)),
        [(a, "v") for a in (cot, w, later_slope, *arrays, *near, *far)],
        [pltpu.VMEM((2, rows, width), BF16)],
        min(60, 14 + 6 * layers),
    )


def back_call(diag, start, w, own, rest, later_mix, later_slope, matrix):
    arrays, readers = matrix
    dpre_start, sums, carry = start
    mix, slope = own[1], own[2]
    mix_rest, slope_rest = rest[1], rest[2]
    layers = w.shape[0]
    rows, width = mix.shape
    piece = rows // layers
    n_dom = lax.axis_size("dom")
    others = n_dom // 4
    out_rows = width // n_dom
    half = width // 2
    m = len(arrays)
    last = layers - 1

    def body(dps_r, sums_r, carry_r, mix_r, slope_r, mixn_r, slopen_r, later_mix_r, later_slope_r, w_r, *refs):
        own_at, near_at, far_at = readers(refs[:m])
        got_r = refs[m : m + layers]
        outs = refs[m + layers :]
        dpre_o, carry_o, mine_o = outs[:3]
        send_o = outs[3 : 2 + others]
        up_s, dmix_s, part_s = outs[2 + others :]
        seg, low, high, place = position()
        for k in range(layers):
            up_s[3, piece_slice(seg, k, layers, piece), :] = got_r[k][...]

        def weight_part(k, dpre_at):
            at = pl.ds(pl.multiple_of(high * half, half), half)
            chosen = [later_mix_r[k - 1, g, :, at] if k else (mixn_r[g - 1, :, at] if g else mix_r[:, at]) for g in range(4)]
            part_s[...] = beta_of(k) * mm_tn(along(0, *chosen), along(0, *[dpre_at(g) for g in range(4)]))

        dpre = ((0.5 * up_s[3]).astype(F32) * later_slope_r[last - 1, 3]).astype(BF16)
        dpre_o[pl.ds(3 * rows, rows), :] = dpre
        dmix = dmix_of(dpre, w_r[last], last)
        extra = (None, mm_tn(far_at(3), dmix), mm_tn(near_at(3), dmix), mm_tn(own_at(3), dmix))
        for g in range(4):
            total = sums_r[g] if g == 0 else sums_r[g] + extra[g]
            up_s[g] = ((0.5 - 0.5 * SHARE) * total).astype(BF16)

        @pl.when(seg == last)
        def _():
            weight_part(last, lambda g: dps_r[pl.ds(g * rows, rows), :] if g < 3 else dpre_o[pl.ds(g * rows, rows), :])

        carry_o[...] = carry_r[...]
        for k in range(last - 1, -1, -1):
            for g in range(4):
                slope_now = later_slope_r[k - 1, g] if k else (slopen_r[g - 1] if g else slope_r[...])
                dpre = (up_s[g].astype(F32) * slope_now).astype(BF16)
                dpre_o[pl.ds(g * rows, rows), :] = dpre
                if k:
                    dmix = dmix_of(dpre, w_r[k], k)
                    dmix_s[g] = dmix
                    if g == 0:
                        carry_o[...] = SHARE * dmix.astype(F32) + carry_o[...]

            @pl.when(seg == k)
            def _():
                weight_part(k, lambda g: dpre_o[pl.ds(g * rows, rows), :])

            if k:
                for g in range(4):
                    total = mm_tn(
                        along(0, own_at(g), near_at(g ^ 1), far_at(g ^ 2)), along(0, dmix_s[g], dmix_s[g ^ 1], dmix_s[g ^ 2])
                    )
                    up_s[g] = ((0.5 - 0.5 * SHARE) * total).astype(BF16)

        def block(b):
            at = (place ^ b) * (2 * out_rows) + low * out_rows
            return part_s[pl.ds(pl.multiple_of(at, out_rows), out_rows), :]

        mine_o[...] = block(0)
        for b in range(1, others):
            send_o[b - 1][...] = block(b).astype(BF16)

    got = call(
        body,
        (sds((4 * rows, width), BF16), sds((rows, width), F32), sds((out_rows, width), F32))
        + tuple(sds((out_rows, width), BF16) for _ in range(1, others)),
        [
            (a, "v")
            for a in (
                dpre_start,
                sums,
                carry,
                mix,
                slope,
                mix_rest,
                slope_rest,
                later_mix,
                later_slope,
                w,
                *arrays,
                *diag,
            )
        ],
        [
            pltpu.VMEM((4, rows, width), BF16),
            pltpu.VMEM((4, rows, width), BF16),
            pltpu.VMEM((half, width), F32),
        ],
        min(60, 14 + 6 * layers),
    )
    return got[0], got[1], got[2], got[3:]


def feat_call(dpre, carry, w, matrix):
    arrays, readers = matrix
    layers = w.shape[0]
    rows, width = carry.shape
    cols = width // layers
    sliced = cols % 128 == 0
    kept = cols if sliced else width
    m = len(arrays)
    beta = beta_of(0)

    def body(dpre_r, carry_r, w_r, *refs):
        own_at, near_at, far_at = readers(refs[:m])
        feat_o = refs[m]
        at = pl.ds(pl.multiple_of(lax.axis_index("segment") * cols, cols), cols) if sliced else slice(None)
        w_cols = w_r[0, :, at]
        dmix = []
        for g in range(3):
            d_at = pl.ds(g * rows, rows)
            through = mm(dpre_r[d_at, :], w_cols)
            dmix.append(((1.0 - beta) * dpre_r[d_at, at].astype(F32) + beta * through).astype(BF16))
        sums = mm_tn(along(0, own_at(0), near_at(1), far_at(2)), along(0, *dmix))
        feat_o[...] = (1.0 - SHARE) * sums + (carry_r[:, at] + SHARE * dmix[0].astype(F32))

    (feat,) = call(body, (sds((rows, kept), F32),), [(a, "v") for a in (dpre, carry, w, *arrays)], vmem=12)
    return feat if sliced else lax.dynamic_slice_in_dim(feat, lax.axis_index("segment") * cols, cols, 1)


def step(feats, adj, couple, send_rows, weights, cot):
    layers = lax.axis_size("segment")
    n_dom = lax.axis_size("dom")
    top = n_dom // 2
    others = n_dom // 4

    fwd_mine, cot_mine = pack_call(feats, adj, couple, cot, layers)
    far = swapped(fwd_mine, top)
    near = swapped(fwd_mine, 1)
    w_pieces = every_piece(weights)
    far_sr = swapped(send_rows, top)
    near_sr = swapped(send_rows, 1)
    diag_sr = swapped(send_rows, top + 1)
    prep = prep_call(feats, adj, couple, send_rows)
    nears = every_piece(near)
    diag = swapped(far, 1)
    fars = every_piece(far)
    far_cot = swapped(cot_mine, top)
    own = own_call(nears, fars, near_sr, far_sr, w_pieces, prep)
    diags = every_piece(diag)
    near_cot = swapped(cot_mine, 1)
    rest = rest_call(diags, diag_sr, own)
    diag_cot = swapped(far_cot, 1)
    far_cots = every_piece(far_cot)
    near_cots = every_piece(near_cot)
    matrix = matrix_of(prep, own, rest)
    w, w_t = own[-3], own[-1]
    acts, later_mix, later_slope = later_call(w, own, rest, matrix)
    diag_cots = every_piece(diag_cot)
    start = back_start_call(cot, near_cots, far_cots, w_t, later_slope, matrix)
    dpre, carry, wgrad, sends = back_call(diag_cots, start, w_t, own, rest, later_mix, later_slope, matrix
    )
    for m in range(1, others):
        wgrad = wgrad + swapped(sends[m - 1], 2 * m).astype(F32)
    feat = feat_call(dpre, carry, w_t, matrix)
    return (acts[None], wgrad[None], feat)


def solution(mesh):
    in_specs = (
        P("dom", None),
        P("dom", None),
        P("dom", None),
        P("dom", None),
        P("segment", None),
        P("dom", None),
    )
    out_specs = (P("segment", "dom", None), P("segment", "dom", None), P("dom", "segment"))
    return jax.shard_map(step, mesh=mesh, in_specs=in_specs, out_specs=out_specs, check_vma=False)
```

```python
import math

import jax
import jax.numpy as jnp
from jax import lax
from jax.experimental import pallas as pl
from jax.experimental.pallas import tpu as pltpu
from jax.sharding import PartitionSpec as P


SHARE = 0.1
BETA_SCALE = 0.5
BF16 = jnp.bfloat16
F32 = jnp.float32


def swapped(x, mask):
    return lax.ppermute(x, "dom", [(i, i ^ mask) for i in range(lax.axis_size("dom"))])


def every_piece(x):
    n = lax.axis_size("segment")
    return [x] + [lax.ppermute(x, "segment", [(i, (i + k) % n) for i in range(n)]) for k in range(1, n)]


def beta_of(k):
    return math.log(BETA_SCALE / (k + 1.0) + 1.0)


def mm(a, b):
    return jnp.dot(a, b, preferred_element_type=F32)


def mm_nt(a, b):
    return lax.dot_general(a, b, (((1,), (1,)), ((), ())), preferred_element_type=F32)


def mm_tn(a, b):
    return lax.dot_general(a, b, (((0,), (0,)), ((), ())), preferred_element_type=F32)


def position():
    n = lax.axis_size("dom")
    dom = lax.axis_index("dom")
    return lax.axis_index("segment"), lax.rem(dom, 2), lax.div(dom, n // 2), lax.rem(lax.div(dom, 2), n // 4)


def place_of(seg, k, n):
    return lax.rem(seg - k + n, n)


def in_hbm(x):
    return pltpu.with_memory_space_constraint(x, pltpu.HBM)


def call(body, out_shape, ins, scratch=(), vmem=20):
    spaces = {"h": pltpu.HBM, "v": pltpu.VMEM}
    specs = [pl.BlockSpec(memory_space=spaces[m]) for _, m in ins]
    arrays = [in_hbm(a) if m == "h" else a for a, m in ins]
    return pl.pallas_call(
        body,
        out_shape=tuple(out_shape),
        in_specs=specs,
        out_specs=tuple(pl.BlockSpec(memory_space=pltpu.VMEM) for _ in out_shape),
        scratch_shapes=list(scratch),
        compiler_params=pltpu.CompilerParams(vmem_limit_bytes=vmem << 20),
    )(*arrays)


sds = jax.ShapeDtypeStruct


def pack_call(feats, adj, couple, cot, layers):
    rows, width = feats.shape
    piece = rows // layers

    def body(feats_r, adj_r, couple_r, cot_r, fwd_o, cot_o, sems):
        at = pl.ds(pl.multiple_of(lax.axis_index("segment") * piece, piece), piece)
        split = adj_r.shape[1]
        copies = [
            pltpu.make_async_copy(adj_r.at[at, :], fwd_o.at[:piece, :split], sems.at[0]),
            pltpu.make_async_copy(couple_r.at[at, :], fwd_o.at[:piece, split:], sems.at[1]),
            pltpu.make_async_copy(feats_r.at[at, :], fwd_o.at[piece:, :], sems.at[2]),
            pltpu.make_async_copy(cot_r.at[at, :], cot_o, sems.at[3]),
        ]
        for c in copies:
            c.start()
        for c in copies:
            c.wait()

    return call(
        body,
        (sds((2 * piece, width), BF16), sds((piece, width), BF16)),
        [(feats, "h"), (adj, "h"), (couple, "h"), (cot, "h")],
        [pltpu.SemaphoreType.DMA((4,))],
        4,
    )


def picks_of(sr, rows):
    ids = lax.broadcasted_iota(jnp.int32, (rows, sr.shape[1]), 0).astype(F32)
    return (ids == sr).astype(F32).astype(BF16)


def scaled(first):
    return SHARE * first.astype(F32)


def mixed_of(agg, first_scaled):
    return ((1.0 - SHARE) * agg + first_scaled).astype(BF16)


def activate(mixed, through, k):
    beta = beta_of(k)
    half = (0.5 - 0.5 * beta) * mixed.astype(F32) + (0.5 * beta) * through
    t = jnp.tanh(half)
    up = 1.0 + t
    return up * (1.0 + half * (1.0 - t)), (half * up).astype(BF16)


def along(dim, *parts):
    return jnp.concatenate(parts, axis=dim)


def piece_slice(seg, k, layers, piece):
    return pl.ds(pl.multiple_of(place_of(seg, k, layers) * piece, piece), piece)


def prep_call(feats, adj, couple, send_rows):
    rows, width = feats.shape

    def body(feats_r, adj_r, couple_r, sr_r, x_o, own_o, couple_o, pick_o, agg_o, sr_s, sems):
        copies = [
            pltpu.make_async_copy(sr_r, sr_s, sems.at[0]),
            pltpu.make_async_copy(couple_r, couple_o, sems.at[1]),
            pltpu.make_async_copy(feats_r, x_o, sems.at[2]),
            pltpu.make_async_copy(adj_r, own_o, sems.at[3]),
        ]
        for c in copies:
            c.start()
        for c in copies:
            c.wait()
        pick_o[...] = picks_of(sr_s[...].astype(F32), rows)
        agg_o[...] = mm(own_o[...], x_o[...])

    return call(
        body,
        (
            sds((rows, width), BF16),
            sds((rows, rows), BF16),
            sds((rows, couple.shape[1]), BF16),
            sds((rows, send_rows.shape[1]), BF16),
            sds((rows, width), F32),
        ),
        [(feats, "h"), (adj, "h"), (couple, "h"), (send_rows, "h")],
        [pltpu.VMEM(send_rows.shape, jnp.int32), pltpu.SemaphoreType.DMA((4,))],
        8,
    )


def own_call(near, far, near_sr, far_sr, w_pieces, prep):
    x, _, couple, pick, agg = prep
    layers = len(near)
    rows, width = x.shape
    piece = rows // layers
    bound = couple.shape[1] // 2

    def body(x_r, couple_r, pick_r, agg_r, near_sr_r, far_sr_r, *refs):
        got_r = [refs[g * layers : (g + 1) * layers] for g in range(2)]
        w_r = refs[2 * layers : 3 * layers]
        outs = refs[3 * layers :]
        x12_o, mix_o, slope_o, x1_o, sums_o, own12_o, near01_o, far02_o, cp_o, pick_o, w_o, first_o, wt_o, ac_s, sem = outs
        seg = lax.axis_index("segment")
        w_copy = pltpu.make_async_copy(w_r[0], w_o.at[seg], sem)
        w_copy.start()
        for k in range(1, layers):
            w_o[place_of(seg, k, layers)] = w_r[k][...]
        picks = []
        for g in range(2):
            for k in range(layers):
                at = piece_slice(seg, k, layers, piece)
                own12_o[g, at, :] = got_r[g][k][:piece, :rows]
                ac_s[g, at, :] = got_r[g][k][:piece, rows:]
                x12_o[g, at, :] = got_r[g][k][piece : 2 * piece, :]
            picks.append(picks_of((near_sr_r, far_sr_r)[g][...].astype(F32), rows))
        near01_o[0] = mm_nt(couple_r[:, :bound], picks[0][:, :bound]).astype(BF16)
        far02_o[0] = mm_nt(couple_r[:, bound:], picks[1][:, bound:]).astype(BF16)
        near01_o[1] = mm_nt(ac_s[0, :, :bound], pick_r[:, :bound]).astype(BF16)
        far02_o[1] = mm_nt(ac_s[1, :, bound:], pick_r[:, bound:]).astype(BF16)
        cp_o[0] = ac_s[0, :, bound:]
        cp_o[1] = ac_s[1, :, :bound]
        pick_o[0] = picks[0][:, bound:]
        pick_o[1] = picks[1][:, :bound]
        sums_o[0] = mm(along(1, own12_o[0], near01_o[1]), along(0, x12_o[0], x_r[...]))
        sums_o[1] = mm(along(1, own12_o[1], far02_o[1]), along(0, x12_o[1], x_r[...]))
        first_o[0] = scaled(x_r[...])
        first_o[1] = scaled(x12_o[0])
        first_o[2] = scaled(x12_o[1])
        w_copy.wait()
        for k in range(layers):
            wt_o[k] = w_o[k].T
        agg = agg_r[...] + mm(along(1, near01_o[0], far02_o[0]), along(0, x12_o[0], x12_o[1]))
        mixed = mixed_of(agg, first_o[0])
        mix_o[...] = mixed
        slope_o[...], x1_o[...] = activate(mixed, mm(mixed, w_o[0]), 0)

    return call(
        body,
        (
            sds((2, rows, width), BF16),
            sds((rows, width), BF16),
            sds((rows, width), F32),
            sds((rows, width), BF16),
            sds((2, rows, width), F32),
            sds((2, rows, rows), BF16),
            sds((2, rows, rows), BF16),
            sds((2, rows, rows), BF16),
            sds((2, rows, bound), BF16),
            sds((2, rows, bound), BF16),
            sds((layers, width, width), BF16),
            sds((3, rows, width), F32),
            sds((layers, width, width), BF16),
        ),
        [(a, "v") for a in (x, couple, pick, agg, near_sr, far_sr, *near, *far)]
        + [(w_pieces[0], "h")]
        + [(w, "v") for w in w_pieces[1:]],
        [pltpu.VMEM((2, rows, 2 * bound), BF16), pltpu.SemaphoreType.DMA],
        14 + 2 * layers,
    )


def rest_call(diag, diag_sr, own):
    x12, _, _, _, sums, _, _, _, cp, pick, w, first, _ = own
    layers = len(diag)
    _, rows, width = x12.shape
    piece = rows // layers
    bound = cp.shape[2]

    def body(x12_r, sums_r, cp_r, pick_r, w_r, first_r, sr_r, *refs):
        got_r = refs[:layers]
        first3_o, x3_s, mix_o, slope_o, x1_o, own3_o, near23_o, far13_o, back3_o, ac_s = (refs[layers], refs[-1], *refs[layers + 1 : -1])
        seg = lax.axis_index("segment")
        for k in range(layers):
            at = piece_slice(seg, k, layers, piece)
            own3_o[at, :] = got_r[k][:piece, :rows]
            ac_s[at, :] = got_r[k][:piece, rows:]
            x3_s[at, :] = got_r[k][piece : 2 * piece, :]
        first3_o[...] = scaled(x3_s[...])
        picks = picks_of(sr_r[...].astype(F32), rows)
        far13_o[0] = mm_nt(cp_r[0], picks[:, bound:]).astype(BF16)
        near23_o[0] = mm_nt(cp_r[1], picks[:, :bound]).astype(BF16)
        near23_o[1] = mm_nt(ac_s[:, :bound], pick_r[1]).astype(BF16)
        far13_o[1] = mm_nt(ac_s[:, bound:], pick_r[0]).astype(BF16)
        back3_o[0] = mm_nt(pick_r[0], ac_s[:, bound:]).astype(BF16)
        back3_o[1] = mm_nt(pick_r[1], ac_s[:, :bound]).astype(BF16)
        back3_o[2] = own3_o[...].T
        for g in range(3):
            if g < 2:
                agg = sums_r[g] + mm((far13_o, near23_o)[g][0], x3_s[...])
            else:
                agg = mm(along(1, own3_o[...], near23_o[1], far13_o[1]), along(0, x3_s[...], x12_r[1], x12_r[0]))
            mixed = mixed_of(agg, first_r[g + 1] if g < 2 else first3_o[...])
            mix_o[g] = mixed
        through = mm(along(0, *[mix_o[g] for g in range(3)]), w_r[0])
        for g in range(3):
            slope_o[g], x1_o[g] = activate(mix_o[g], through[g * rows : (g + 1) * rows], 0)

    return call(
        body,
        (
            sds((rows, width), F32),
            sds((3, rows, width), BF16),
            sds((3, rows, width), F32),
            sds((3, rows, width), BF16),
            sds((rows, rows), BF16),
            sds((2, rows, rows), BF16),
            sds((2, rows, rows), BF16),
            sds((3, rows, rows), BF16),
        ),
        [(a, "v") for a in (x12, sums, cp, pick, w, first, diag_sr, *diag)],
        [pltpu.VMEM((rows, 2 * bound), BF16), pltpu.VMEM((rows, width), BF16)],
        16,
    )


def matrix_of(prep, own, rest):
    arrays = (prep[1], own[5], rest[4], own[6], rest[5], own[7], rest[6])

    def readers(refs):
        own0, own12, own3, near01, near23, far02, far13 = refs
        return (
            lambda g: own0[...] if g == 0 else own3[...] if g == 3 else own12[g - 1],
            lambda g: (near01, near23)[g // 2][g % 2],
            lambda g: (far02, far13)[g % 2][g // 2],
        )

    return arrays, readers


def later_call(w, own, rest, matrix):
    arrays, readers = matrix
    layers = w.shape[0]
    rows, width = own[1].shape
    m = len(arrays)

    def body(first_r, first3_r, x1_r, x1n_r, w_r, *refs):
        own_at, near_at, far_at = readers(refs[:m])
        acts_o, mix_o, slope_o, xa_s, xb_s = refs[m:]
        seg = lax.axis_index("segment")

        @pl.when(seg == 0)
        def _():
            acts_o[...] = x1_r[...]

        def src(g):
            return x1n_r[g - 1] if g else x1_r[...]

        for k in range(1, layers):
            dst = (xa_s, xb_s)[k % 2]
            own_out = {}
            for some in ((0, 1, 2, 3),):
                for g in some:
                    agg = mm(along(1, own_at(g), near_at(g), far_at(g)), along(0, src(g), src(g ^ 1), src(g ^ 2)))
                    mix_o[k - 1, g] = mixed_of(agg, first_r[g] if g < 3 else first3_r[...])
                for c in range(2):
                    at = slice(c * width // 2, (c + 1) * width // 2)
                    through = mm(along(0, *[mix_o[k - 1, g] for g in some]), w_r[k, :, at])
                    for i, g in enumerate(some):
                        out = activate(mix_o[k - 1, g, :, at], through[i * rows : (i + 1) * rows], k)
                        slope_o[k - 1, g, :, at] = out[0]
                        if k + 1 < layers:
                            dst[g, :, at] = out[1]
                        if g == 0:
                            own_out[c] = out[1]
            for c in range(2):

                @pl.when(seg == k)
                def _():
                    acts_o[:, c * width // 2 : (c + 1) * width // 2] = own_out[c]

            def src(g, dst=dst):
                return dst[g]

    return call(
        body,
        (
            sds((rows, width), BF16),
            sds((layers - 1, 4, rows, width), BF16),
            sds((layers - 1, 4, rows, width), F32),
        ),
        [(a, "v") for a in (own[-2], rest[0], own[3], rest[3], w, *arrays)],
        [pltpu.VMEM((4, rows, width), BF16)] * 2,
        min(60, 14 + 6 * layers),
    )


def dmix_of(dpre, w_t, k):
    beta = beta_of(k)
    return ((1.0 - beta) * dpre.astype(F32) + beta * mm(dpre, w_t)).astype(BF16)


def back_start_call(cot, near, far, w, later_slope, matrix):
    arrays, readers = matrix
    layers = w.shape[0]
    rows, width = cot.shape
    piece = rows // layers
    m = len(arrays)
    last = layers - 1

    def body(cot_r, w_r, slope_r, *refs):
        own_at, near_at, far_at = readers(refs[:m])
        got_r = [refs[m + g * layers : m + (g + 1) * layers] for g in range(2)]
        dpre_o, sums_o, carry_o, up_s = refs[m + 2 * layers :]
        seg = lax.axis_index("segment")
        for g in range(2):
            for k in range(layers):
                up_s[g, piece_slice(seg, k, layers, piece), :] = got_r[g][k][...]
        dmix = []
        for g in range(3):
            up = up_s[g - 1] if g else cot_r[...]
            dpre = ((0.5 * up).astype(F32) * slope_r[last - 1, g]).astype(BF16)
            dpre_o[pl.ds(g * rows, rows), :] = dpre
            dmix.append(dmix_of(dpre, w_r[last], last))
        carry_o[...] = SHARE * dmix[0].astype(F32)
        sums_o[0] = mm_tn(along(0, own_at(0), near_at(1), far_at(2)), along(0, *dmix))
        sums_o[1] = mm_tn(along(0, near_at(0), own_at(1)), along(0, dmix[0], dmix[1]))
        sums_o[2] = mm_tn(along(0, far_at(0), own_at(2)), along(0, dmix[0], dmix[2]))
        sums_o[3] = mm_tn(along(0, far_at(1), near_at(2)), along(0, dmix[1], dmix[2]))

    return call(
        body,
        (sds((3 * rows, width), BF16), sds((4, rows, width), F32), sds((rows, width), F32)),
        [(a, "v") for a in (cot, w, later_slope, *arrays, *near, *far)],
        [pltpu.VMEM((2, rows, width), BF16)],
        min(60, 14 + 6 * layers),
    )


def back_call(diag, start, w, own, rest, later_mix, later_slope, matrix):
    arrays, readers = matrix
    dpre_start, sums, carry = start
    mix, slope = own[1], own[2]
    mix_rest, slope_rest = rest[1], rest[2]
    layers = w.shape[0]
    rows, width = mix.shape
    piece = rows // layers
    n_dom = lax.axis_size("dom")
    others = n_dom // 4
    out_rows = width // n_dom
    half = width // 2
    m = len(arrays)
    last = layers - 1

    def body(dps_r, sums_r, carry_r, mix_r, slope_r, mixn_r, slopen_r, later_mix_r, later_slope_r, w_r, back3_r, *refs):
        own_at, near_at, far_at = readers(refs[:m])
        got_r = refs[m : m + layers]
        outs = refs[m + layers :]
        dpre_o, carry_o, mine_o = outs[:3]
        send_o = outs[3 : 2 + others]
        up_s, dmix_s, part_s = outs[2 + others :]
        seg, low, high, place = position()
        for k in range(layers):
            up_s[3, piece_slice(seg, k, layers, piece), :] = got_r[k][...]

        def weight_part(k, dpre_at):
            at = pl.ds(pl.multiple_of(high * half, half), half)
            chosen = [later_mix_r[k - 1, g, :, at] if k else (mixn_r[g - 1, :, at] if g else mix_r[:, at]) for g in range(4)]
            part_s[...] = beta_of(k) * mm_tn(along(0, *chosen), along(0, *[dpre_at(g) for g in range(4)]))

        dpre = ((0.5 * up_s[3]).astype(F32) * later_slope_r[last - 1, 3]).astype(BF16)
        dpre_o[pl.ds(3 * rows, rows), :] = dpre
        dmix = dmix_of(dpre, w_r[last], last)
        extra = (None, *[mm(back3_r[n], dmix) for n in range(3)])
        for g in range(4):
            total = sums_r[g] if g == 0 else sums_r[g] + extra[g]
            up_s[g] = ((0.5 - 0.5 * SHARE) * total).astype(BF16)

        @pl.when(seg == last)
        def _():
            weight_part(last, lambda g: dps_r[pl.ds(g * rows, rows), :] if g < 3 else dpre_o[pl.ds(g * rows, rows), :])

        carry_o[...] = carry_r[...]
        for k in range(last - 1, -1, -1):
            for g in range(4):
                slope_now = later_slope_r[k - 1, g] if k else (slopen_r[g - 1] if g else slope_r[...])
                dpre = (up_s[g].astype(F32) * slope_now).astype(BF16)
                dpre_o[pl.ds(g * rows, rows), :] = dpre
                if k:
                    dmix = dmix_of(dpre, w_r[k], k)
                    dmix_s[g] = dmix
                    if g == 0:
                        carry_o[...] = SHARE * dmix.astype(F32) + carry_o[...]

            @pl.when(seg == k)
            def _():
                weight_part(k, lambda g: dpre_o[pl.ds(g * rows, rows), :])

            if k:
                for g in range(4):
                    total = mm_tn(
                        along(0, own_at(g), near_at(g ^ 1), far_at(g ^ 2)), along(0, dmix_s[g], dmix_s[g ^ 1], dmix_s[g ^ 2])
                    )
                    up_s[g] = ((0.5 - 0.5 * SHARE) * total).astype(BF16)

        def block(b):
            at = (place ^ b) * (2 * out_rows) + low * out_rows
            return part_s[pl.ds(pl.multiple_of(at, out_rows), out_rows), :]

        mine_o[...] = block(0)
        for b in range(1, others):
            send_o[b - 1][...] = block(b).astype(BF16)

    got = call(
        body,
        (sds((4 * rows, width), BF16), sds((rows, width), F32), sds((out_rows, width), F32))
        + tuple(sds((out_rows, width), BF16) for _ in range(1, others)),
        [
            (a, "v")
            for a in (
                dpre_start,
                sums,
                carry,
                mix,
                slope,
                mix_rest,
                slope_rest,
                later_mix,
                later_slope,
                w,
                rest[7],
                *arrays,
                *diag,
            )
        ],
        [
            pltpu.VMEM((4, rows, width), BF16),
            pltpu.VMEM((4, rows, width), BF16),
            pltpu.VMEM((half, width), F32),
        ],
        min(60, 14 + 6 * layers),
    )
    return got[0], got[1], got[2], got[3:]


def feat_call(dpre, carry, w, acts, matrix):
    arrays, readers = matrix
    layers = w.shape[0]
    rows, width = carry.shape
    cols = width // layers
    sliced = cols % 128 == 0
    kept = cols if sliced else width
    m = len(arrays)
    beta = beta_of(0)

    def body(dpre_r, carry_r, w_r, acts_r, *refs):
        own_at, near_at, far_at = readers(refs[:m])
        feat_o, acts_o = refs[m:]
        acts_o[...] = acts_r[...]
        at = pl.ds(pl.multiple_of(lax.axis_index("segment") * cols, cols), cols) if sliced else slice(None)
        w_cols = w_r[0, :, at]
        dmix = []
        for g in range(3):
            d_at = pl.ds(g * rows, rows)
            through = mm(dpre_r[d_at, :], w_cols)
            dmix.append(((1.0 - beta) * dpre_r[d_at, at].astype(F32) + beta * through).astype(BF16))
        sums = mm_tn(along(0, own_at(0), near_at(1), far_at(2)), along(0, *dmix))
        feat_o[...] = (1.0 - SHARE) * sums + (carry_r[:, at] + SHARE * dmix[0].astype(F32))

    feat, acts = call(
        body,
        (sds((rows, kept), F32), sds(acts.shape, acts.dtype)),
        [(a, "v") for a in (dpre, carry, w, acts, *arrays)],
        vmem=12,
    )
    feat = feat if sliced else lax.dynamic_slice_in_dim(feat, lax.axis_index("segment") * cols, cols, 1)
    return feat, acts


def step(feats, adj, couple, send_rows, weights, cot):
    layers = lax.axis_size("segment")
    n_dom = lax.axis_size("dom")
    top = n_dom // 2
    others = n_dom // 4

    fwd_mine, cot_mine = pack_call(feats, adj, couple, cot, layers)
    far = swapped(fwd_mine, top)
    near = swapped(fwd_mine, 1)
    w_pieces = every_piece(weights)
    far_sr = swapped(send_rows, top)
    near_sr = swapped(send_rows, 1)
    diag_sr = swapped(send_rows, top + 1)
    prep = prep_call(feats, adj, couple, send_rows)
    nears = every_piece(near)
    diag = swapped(far, 1)
    fars = every_piece(far)
    far_cot = swapped(cot_mine, top)
    own = own_call(nears, fars, near_sr, far_sr, w_pieces, prep)
    diags = every_piece(diag)
    near_cot = swapped(cot_mine, 1)
    rest = rest_call(diags, diag_sr, own)
    diag_cot = swapped(far_cot, 1)
    far_cots = every_piece(far_cot)
    near_cots = every_piece(near_cot)
    matrix = matrix_of(prep, own, rest)
    w, w_t = own[-3], own[-1]
    acts, later_mix, later_slope = later_call(w, own, rest, matrix)
    diag_cots = every_piece(diag_cot)
    start = back_start_call(cot, near_cots, far_cots, w_t, later_slope, matrix)
    dpre, carry, wgrad, sends = back_call(diag_cots, start, w_t, own, rest, later_mix, later_slope, matrix
    )
    for m in range(1, others):
        wgrad = wgrad + swapped(sends[m - 1], 2 * m).astype(F32)
    feat, acts = feat_call(dpre, carry, w_t, acts, matrix)
    return (acts[None], wgrad[None], feat)


def solution(mesh):
    in_specs = (
        P("dom", None),
        P("dom", None),
        P("dom", None),
        P("dom", None),
        P("segment", None),
        P("dom", None),
    )
    out_specs = (P("segment", "dom", None), P("segment", "dom", None), P("dom", "segment"))
    return jax.shard_map(step, mesh=mesh, in_specs=in_specs, out_specs=out_specs, check_vma=False)
```

```python
import math

import jax
import jax.numpy as jnp
from jax import lax
from jax.experimental import pallas as pl
from jax.experimental.pallas import tpu as pltpu
from jax.sharding import PartitionSpec as P


SHARE = 0.1
BETA_SCALE = 0.5
BF16 = jnp.bfloat16
F32 = jnp.float32


def swapped(x, mask):
    return lax.ppermute(x, "dom", [(i, i ^ mask) for i in range(lax.axis_size("dom"))])


def every_piece(x):
    n = lax.axis_size("segment")
    return [x] + [lax.ppermute(x, "segment", [(i, (i + k) % n) for i in range(n)]) for k in range(1, n)]


def beta_of(k):
    return math.log(BETA_SCALE / (k + 1.0) + 1.0)


def mm(a, b):
    return jnp.dot(a, b, preferred_element_type=F32)


def mm_nt(a, b):
    return lax.dot_general(a, b, (((1,), (1,)), ((), ())), preferred_element_type=F32)


def mm_tn(a, b):
    return lax.dot_general(a, b, (((0,), (0,)), ((), ())), preferred_element_type=F32)


def position():
    n = lax.axis_size("dom")
    dom = lax.axis_index("dom")
    return lax.axis_index("segment"), lax.rem(dom, 2), lax.div(dom, n // 2), lax.rem(lax.div(dom, 2), n // 4)


def place_of(seg, k, n):
    return lax.rem(seg - k + n, n)


def in_hbm(x):
    return pltpu.with_memory_space_constraint(x, pltpu.HBM)


def call(body, out_shape, ins, scratch=(), vmem=20):
    spaces = {"h": pltpu.HBM, "v": pltpu.VMEM}
    specs = [pl.BlockSpec(memory_space=spaces[m]) for _, m in ins]
    arrays = [in_hbm(a) if m == "h" else a for a, m in ins]
    return pl.pallas_call(
        body,
        out_shape=tuple(out_shape),
        in_specs=specs,
        out_specs=tuple(pl.BlockSpec(memory_space=pltpu.VMEM) for _ in out_shape),
        scratch_shapes=list(scratch),
        compiler_params=pltpu.CompilerParams(vmem_limit_bytes=vmem << 20),
    )(*arrays)


sds = jax.ShapeDtypeStruct


def pack_call(feats, adj, couple, cot, layers):
    rows, width = feats.shape
    piece = rows // layers

    def body(feats_r, adj_r, couple_r, cot_r, fwd_o, cot_o, sems):
        at = pl.ds(pl.multiple_of(lax.axis_index("segment") * piece, piece), piece)
        split = adj_r.shape[1]
        copies = [
            pltpu.make_async_copy(adj_r.at[at, :], fwd_o.at[:piece, :split], sems.at[0]),
            pltpu.make_async_copy(couple_r.at[at, :], fwd_o.at[:piece, split:], sems.at[1]),
            pltpu.make_async_copy(feats_r.at[at, :], fwd_o.at[piece:, :], sems.at[2]),
            pltpu.make_async_copy(cot_r.at[at, :], cot_o, sems.at[3]),
        ]
        for c in copies:
            c.start()
        for c in copies:
            c.wait()

    return call(
        body,
        (sds((2 * piece, width), BF16), sds((piece, width), BF16)),
        [(feats, "h"), (adj, "h"), (couple, "h"), (cot, "h")],
        [pltpu.SemaphoreType.DMA((4,))],
        4,
    )


def picks_of(sr, rows):
    ids = lax.broadcasted_iota(jnp.int32, (rows, sr.shape[1]), 0).astype(F32)
    return (ids == sr).astype(F32).astype(BF16)


def scaled(first):
    return SHARE * first.astype(F32)


def mixed_of(agg, first_scaled):
    return ((1.0 - SHARE) * agg + first_scaled).astype(BF16)


def activate(mixed, through, k):
    beta = beta_of(k)
    half = (0.5 - 0.5 * beta) * mixed.astype(F32) + (0.5 * beta) * through
    t = jnp.tanh(half)
    up = 1.0 + t
    return up * (1.0 + half * (1.0 - t)), (half * up).astype(BF16)


def along(dim, *parts):
    return jnp.concatenate(parts, axis=dim)


def piece_slice(seg, k, layers, piece):
    return pl.ds(pl.multiple_of(place_of(seg, k, layers) * piece, piece), piece)


def prep_call(feats, adj, couple, send_rows):
    rows, width = feats.shape

    def body(feats_r, adj_r, couple_r, sr_r, x_o, own_o, couple_o, pick_o, agg_o, sr_s, sems):
        copies = [
            pltpu.make_async_copy(sr_r, sr_s, sems.at[0]),
            pltpu.make_async_copy(couple_r, couple_o, sems.at[1]),
            pltpu.make_async_copy(feats_r, x_o, sems.at[2]),
            pltpu.make_async_copy(adj_r, own_o, sems.at[3]),
        ]
        for c in copies:
            c.start()
        for c in copies:
            c.wait()
        pick_o[...] = picks_of(sr_s[...].astype(F32), rows)
        agg_o[...] = mm(own_o[...], x_o[...])

    return call(
        body,
        (
            sds((rows, width), BF16),
            sds((rows, rows), BF16),
            sds((rows, couple.shape[1]), BF16),
            sds((rows, send_rows.shape[1]), BF16),
            sds((rows, width), F32),
        ),
        [(feats, "h"), (adj, "h"), (couple, "h"), (send_rows, "h")],
        [pltpu.VMEM(send_rows.shape, jnp.int32), pltpu.SemaphoreType.DMA((4,))],
        8,
    )


def own_call(near, far, near_sr, far_sr, w_pieces, prep):
    x, _, couple, pick, agg = prep
    layers = len(near)
    rows, width = x.shape
    piece = rows // layers
    bound = couple.shape[1] // 2

    def body(x_r, couple_r, pick_r, agg_r, near_sr_r, far_sr_r, *refs):
        got_r = [refs[g * layers : (g + 1) * layers] for g in range(2)]
        w_r = refs[2 * layers : 3 * layers]
        outs = refs[3 * layers :]
        x12_o, mix_o, slope_o, x1_o, sums_o, own12_o, near01_o, far02_o, cp_o, pick_o, w_o, first_o, wt_o, ac_s, sem = outs
        seg = lax.axis_index("segment")
        w_copy = pltpu.make_async_copy(w_r[0], w_o.at[seg], sem)
        w_copy.start()
        for k in range(1, layers):
            w_o[place_of(seg, k, layers)] = w_r[k][...]
        picks = []
        for g in range(2):
            for k in range(layers):
                at = piece_slice(seg, k, layers, piece)
                own12_o[g, at, :] = got_r[g][k][:piece, :rows]
                ac_s[g, at, :] = got_r[g][k][:piece, rows:]
                x12_o[g, at, :] = got_r[g][k][piece : 2 * piece, :]
            picks.append(picks_of((near_sr_r, far_sr_r)[g][...].astype(F32), rows))
        near01_o[0] = mm_nt(couple_r[:, :bound], picks[0][:, :bound]).astype(BF16)
        far02_o[0] = mm_nt(couple_r[:, bound:], picks[1][:, bound:]).astype(BF16)
        near01_o[1] = mm_nt(ac_s[0, :, :bound], pick_r[:, :bound]).astype(BF16)
        far02_o[1] = mm_nt(ac_s[1, :, bound:], pick_r[:, bound:]).astype(BF16)
        cp_o[0] = ac_s[0, :, bound:]
        cp_o[1] = ac_s[1, :, :bound]
        pick_o[0] = picks[0][:, bound:]
        pick_o[1] = picks[1][:, :bound]
        sums_o[0] = mm(along(1, own12_o[0], near01_o[1]), along(0, x12_o[0], x_r[...]))
        sums_o[1] = mm(along(1, own12_o[1], far02_o[1]), along(0, x12_o[1], x_r[...]))
        first_o[0] = scaled(x_r[...])
        first_o[1] = scaled(x12_o[0])
        first_o[2] = scaled(x12_o[1])
        w_copy.wait()
        for k in range(layers):
            wt_o[k] = w_o[k].T
        agg = agg_r[...] + mm(along(1, near01_o[0], far02_o[0]), along(0, x12_o[0], x12_o[1]))
        mixed = mixed_of(agg, first_o[0])
        mix_o[...] = mixed
        slope_o[...], x1_o[...] = activate(mixed, mm(mixed, w_o[0]), 0)

    return call(
        body,
        (
            sds((2, rows, width), BF16),
            sds((rows, width), BF16),
            sds((rows, width), F32),
            sds((rows, width), BF16),
            sds((2, rows, width), F32),
            sds((2, rows, rows), BF16),
            sds((2, rows, rows), BF16),
            sds((2, rows, rows), BF16),
            sds((2, rows, bound), BF16),
            sds((2, rows, bound), BF16),
            sds((layers, width, width), BF16),
            sds((3, rows, width), F32),
            sds((layers, width, width), BF16),
        ),
        [(a, "v") for a in (x, couple, pick, agg, near_sr, far_sr, *near, *far)]
        + [(w_pieces[0], "h")]
        + [(w, "v") for w in w_pieces[1:]],
        [pltpu.VMEM((2, rows, 2 * bound), BF16), pltpu.SemaphoreType.DMA],
        14 + 2 * layers,
    )


def rest_call(diag, diag_sr, own):
    x12, _, _, _, sums, _, _, _, cp, pick, w, first, _ = own
    layers = len(diag)
    _, rows, width = x12.shape
    piece = rows // layers
    bound = cp.shape[2]

    def body(x12_r, sums_r, cp_r, pick_r, w_r, first_r, sr_r, *refs):
        got_r = refs[:layers]
        first3_o, x3_s, mix_o, slope_o, x1_o, own3_o, near23_o, far13_o, ac_s = (refs[layers], refs[-1], *refs[layers + 1 : -1])
        seg = lax.axis_index("segment")
        for k in range(layers):
            at = piece_slice(seg, k, layers, piece)
            own3_o[at, :] = got_r[k][:piece, :rows]
            ac_s[at, :] = got_r[k][:piece, rows:]
            x3_s[at, :] = got_r[k][piece : 2 * piece, :]
        first3_o[...] = scaled(x3_s[...])
        picks = picks_of(sr_r[...].astype(F32), rows)
        far13_o[0] = mm_nt(cp_r[0], picks[:, bound:]).astype(BF16)
        near23_o[0] = mm_nt(cp_r[1], picks[:, :bound]).astype(BF16)
        near23_o[1] = mm_nt(ac_s[:, :bound], pick_r[1]).astype(BF16)
        far13_o[1] = mm_nt(ac_s[:, bound:], pick_r[0]).astype(BF16)
        for g in range(3):
            if g < 2:
                agg = sums_r[g] + mm((far13_o, near23_o)[g][0], x3_s[...])
            else:
                agg = mm(along(1, own3_o[...], near23_o[1], far13_o[1]), along(0, x3_s[...], x12_r[1], x12_r[0]))
            mixed = mixed_of(agg, first_r[g + 1] if g < 2 else first3_o[...])
            mix_o[g] = mixed
        through = mm(along(0, *[mix_o[g] for g in range(3)]), w_r[0])
        for g in range(3):
            slope_o[g], x1_o[g] = activate(mix_o[g], through[g * rows : (g + 1) * rows], 0)

    return call(
        body,
        (
            sds((rows, width), F32),
            sds((3, rows, width), BF16),
            sds((3, rows, width), F32),
            sds((3, rows, width), BF16),
            sds((rows, rows), BF16),
            sds((2, rows, rows), BF16),
            sds((2, rows, rows), BF16),
        ),
        [(a, "v") for a in (x12, sums, cp, pick, w, first, diag_sr, *diag)],
        [pltpu.VMEM((rows, 2 * bound), BF16), pltpu.VMEM((rows, width), BF16)],
        16,
    )


def matrix_of(prep, own, rest):
    arrays = (prep[1], own[5], rest[4], own[6], rest[5], own[7], rest[6])

    def readers(refs):
        own0, own12, own3, near01, near23, far02, far13 = refs
        return (
            lambda g: own0[...] if g == 0 else own3[...] if g == 3 else own12[g - 1],
            lambda g: (near01, near23)[g // 2][g % 2],
            lambda g: (far02, far13)[g % 2][g // 2],
        )

    return arrays, readers


def later_call(w, own, rest, matrix):
    arrays, readers = matrix
    layers = w.shape[0]
    rows, width = own[1].shape
    m = len(arrays)

    def body(first_r, first3_r, x1_r, x1n_r, w_r, *refs):
        own_at, near_at, far_at = readers(refs[:m])
        acts_o, mix_o, slope_o, xa_s, xb_s = refs[m:]
        seg = lax.axis_index("segment")

        @pl.when(seg == 0)
        def _():
            acts_o[...] = x1_r[...]

        def src(g):
            return x1n_r[g - 1] if g else x1_r[...]

        for k in range(1, layers):
            dst = (xa_s, xb_s)[k % 2]
            own_out = {}
            for some in ((0, 1, 2, 3),):
                for g in some:
                    agg = mm(along(1, own_at(g), near_at(g), far_at(g)), along(0, src(g), src(g ^ 1), src(g ^ 2)))
                    mix_o[k - 1, g] = mixed_of(agg, first_r[g] if g < 3 else first3_r[...])
                for c in range(2):
                    at = slice(c * width // 2, (c + 1) * width // 2)
                    through = mm(along(0, *[mix_o[k - 1, g] for g in some]), w_r[k, :, at])
                    for i, g in enumerate(some):
                        out = activate(mix_o[k - 1, g, :, at], through[i * rows : (i + 1) * rows], k)
                        slope_o[k - 1, g, :, at] = out[0]
                        if k + 1 < layers:
                            dst[g, :, at] = out[1]
                        if g == 0:
                            own_out[c] = out[1]
            for c in range(2):

                @pl.when(seg == k)
                def _():
                    acts_o[:, c * width // 2 : (c + 1) * width // 2] = own_out[c]

            def src(g, dst=dst):
                return dst[g]

    return call(
        body,
        (
            sds((rows, width), BF16),
            sds((layers - 1, 4, rows, width), BF16),
            sds((layers - 1, 4, rows, width), F32),
        ),
        [(a, "v") for a in (own[-2], rest[0], own[3], rest[3], w, *arrays)],
        [pltpu.VMEM((4, rows, width), BF16)] * 2,
        min(60, 14 + 6 * layers),
    )


def dmix_of(dpre, w_t, k):
    beta = beta_of(k)
    return ((1.0 - beta) * dpre.astype(F32) + beta * mm(dpre, w_t)).astype(BF16)


def back_start_call(cot, near, far, w, later_slope, matrix):
    arrays, readers = matrix
    layers = w.shape[0]
    rows, width = cot.shape
    piece = rows // layers
    m = len(arrays)
    last = layers - 1

    def body(cot_r, w_r, slope_r, *refs):
        own_at, near_at, far_at = readers(refs[:m])
        got_r = [refs[m + g * layers : m + (g + 1) * layers] for g in range(2)]
        dpre_o, sums_o, carry_o, up_s = refs[m + 2 * layers :]
        seg = lax.axis_index("segment")
        for g in range(2):
            for k in range(layers):
                up_s[g, piece_slice(seg, k, layers, piece), :] = got_r[g][k][...]
        dmix = []
        for g in range(3):
            up = up_s[g - 1] if g else cot_r[...]
            dpre = ((0.5 * up).astype(F32) * slope_r[last - 1, g]).astype(BF16)
            dpre_o[pl.ds(g * rows, rows), :] = dpre
            dmix.append(dmix_of(dpre, w_r[last], last))
        carry_o[...] = SHARE * dmix[0].astype(F32)
        sums_o[0] = mm_tn(along(0, own_at(0), near_at(1), far_at(2)), along(0, *dmix))
        sums_o[1] = mm_tn(along(0, near_at(0), own_at(1)), along(0, dmix[0], dmix[1]))
        sums_o[2] = mm_tn(along(0, far_at(0), own_at(2)), along(0, dmix[0], dmix[2]))
        sums_o[3] = mm_tn(along(0, far_at(1), near_at(2)), along(0, dmix[1], dmix[2]))

    return call(
        body,
        (sds((3 * rows, width), BF16), sds((4, rows, width), F32), sds((rows, width), F32)),
        [(a, "v") for a in (cot, w, later_slope, *arrays, *near, *far)],
        [pltpu.VMEM((2, rows, width), BF16)],
        min(60, 14 + 6 * layers),
    )


def back_call(diag, start, w, own, rest, later_mix, later_slope, matrix):
    arrays, readers = matrix
    dpre_start, sums, carry = start
    mix, slope = own[1], own[2]
    mix_rest, slope_rest = rest[1], rest[2]
    layers = w.shape[0]
    rows, width = mix.shape
    piece = rows // layers
    n_dom = lax.axis_size("dom")
    others = n_dom // 4
    out_rows = width // n_dom
    half = width // 2
    m = len(arrays)
    last = layers - 1

    def body(dps_r, sums_r, carry_r, mix_r, slope_r, mixn_r, slopen_r, later_mix_r, later_slope_r, w_r, *refs):
        own_at, near_at, far_at = readers(refs[:m])
        got_r = refs[m : m + layers]
        outs = refs[m + layers :]
        dpre_o, carry_o, mine_o = outs[:3]
        send_o = outs[3 : 2 + others]
        up_s, dmix_s, part_s = outs[2 + others :]
        seg, low, high, place = position()
        for k in range(layers):
            up_s[3, piece_slice(seg, k, layers, piece), :] = got_r[k][...]

        def weight_part(k, dpre_at):
            at = pl.ds(pl.multiple_of(high * half, half), half)
            chosen = [later_mix_r[k - 1, g, :, at] if k else (mixn_r[g - 1, :, at] if g else mix_r[:, at]) for g in range(4)]
            part_s[...] = beta_of(k) * mm_tn(along(0, *chosen), along(0, *[dpre_at(g) for g in range(4)]))

        dpre = ((0.5 * up_s[3]).astype(F32) * later_slope_r[last - 1, 3]).astype(BF16)
        dpre_o[pl.ds(3 * rows, rows), :] = dpre
        dmix = dmix_of(dpre, w_r[last], last)
        extra = (None, mm_tn(far_at(3), dmix), mm_tn(near_at(3), dmix), mm_tn(own_at(3), dmix))
        for g in range(4):
            total = sums_r[g] if g == 0 else sums_r[g] + extra[g]
            up_s[g] = ((0.5 - 0.5 * SHARE) * total).astype(BF16)

        @pl.when(seg == last)
        def _():
            weight_part(last, lambda g: dps_r[pl.ds(g * rows, rows), :] if g < 3 else dpre_o[pl.ds(g * rows, rows), :])

        carry_o[...] = carry_r[...]
        for k in range(last - 1, -1, -1):
            for g in range(4):
                slope_now = later_slope_r[k - 1, g] if k else (slopen_r[g - 1] if g else slope_r[...])
                dpre = (up_s[g].astype(F32) * slope_now).astype(BF16)
                dpre_o[pl.ds(g * rows, rows), :] = dpre
                if k:
                    dmix = dmix_of(dpre, w_r[k], k)
                    dmix_s[g] = dmix
                    if g == 0:
                        carry_o[...] = SHARE * dmix.astype(F32) + carry_o[...]

            @pl.when(seg == k)
            def _():
                weight_part(k, lambda g: dpre_o[pl.ds(g * rows, rows), :])

            if k:
                for g in range(4):
                    total = mm_tn(
                        along(0, own_at(g), near_at(g ^ 1), far_at(g ^ 2)), along(0, dmix_s[g], dmix_s[g ^ 1], dmix_s[g ^ 2])
                    )
                    up_s[g] = ((0.5 - 0.5 * SHARE) * total).astype(BF16)

        def block(b):
            at = (place ^ b) * (2 * out_rows) + low * out_rows
            return part_s[pl.ds(pl.multiple_of(at, out_rows), out_rows), :]

        mine_o[...] = block(0)
        for b in range(1, others):
            send_o[b - 1][...] = block(b).astype(BF16)

    got = call(
        body,
        (sds((4 * rows, width), BF16), sds((rows, width), F32), sds((out_rows, width), F32))
        + tuple(sds((out_rows, width), BF16) for _ in range(1, others)),
        [
            (a, "v")
            for a in (
                dpre_start,
                sums,
                carry,
                mix,
                slope,
                mix_rest,
                slope_rest,
                later_mix,
                later_slope,
                w,
                *arrays,
                *diag,
            )
        ],
        [
            pltpu.VMEM((4, rows, width), BF16),
            pltpu.VMEM((4, rows, width), BF16),
            pltpu.VMEM((half, width), F32),
        ],
        min(60, 14 + 6 * layers),
    )
    return got[0], got[1], got[2], got[3:]


def feat_call(dpre, carry, w, acts, matrix):
    arrays, readers = matrix
    layers = w.shape[0]
    rows, width = carry.shape
    cols = width // layers
    sliced = cols % 128 == 0
    kept = cols if sliced else width
    m = len(arrays)
    beta = beta_of(0)

    def body(dpre_r, carry_r, w_r, acts_r, *refs):
        own_at, near_at, far_at = readers(refs[:m])
        feat_o, acts_o = refs[m:]
        acts_o[...] = acts_r[...]
        at = pl.ds(pl.multiple_of(lax.axis_index("segment") * cols, cols), cols) if sliced else slice(None)
        w_cols = w_r[0, :, at]
        dmix = []
        for g in range(3):
            d_at = pl.ds(g * rows, rows)
            through = mm(dpre_r[d_at, :], w_cols)
            dmix.append(((1.0 - beta) * dpre_r[d_at, at].astype(F32) + beta * through).astype(BF16))
        sums = mm_tn(along(0, own_at(0), near_at(1), far_at(2)), along(0, *dmix))
        feat_o[...] = (1.0 - SHARE) * sums + (carry_r[:, at] + SHARE * dmix[0].astype(F32))

    feat, acts = call(
        body,
        (sds((rows, kept), F32), sds(acts.shape, acts.dtype)),
        [(a, "v") for a in (dpre, carry, w, acts, *arrays)],
        vmem=12,
    )
    feat = feat if sliced else lax.dynamic_slice_in_dim(feat, lax.axis_index("segment") * cols, cols, 1)
    return feat, acts


def step(feats, adj, couple, send_rows, weights, cot):
    layers = lax.axis_size("segment")
    n_dom = lax.axis_size("dom")
    top = n_dom // 2
    others = n_dom // 4

    fwd_mine, cot_mine = pack_call(feats, adj, couple, cot, layers)
    far = swapped(fwd_mine, top)
    near = swapped(fwd_mine, 1)
    w_pieces = every_piece(weights)
    far_sr = swapped(send_rows, top)
    near_sr = swapped(send_rows, 1)
    diag_sr = swapped(send_rows, top + 1)
    prep = prep_call(feats, adj, couple, send_rows)
    nears = every_piece(near)
    diag = swapped(far, 1)
    fars = every_piece(far)
    far_cot = swapped(cot_mine, top)
    own = own_call(nears, fars, near_sr, far_sr, w_pieces, prep)
    diags = every_piece(diag)
    near_cot = swapped(cot_mine, 1)
    rest = rest_call(diags, diag_sr, own)
    diag_cot = swapped(far_cot, 1)
    far_cots = every_piece(far_cot)
    near_cots = every_piece(near_cot)
    matrix = matrix_of(prep, own, rest)
    w, w_t = own[-3], own[-1]
    acts, later_mix, later_slope = later_call(w, own, rest, matrix)
    diag_cots = every_piece(diag_cot)
    start = back_start_call(cot, near_cots, far_cots, w_t, later_slope, matrix)
    dpre, carry, wgrad, sends = back_call(diag_cots, start, w_t, own, rest, later_mix, later_slope, matrix
    )
    for m in range(1, others):
        wgrad = wgrad + swapped(sends[m - 1], 2 * m).astype(F32)
    feat, acts = feat_call(dpre, carry, w_t, acts, matrix)
    return (acts[None], wgrad[None], feat)


def solution(mesh):
    in_specs = (
        P("dom", None),
        P("dom", None),
        P("dom", None),
        P("dom", None),
        P("segment", None),
        P("dom", None),
    )
    out_specs = (P("segment", "dom", None), P("segment", "dom", None), P("dom", "segment"))
    return jax.shard_map(step, mesh=mesh, in_specs=in_specs, out_specs=out_specs, check_vma=False)
```
